128 devices in a mesh: gx: 8 (over y, x_lo), gy: 8 (over z, core), sa: 2 (over x_hi).
Axes of the slice: x: 4 (x_hi: 2, x_lo: 2; x = x_hi * 2 + x_lo), y: 4, z: 4, core: 2. Of those that a mesh axis runs over, the one named last changes fastest.
Arguments:
- sweep_bricks: bfloat16 [8, 8, 256, 64, 128], P('gx', 'gy', 'sa'), may hold values from -24 to 24
- target_rank: int32 [8, 8, 256, 1], P('gx', 'gy', 'sa'), may hold values from 0 to 15; in each aligned block of 128 rows (0 to 127, 128 to 255, ..., all dimensions but the last counted through in order) at most 16 rows name the same one
- target_slot: int32 [8, 8, 256], P('gx', 'gy', 'sa'), may hold values from 0 to 15
- conv_first: bfloat16 [27, 128, 128], replicated, may hold values from -0.109375 to 0.109375
- conv_second: bfloat16 [27, 128, 128], replicated, may hold values from -0.109375 to 0.109375
- norm_gain: float32 [128], replicated, may hold values from 0.1 to 1.9
- out_grad: bfloat16 [64, 128, 16, 128], P('gx', 'gy', 'sa'), may hold values from -6 to 6
Outputs:
- block_out: bfloat16 [64, 128, 16, 128], P('gx', 'gy', 'sa')
- grid_grad: bfloat16 [64, 128, 16, 128], P('gx', 'gy', 'sa')
- conv_first_grad: float32 [27, 128, 128], replicated
- conv_second_grad: float32 [27, 128, 128], replicated
- gain_grad: float32 [128], replicated
The draws below stay inside these ranges and needn't reach their ends.
Inputs may be any that keep to these rules, and one draw needn't show every extreme that they name: `target_rank`: A contribution stays at its gy index; at most 16 of the rows of one device name the same destination, and some destination receives exactly 16 of them. `target_slot`: brick position (bx * 4 + by) * 2 + bz of the destination's 2 x 4 x 2 bricks.
All inputs are finite; a program needn't handle non-finite values.
Results may differ from the reference program's by a relative error of at most 0.017.
Values may be sent and summed in bfloat16 or wider, within the bound.
No kernel may reach another device: no remote copies, remote signals or barrier semaphores. Data moves between devices by JAX's collectives and lax.ppermute only.
A program may use at most 64 MiB of HBM per device.

```python
import math
import jax
import jax.numpy as jnp
import numpy as np
from jax import lax

C = 128
BRICK = 64
BX = 2
BY = 4
BZ = 2
SEND = 128
CAP = 16
NX = 64
NY = 128
NZ = 16
N_GX = 8
N_GY = 8
N_SA = 2


def draw_sweep_bricks(key, part):
    key_entries, key_scales = jax.random.split(key, 2)
    extent = (N_GX, N_GY, N_SA * SEND, BRICK, C)
    row_extent = (N_GX, N_GY, N_SA * SEND, 1, 1)
    entries = jnp.clip(jax.random.normal(key_entries, extent, jnp.float32), -6.0, 6.0)
    scales = jnp.exp(jax.random.uniform(key_scales, row_extent, jnp.float32, math.log(0.4), math.log(4.0)))
    return (entries * scales).astype(jnp.bfloat16)


def place_ends(drawn, key, smallest, largest):
    longest = drawn.shape.index(max(drawn.shape))
    spots = []
    for shift in (0, 1):
        where = [jax.random.randint(jax.random.fold_in(key, axis), (), 0, length) for axis, length in enumerate(drawn.shape)]
        where[longest] = (where[longest] + shift) % drawn.shape[longest]
        spots.append(tuple(where))
    return drawn.at[spots[0]].set(smallest).at[spots[1]].set(largest)


def block_scale(key, dims, cuts, least, largest):
    def one(position, parts):
        heights = jax.random.uniform(jax.random.fold_in(jax.random.fold_in(key, 6), position), (parts,), jnp.float32, least / len(cuts), largest / len(cuts))
        return jnp.repeat(jnp.exp(heights), dims[position] // parts).reshape((-1,) + (1,) * (len(dims) - position - 1))

    loudness = one(*cuts[0])
    for cut in cuts[1:]:
        loudness = loudness * one(*cut)
    return loudness


def shared_out(rng, own, number, rows, amount, top, most, skew):
    sequence = jax.random.permutation(rng, amount)
    packed, usual = shares(amount, rows * top, most, skew, True), shares(amount, rows * top, most, skew, False)
    places = jnp.arange(amount)

    def named(lengths, rotation):
        used = int((lengths > 0).sum())
        fixed = max(1, used // 4)
        shifted = fixed + (places - fixed + rotation * (used - fixed)) % max(1, amount - fixed)
        return jnp.zeros((amount,), jnp.int32).at[sequence[jnp.where(places < fixed, places, shifted)]].set(jnp.asarray(lengths, jnp.int32))

    lengths = jnp.where(number % 4 == 0, named(packed, number // 4), named(usual, number - number // 4 - 1))
    mixed = jax.random.permutation(jax.random.fold_in(own, 3), amount)
    donor, sink = mixed[0:amount // 2 * 2:2], mixed[1:amount // 2 * 2:2]
    slack = jnp.minimum(lengths[donor] - 1, most - lengths[sink]) // 2
    slack = jnp.where((donor == sequence[0]) | (sink == sequence[0]) | (lengths[sink] == 0), 0, jnp.maximum(slack, 0))
    shifted = jax.random.randint(jax.random.fold_in(own, 4), (amount // 2,), 0, 1 << 20) % (slack + 1)
    lengths = lengths.at[donor].add(-shifted).at[sink].add(shifted)
    members = jnp.searchsorted(jnp.cumsum(lengths), jnp.arange(rows * top), side="right").astype(jnp.int32)
    table = members.reshape(top, rows).T
    table = table[jax.random.permutation(jax.random.fold_in(own, 1), rows)]
    rotation = jax.random.randint(jax.random.fold_in(own, 2), (rows, 1), 0, top)
    return jnp.take_along_axis(table, (jnp.arange(top)[None, :] + rotation) % top, axis=1)


def shares(count, total, limit, slope, full):
    loads = [(1 << 20) // math.isqrt(rank ** slope) + 1 for rank in range(1, count + 1)]
    largest = limit if full else min(limit, max(-(-total // count), total * loads[0] // sum(loads)))
    least = 1 if total - largest >= count - 1 else 0
    holding, surplus = [largest] + [least] * (count - 1), total - largest - least * (count - 1)
    while surplus > 0:
        movable = [i for i in range(1, count) if holding[i] < largest] or [i for i in range(1, count) if holding[i] < limit]
        mass, left = sum([loads[i] for i in movable]), surplus
        for i in movable:
            more = min(limit - holding[i], max(1, left * loads[i] // mass), surplus)
            holding[i] = holding[i] + more
            surplus = surplus - more
    return np.array(holding)


def scatter_about(stream_key, shape, scale, bound, cuts=(), dtype=jnp.bfloat16):
    array = scale * jax.random.normal(stream_key, shape, jnp.float32)
    if cuts:
        array = array * block_scale(stream_key, shape, cuts, -0.22, 0.18)
    return jnp.clip(array, -bound, bound).astype(dtype)


def setup_inputs(seed: int = 0) -> dict:
    key_list = jax.random.split(jax.random.key(seed), 8)
    sweep_bricks = draw_sweep_bricks(jax.random.fold_in(key_list[7], 71), 0)
    target_rank_keys = jax.random.split(jax.random.fold_in(key_list[1], 1), N_GX * N_GY * (N_SA * SEND) // SEND)
    target_rank_turns = jax.random.permutation(jax.random.fold_in(key_list[1], 3), N_GX * N_GY * (N_SA * SEND) // SEND)
    target_rank = jax.vmap(lambda own, number: shared_out(jax.random.fold_in(key_list[1], 2), own, number, SEND, N_GX * N_SA, 1, CAP, 2))(target_rank_keys, target_rank_turns).reshape((N_GX, N_GY, N_SA * SEND, 1))
    target_slot = place_ends(jax.random.randint(key_list[2], (N_GX, N_GY, N_SA * SEND), 0, BX * BY * BZ), jax.random.fold_in(key_list[2], 1), 0, (BX * BY * BZ) - 1).astype(jnp.int32)
    conv_first = scatter_about(key_list[3], (27, C, C), (27 * C) ** -0.5, 0.109375)
    conv_second = scatter_about(key_list[4], (27, C, C), (27 * C) ** -0.5, 0.109375)
    norm_gain = jnp.clip(1.0 + 0.18 * jax.random.normal(key_list[5], (C,), jnp.float32), 0.1, 1.9)
    out_grad = scatter_about(key_list[6], (NX, NY, NZ, C), 1.0, 6.0, ((0, 8), (1, 8), (2, 2)))
    return dict(sweep_bricks=sweep_bricks, target_rank=target_rank, target_slot=target_slot, conv_first=conv_first, conv_second=conv_second, norm_gain=norm_gain, out_grad=out_grad)


epsilon = 1e-06

def apply_conv(padded, weights):
    extent_x = padded.shape[0] - 2
    extent_y = padded.shape[1] - 2
    extent_z = padded.shape[2] - 2
    channels = padded.shape[3]
    summed = jnp.zeros((extent_x * extent_y * extent_z, weights.shape[2]), jnp.float32)
    for offset in range(27):
        along_x, along_y, along_z = (offset // 9, offset // 3 % 3, offset % 3)
        window = padded[along_x:along_x + extent_x, along_y:along_y + extent_y, along_z:along_z + extent_z]
        summed = summed + jnp.dot(window.reshape(-1, channels), weights[offset], preferred_element_type=jnp.float32)
    return summed.reshape(extent_x, extent_y, extent_z, weights.shape[2])

def transposed_conv(padded, weights):
    extent_x = padded.shape[0] - 2
    extent_y = padded.shape[1] - 2
    extent_z = padded.shape[2] - 2
    channels = padded.shape[3]
    summed = jnp.zeros((extent_x * extent_y * extent_z, weights.shape[1]), jnp.float32)
    for offset in range(27):
        along_x, along_y, along_z = (2 - offset // 9, 2 - offset // 3 % 3, 2 - offset % 3)
        window = padded[along_x:along_x + extent_x, along_y:along_y + extent_y, along_z:along_z + extent_z]
        summed = summed + lax.dot_general(window.reshape(-1, channels), weights[offset], (((1,), (1,)), ((), ())), preferred_element_type=jnp.float32)
    return summed.reshape(extent_x, extent_y, extent_z, weights.shape[1])

def weight_grads(padded, grads):
    extent_x, extent_y, extent_z, channels = grads.shape
    grad_rows = grads.reshape(-1, channels)
    pieces = []
    for offset in range(27):
        along_x, along_y, along_z = (offset // 9, offset // 3 % 3, offset % 3)
        window = padded[along_x:along_x + extent_x, along_y:along_y + extent_y, along_z:along_z + extent_z]
        pieces.append(lax.dot_general(window.reshape(-1, padded.shape[3]), grad_rows, (((0,), (0,)), ((), ())), preferred_element_type=jnp.float32))
    return jnp.stack(pieces)

def pad_cells(values):
    return jnp.pad(values, ((1, 1), (1, 1), (1, 1), (0, 0)))

def arrange(values):
    moved = values.transpose(0, 3, 6, 1, 4, 7, 2, 5, 8, 9)
    return moved.reshape(N_GX * BX * 4, N_GY * BY * 4, N_SA * BZ * 4, values.shape[9])

def reference(sweep_bricks, target_rank, target_slot, conv_first, conv_second, norm_gain, out_grad):
    positions = BX * BY * BZ
    devices = N_GX * N_GY * N_SA
    along_gy = lax.broadcasted_iota(jnp.int32, (N_GX, N_GY, N_SA * SEND), 1)
    ranks = target_rank[..., 0].astype(jnp.int32)
    owner = (ranks // N_SA * N_GY + along_gy) * N_SA + ranks % N_SA
    brick_index = (owner * positions + target_slot.astype(jnp.int32)).reshape(-1)
    rows = sweep_bricks.reshape(-1, BRICK * C).astype(jnp.float32)
    summed = jax.ops.segment_sum(rows, brick_index, num_segments=devices * positions)
    counts = jax.ops.segment_sum(jnp.ones(brick_index.shape, jnp.float32), brick_index, num_segments=devices * positions)
    grid = arrange(summed.astype(jnp.bfloat16).reshape(N_GX, N_GY, N_SA, BX, BY, BZ, 4, 4, 4, C))
    live_bricks = (counts > 0).astype(jnp.float32).reshape(N_GX, N_GY, N_SA, BX, BY, BZ, 1, 1, 1, 1)
    live = arrange(jnp.broadcast_to(live_bricks, (N_GX, N_GY, N_SA, BX, BY, BZ, 4, 4, 4, 1)))
    grid_f = grid.astype(jnp.float32)
    gain_f = norm_gain.astype(jnp.float32)
    inverse = lax.rsqrt(lax.optimization_barrier(jnp.mean(grid_f * grid_f, axis=-1, keepdims=True)) + epsilon)
    normed = (grid_f * inverse * gain_f).astype(jnp.bfloat16)
    normed_pad = pad_cells(normed)
    before_act = live * apply_conv(normed_pad, conv_first)
    sigmoid_act = jax.nn.sigmoid(before_act)
    active = (before_act * sigmoid_act).astype(jnp.bfloat16)
    active_pad = pad_cells(active)
    branch = live * apply_conv(active_pad, conv_second)
    block_out = (grid_f + branch).astype(jnp.bfloat16)
    out_grad_f = out_grad.astype(jnp.float32)
    out_masked = (live * out_grad_f).astype(jnp.bfloat16)
    factor = 1.0 / math.sqrt(float(NX * NY * NZ))
    second_grad = weight_grads(active_pad, out_masked)
    active_grad = transposed_conv(pad_cells(out_masked), conv_second)
    pre_grad = (active_grad * sigmoid_act * (1.0 + before_act * (1.0 - sigmoid_act))).astype(jnp.bfloat16)
    first_grad = weight_grads(normed_pad, pre_grad)
    normed_grad = live * transposed_conv(pad_cells(pre_grad), conv_first)
    gain_grad = lax.optimization_barrier(jnp.sum((normed_grad * grid_f * inverse).reshape(-1, C), axis=0))
    upstream = normed_grad * gain_f
    centred = lax.optimization_barrier(jnp.mean(grid_f * upstream, axis=-1, keepdims=True))
    grid_grad = (out_grad_f + live * (inverse * upstream - grid_f * inverse ** 3 * centred)).astype(jnp.bfloat16)
    return (block_out, grid_grad, first_grad * factor, second_grad * factor, gain_grad * factor)
```

```python
import math

import jax
import jax.numpy as jnp
from jax import lax
from jax.experimental import pallas as pl
from jax.experimental.pallas import tpu as pltpu
from jax.sharding import Mesh
from jax.sharding import PartitionSpec as P

epsilon = 1e-06
DEAD = 1.0e30
OUT = -1.0e30
LIMIT = 1.0e29
GX = ("y", "xl")
GY = ("z", "c")
SA = "xh"
PLANE = ("y", "xl", "xh")
PEERS = ("y", "xl", "z", "xh")
F32 = jnp.float32
BF16 = jnp.bfloat16
VM = pl.BlockSpec(memory_space=pltpu.VMEM)
SM = pl.BlockSpec(memory_space=pltpu.SMEM)


def sum_bricks_kernel(arrived_ref, grid_ref, cells):
    values = arrived_ref[...].astype(F32)[:, 0]
    held = values < LIMIT
    total = jnp.sum(jnp.where(held, values, 0.0), axis=0)
    lowest = jnp.min(values, axis=0)
    total = jnp.where(lowest < LIMIT, total, DEAD).reshape(2, 4, 4, 4, 128)
    cells[:, :, 0:4, :] = total[0]
    cells[:, :, 4:8, :] = total[1]
    grid_ref[...] = cells[...].astype(BF16)


def sum_bricks(arrived):
    return pl.pallas_call(
        sum_bricks_kernel,
        out_shape=jax.ShapeDtypeStruct((8, 16, 8, 128), BF16),
        grid=(2, 4),
        in_specs=[pl.BlockSpec((16, 1, 2, 64, 128), lambda i, j: (0, i * 4 + j, 0, 0, 0))],
        out_specs=pl.BlockSpec((4, 4, 8, 128), lambda i, j: (i, j, 0, 0)),
        scratch_shapes=[pltpu.VMEM((4, 4, 8, 128), F32)],
        cost_estimate=pl.CostEstimate(flops=8 << 20, bytes_accessed=5 << 20, transcendentals=0),
    )(arrived.reshape(16, 8, 2, 64, 128))


def window_rows(ref, x, y, slabs, rows):
    part = ref[pl.ds(x, slabs), pl.ds(y, rows), :, :]
    return part.reshape(slabs * rows * 16, part.shape[3])


def gather_windows(ref, x, slabs, rows, sign):
    parts = []
    for i in range(3):
        for j in range(3):
            a, b = (i, j) if sign > 0 else (2 - i, 2 - j)
            parts.append(window_rows(ref, x + a, b, slabs, rows))
    return jnp.concatenate(parts, axis=1)


def neighbours(value, sign):
    count = value.shape[0]
    below = pltpu.roll(value, 1, 0)
    above = pltpu.roll(value, count - 1, 0)
    order = (below, value, above) if sign > 0 else (above, value, below)
    return jnp.concatenate([part.astype(BF16) for part in order], axis=1)


def fill(volume, centre, x_low, x_high, y_low, y_high, z_side, side, outside):
    volume[...] = jnp.full(volume.shape, outside, F32)
    volume[2:10, 2:18, 2:10, :] = centre[...].astype(F32)
    volume[0:2, 2:18, 2:10, :] = x_low[...].astype(F32)
    volume[10:12, 2:18, 2:10, :] = x_high[...].astype(F32)
    volume[:, 0:2, 2:10, :] = y_low[...].astype(F32)
    volume[:, 18:20, 2:10, :] = y_high[...].astype(F32)

    @pl.when(side == 0)
    def _():
        volume[:, :, 10:12, :] = z_side[...].astype(F32)

    @pl.when(side == 1)
    def _():
        volume[:, :, 0:2, :] = z_side[...].astype(F32)


def grads_kernel(
    where_ref,
    gain,
    g0, g1, g2, g3, g4, g5,
    o0, o1, o2, o3, o4, o5,
    first,
    second_t,
    act_ref,
    pre3_ref,
    own_ref,
    send_ref,
    cells,
    cots,
    normed3,
    masked3,
    act_t,
    normed_t,
):
    side = where_ref[0]
    core = where_ref[1]
    fill(cells, g0, g1, g2, g3, g4, g5, side, OUT)
    fill(cots, o0, o1, o2, o3, o4, o5, side, 0.0)
    z_of = lax.broadcasted_iota(jnp.int32, (256, 128), 0) % 16
    inside = (z_of >= 2) & (z_of < 10)

    def prepare(x, carry):
        values = cells[x].reshape(320, 128)
        live = jnp.abs(values) < LIMIT
        held = jnp.where(live, values, 0.0)
        inverse = lax.rsqrt(jnp.mean(held * held, axis=-1, keepdims=True) + epsilon)
        normed = held * inverse * gain[...]
        normed3[x] = neighbours(normed, 1).reshape(20, 16, 384)
        masked = jnp.where(live, cots[x].reshape(320, 128), 0.0)
        masked3[x] = neighbours(masked, -1).reshape(20, 16, 384)
        return carry

    lax.fori_loop(0, 12, prepare, 0)

    def turn(x, carry):
        normed = normed3[x + 2, 2:18, :, 128:256].reshape(256, 128).astype(F32)
        columns = pl.ds(pl.multiple_of(x * 256, 256), 256)
        normed_t[:, columns] = jnp.where(inside, normed, 0.0).T.astype(BF16)
        return carry

    lax.fori_loop(0, 8, turn, 0)

    def convolve(step, carry):
        x = step * 2
        values = cells[pl.ds(x + 1, 2), 1:19, :, :].reshape(576, 128)
        before = jnp.dot(
            gather_windows(normed3, x, 2, 18, 1), first[...], preferred_element_type=F32
        )
        before = jnp.where(jnp.abs(values) < LIMIT, before, 0.0)
        sigmoid = jax.nn.sigmoid(before)
        active = before * sigmoid
        act_ref[pl.ds(x, 2)] = active.astype(BF16).reshape(2, 18, 16, 128)
        active_grad = jnp.dot(
            gather_windows(masked3, x, 2, 18, -1), second_t[...], preferred_element_type=F32
        )
        pre = active_grad * sigmoid * (1.0 + before * (1.0 - sigmoid))
        pre = jnp.where(values > -LIMIT, pre, 0.0)
        pre3_ref[pl.ds(x, 2)] = neighbours(pre, -1).reshape(2, 18, 16, 384)
        return carry

    lax.fori_loop(0, 5, convolve, 0)

    def turn_active(x, carry):
        active = act_ref[x + 1, 1:17].reshape(256, 128).astype(F32)
        columns = pl.ds(pl.multiple_of(x * 256, 256), 256)
        act_t[:, columns] = jnp.where(inside, active, 0.0).T.astype(BF16)
        return carry

    lax.fori_loop(0, 8, turn_active, 0)

    for which, left, right, start in ((1, act_t, masked3, 3), (0, normed_t, pre3_ref, 2)):
        for target, here in ((own_ref, which), (send_ref, 1 - which)):

            @pl.when(core == here)
            def _():
                def weights(at, carry):
                    i = at // 3
                    j = at - i * 3
                    cot = window_rows(right, start - i, start - j, 8, 16)
                    total = jnp.dot(left[...], cot, preferred_element_type=F32).astype(BF16)
                    for k in range(3):
                        target[at * 3 + k] = total[:, k * 128 : (k + 1) * 128]
                    return carry

                lax.fori_loop(0, 9, weights, 0)

    own_ref[27] = jnp.zeros((128, 128), BF16)
    send_ref[27] = jnp.zeros((128, 128), BF16)


def grads_call(where, gain, grid_parts, cot_parts, first, second_t):
    return pl.pallas_call(
        grads_kernel,
        out_shape=(
            jax.ShapeDtypeStruct((10, 18, 16, 128), BF16),
            jax.ShapeDtypeStruct((10, 18, 16, 384), BF16),
            jax.ShapeDtypeStruct((28, 128, 128), BF16),
            jax.ShapeDtypeStruct((28, 128, 128), BF16),
        ),
        in_specs=[SM] + [VM] * 15,
        out_specs=(VM,) * 4,
        scratch_shapes=[
            pltpu.VMEM((12, 20, 16, 128), F32),
            pltpu.VMEM((12, 20, 16, 128), F32),
            pltpu.VMEM((12, 20, 16, 384), BF16),
            pltpu.VMEM((12, 20, 16, 384), BF16),
            pltpu.VMEM((128, 2048), BF16),
            pltpu.VMEM((128, 2048), BF16),
        ],
        compiler_params=pltpu.CompilerParams(vmem_limit_bytes=40 << 20),
        cost_estimate=pl.CostEstimate(flops=10 << 30, bytes_accessed=8 << 20, transcendentals=1 << 20),
    )(where, gain, *grid_parts, *cot_parts, first, second_t)


def outputs_kernel(
    gain, grid, out_grad, act, pre3, second, first_t, block_ref, grad_ref, gain_ref, act3, spread
):
    def prepare(x, carry):
        act3[x] = neighbours(act[x].reshape(288, 128).astype(F32), 1).reshape(18, 16, 384)
        return carry

    lax.fori_loop(0, 10, prepare, 0)
    gains = gain[...]

    def convolve(step, total):
        x = step * 2
        branch = jnp.dot(
            gather_windows(act3, x, 2, 16, 1), second[...], preferred_element_type=F32
        )
        spread[...] = branch.reshape(2, 16, 16, 128)
        branch = spread[:, :, 2:10, :].reshape(256, 128)
        values = grid[pl.ds(x, 2)].astype(F32).reshape(256, 128)
        live = values < LIMIT
        held = jnp.where(live, values, 0.0)
        block = jnp.where(live, branch, 0.0) + held
        block_ref[pl.ds(x, 2)] = block.astype(BF16).reshape(2, 16, 8, 128)
        normed_grad = jnp.dot(
            gather_windows(pre3, x, 2, 16, -1), first_t[...], preferred_element_type=F32
        )
        spread[...] = normed_grad.reshape(2, 16, 16, 128)
        normed_grad = jnp.where(live, spread[:, :, 2:10, :].reshape(256, 128), 0.0)
        inverse = lax.rsqrt(jnp.mean(held * held, axis=-1, keepdims=True) + epsilon)
        total = total + jnp.sum((normed_grad * held * inverse).reshape(32, 8, 128), axis=0)
        upstream = normed_grad * gains
        centred = jnp.mean(held * upstream, axis=-1, keepdims=True)
        extra = inverse * upstream - held * (inverse * inverse * inverse * centred)
        cot = out_grad[pl.ds(x, 2)].astype(F32).reshape(256, 128)
        grad = cot + jnp.where(live, extra, 0.0)
        grad_ref[pl.ds(x, 2)] = grad.astype(BF16).reshape(2, 16, 8, 128)
        return total

    total = lax.fori_loop(0, 4, convolve, jnp.zeros((8, 128), F32))
    gain_ref[...] = total


def outputs_call(gain, grid, out_grad, act, pre3, second, first_t):
    return pl.pallas_call(
        outputs_kernel,
        out_shape=(
            jax.ShapeDtypeStruct((8, 16, 8, 128), BF16),
            jax.ShapeDtypeStruct((8, 16, 8, 128), BF16),
            jax.ShapeDtypeStruct((8, 128), F32),
        ),
        in_specs=[VM] * 7,
        out_specs=(VM,) * 3,
        scratch_shapes=[
            pltpu.VMEM((10, 18, 16, 384), BF16),
            pltpu.VMEM((2, 16, 16, 128), F32),
        ],
        compiler_params=pltpu.CompilerParams(vmem_limit_bytes=24 << 20),
        cost_estimate=pl.CostEstimate(flops=8 << 30, bytes_accessed=6 << 20, transcendentals=4096),
    )(gain, grid, out_grad, act, pre3, second, first_t)


def swap_edges(block, axis, dim, count, outside):
    forward = [(i, i + 1) for i in range(count - 1)]
    backward = [(b, a) for a, b in forward]
    at = lax.axis_index(axis)
    low = lax.ppermute(lax.slice_in_dim(block, block.shape[dim] - 2, None, axis=dim), axis, forward)
    high = lax.ppermute(lax.slice_in_dim(block, 0, 2, axis=dim), axis, backward)
    if outside is not None:
        low = jnp.where(at == 0, jnp.asarray(outside, BF16), low)
        high = jnp.where(at == count - 1, jnp.asarray(outside, BF16), high)
    return low, high


def edges(volume, outside):
    x_low, x_high = swap_edges(volume, GX, 0, 8, outside)
    sides = []
    wide_low = jnp.concatenate([x_low[:, 14:16], volume[:, 14:16], x_high[:, 14:16]], axis=0)
    wide_high = jnp.concatenate([x_low[:, 0:2], volume[:, 0:2], x_high[:, 0:2]], axis=0)
    forward = [(i, i + 1) for i in range(7)]
    backward = [(b, a) for a, b in forward]
    at = lax.axis_index(GY)
    y_low = lax.ppermute(wide_low, GY, forward)
    y_high = lax.ppermute(wide_high, GY, backward)
    if outside is not None:
        y_low = jnp.where(at == 0, jnp.asarray(outside, BF16), y_low)
        y_high = jnp.where(at == 7, jnp.asarray(outside, BF16), y_high)
    side = lax.axis_index(SA)

    def layer(part):
        return jnp.where(side == 0, part[:, :, 6:8], part[:, :, 0:2])

    middle = jnp.concatenate([layer(x_low), layer(volume), layer(x_high)], axis=0)
    sent = jnp.concatenate([layer(y_low), middle, layer(y_high)], axis=1)
    z_side = lax.ppermute(sent, SA, [(0, 1), (1, 0)])
    return volume, x_low, x_high, y_low, y_high, z_side


def local(sweep_bricks, target_rank, target_slot, conv_first, conv_second, norm_gain, out_grad):
    code = target_rank.reshape(128) * 16 + target_slot.reshape(128)
    placing = code[None, :] == jnp.arange(256, dtype=jnp.int32)[:, None]
    rows = sweep_bricks.reshape(128, 64, 128)
    outgoing = lax.dot_general(
        placing.astype(BF16), rows, (((1,), (0,)), ((), ())), preferred_element_type=F32
    )
    named = jnp.any(placing, axis=1)[:, None, None]
    outgoing = jnp.where(named, outgoing, DEAD).astype(BF16)
    arrived = lax.all_to_all(outgoing, PLANE, split_axis=0, concat_axis=0, tiled=True)
    cot_parts = edges(out_grad, None)
    gain = norm_gain.reshape(1, 128)
    first = conv_first.reshape(3456, 128)
    second = conv_second.reshape(3456, 128)
    first_t = conv_first.transpose(0, 2, 1).reshape(3456, 128)
    second_t = conv_second.transpose(0, 2, 1).reshape(3456, 128)
    grid = sum_bricks(arrived)
    grid_parts = edges(grid, OUT)
    core = lax.axis_index("c")
    where = jnp.stack([lax.axis_index(SA), core]).astype(jnp.int32)
    act, pre3, own, send = grads_call(where, gain, grid_parts, cot_parts, first, second_t)
    other = lax.ppermute(send, "c", [(0, 1), (1, 0)])
    pair = (own.astype(F32) + other.astype(F32)).astype(BF16).reshape(64, 56, 128)
    shares = lax.all_to_all(pair, PEERS, split_axis=0, concat_axis=0, tiled=True)
    block_out, grid_grad, gain_part = outputs_call(
        gain, grid, out_grad, act, pre3, second, first_t
    )
    total = jnp.sum(shares.astype(F32), axis=0).astype(BF16)
    gain_own = jnp.sum(gain_part, axis=0, keepdims=True)
    gain_high = gain_own.astype(BF16)
    gain_low = (gain_own - gain_high.astype(F32)).astype(BF16)
    sent = jnp.concatenate([total, gain_high, gain_low, jnp.zeros((6, 128), BF16)], axis=0)
    sent = jnp.broadcast_to(sent[None], (64, 64, 128))
    gathered = lax.all_to_all(sent, PEERS, split_axis=0, concat_axis=0, tiled=True)
    swapped = lax.ppermute(gathered, "c", [(0, 1), (1, 0)])
    factor = 1.0 / math.sqrt(131072.0)

    def weights(low, high):
        picked = jnp.where(core == 0, low, high)[:, :56].reshape(28, 128, 128)[:27]
        return picked.astype(F32) * factor

    gains = jnp.sum(gathered[:, 56:58].astype(F32), axis=(0, 1))
    gains = gains + jnp.sum(swapped[:, 56:58].astype(F32), axis=(0, 1))
    return (
        block_out,
        grid_grad,
        weights(gathered, swapped),
        weights(swapped, gathered),
        gains * factor,
    )


def solution(mesh):
    inner = Mesh(mesh.devices.reshape(4, 2, 4, 2, 2), ("y", "xl", "z", "c", "xh"))
    in_specs = (
        P(GX, GY, SA, None, None),
        P(GX, GY, SA, None),
        P(GX, GY, SA),
        P(),
        P(),
        P(),
        P(GX, GY, SA, None),
    )
    out_specs = (P(GX, GY, SA, None), P(GX, GY, SA, None), P(), P(), P())
    return jax.shard_map(local, mesh=inner, in_specs=in_specs, out_specs=out_specs, check_vma=False)
```

```python
import math

import jax
import jax.numpy as jnp
from jax import lax
from jax.experimental import pallas as pl
from jax.experimental.pallas import tpu as pltpu
from jax.sharding import Mesh
from jax.sharding import PartitionSpec as P

epsilon = 1e-06
DEAD = 1.0e30
OUT = -1.0e30
LIMIT = 1.0e29
GX = ("y", "xl")
GY = ("z", "c")
SA = "xh"
PLANE = ("y", "xl", "xh")
F32 = jnp.float32
BF16 = jnp.bfloat16
VM = pl.BlockSpec(memory_space=pltpu.VMEM)
SM = pl.BlockSpec(memory_space=pltpu.SMEM)


def place_kernel(code_ref, rows_ref, out_ref, flat, place, lift):
    @pl.when(pl.program_id(0) == 0)
    def _():
        slots = lax.broadcasted_iota(jnp.int32, (256, 128), 0)
        chosen = jnp.where(slots == code_ref[...], 1.0, 0.0)
        place[...] = chosen.astype(BF16)
        named = jnp.max(chosen, axis=1, keepdims=True)
        lift[...] = jnp.broadcast_to(jnp.where(named > 0.0, 0.0, DEAD), (256, 128))

    flat[...] = rows_ref[...].astype(F32).reshape(1024, 128)
    for voxel in range(8):
        values = flat[pl.ds(voxel, 128, stride=8), :].astype(BF16)
        summed = jnp.dot(place[...], values, preferred_element_type=F32) + lift[...]
        out_ref[:, voxel] = summed.astype(BF16).reshape(16, 16, 128)


def place_bricks(code, rows):
    return pl.pallas_call(
        place_kernel,
        out_shape=jax.ShapeDtypeStruct((16, 64, 16, 128), BF16),
        grid=(8,),
        in_specs=[
            pl.BlockSpec((1, 128), lambda i: (0, 0)),
            pl.BlockSpec((128, 8, 128), lambda i: (0, i, 0)),
        ],
        out_specs=pl.BlockSpec((16, 8, 16, 128), lambda i: (0, i, 0, 0)),
        scratch_shapes=[
            pltpu.VMEM((1024, 128), F32),
            pltpu.VMEM((256, 128), BF16),
            pltpu.VMEM((256, 128), F32),
        ],
        compiler_params=pltpu.CompilerParams(vmem_limit_bytes=16 << 20),
        cost_estimate=pl.CostEstimate(flops=1 << 29, bytes_accessed=6 << 20, transcendentals=0),
    )(code, rows)


def sum_bricks_kernel(arrived_ref, cot_ref, both_ref, low_ref, high_ref, sums, cells):
    step = pl.program_id(0)
    shift_x = step // 2
    shift_y = (step % 2) * 2

    @pl.when(step == 0)
    def _():
        both_ref[1] = cot_ref[...]
        low_ref[1] = cot_ref[0:2]
        high_ref[1] = cot_ref[6:8]

    total = jnp.zeros((8, 16, 128), F32)
    filled = jnp.zeros((16, 128), jnp.bool_)
    for source in range(16):
        held = arrived_ref[source, 0].astype(F32) < LIMIT
        filled = filled | held
        total = total + jnp.where(held, arrived_ref[source].astype(F32), 0.0)
    sums[...] = jnp.where(filled, total, DEAD).reshape(128, 128)
    for voxel in range(2):
        for bx in range(2):
            for by in range(4):
                slot = (bx * 4 + by) * 2
                cells[0:4, :] = sums[pl.ds(voxel * 64 + slot, 4, stride=16), :]
                cells[4:8, :] = sums[pl.ds(voxel * 64 + slot + 1, 4, stride=16), :]
                both_ref[0, bx * 4 + shift_x, by * 4 + shift_y + voxel] = cells[...].astype(BF16)

    @pl.when(step == 7)
    def _():
        low_ref[0] = both_ref[0, 0:2]
        high_ref[0] = both_ref[0, 6:8]


def sum_bricks(arrived, out_grad):
    return pl.pallas_call(
        sum_bricks_kernel,
        out_shape=(
            jax.ShapeDtypeStruct((2, 8, 16, 8, 128), BF16),
            jax.ShapeDtypeStruct((2, 2, 16, 8, 128), BF16),
            jax.ShapeDtypeStruct((2, 2, 16, 8, 128), BF16),
        ),
        grid=(8,),
        in_specs=[
            pl.BlockSpec((16, 8, 16, 128), lambda i: (0, i, 0, 0)),
            pl.BlockSpec((8, 16, 8, 128), lambda i: (0, 0, 0, 0)),
        ],
        out_specs=(
            pl.BlockSpec((2, 8, 16, 8, 128), lambda i: (0, 0, 0, 0, 0)),
            pl.BlockSpec((2, 2, 16, 8, 128), lambda i: (0, 0, 0, 0, 0)),
            pl.BlockSpec((2, 2, 16, 8, 128), lambda i: (0, 0, 0, 0, 0)),
        ),
        scratch_shapes=[pltpu.VMEM((128, 128), F32), pltpu.VMEM((8, 128), F32)],
        compiler_params=pltpu.CompilerParams(vmem_limit_bytes=16 << 20),
        cost_estimate=pl.CostEstimate(flops=8 << 20, bytes_accessed=5 << 20, transcendentals=0),
    )(arrived, out_grad)


def window_rows(ref, x, y, slabs, rows):
    part = ref[pl.ds(x, slabs), pl.ds(y, rows), :, :]
    return part.reshape(slabs * rows * 16, part.shape[3])


def gather_windows(ref, x, slabs, rows, sign):
    parts = []
    for i in range(3):
        for j in range(3):
            a, b = (i, j) if sign > 0 else (2 - i, 2 - j)
            parts.append(window_rows(ref, x + a, b, slabs, rows))
    return jnp.concatenate(parts, axis=1)


def neighbours(value, sign):
    count = value.shape[0]
    below = pltpu.roll(value, 1, 0)
    above = pltpu.roll(value, count - 1, 0)
    order = (below, value, above) if sign > 0 else (above, value, below)
    return jnp.concatenate([part.astype(BF16) for part in order], axis=1)


PIECES = (
    (2, 8, 16, 8, 128),
    (2, 2, 16, 8, 128),
    (2, 2, 16, 8, 128),
    (2, 12, 2, 8, 128),
    (2, 12, 2, 8, 128),
    (2, 12, 20, 2, 128),
)


def fill(volume, which, pieces, where_ref, outside):
    centre, x_low, x_high, y_low, y_high, z_side = pieces
    volume[...] = jnp.full(volume.shape, outside, F32)
    volume[2:10, 2:18, 2:10, :] = centre[which].astype(F32)
    volume[0:2, 2:18, 2:10, :] = x_low[which].astype(F32)
    volume[10:12, 2:18, 2:10, :] = x_high[which].astype(F32)
    volume[:, 0:2, 2:10, :] = y_low[which].astype(F32)
    volume[:, 18:20, 2:10, :] = y_high[which].astype(F32)

    @pl.when(where_ref[0] == 0)
    def _():
        volume[:, :, 10:12, :] = z_side[which].astype(F32)

    @pl.when(where_ref[0] == 1)
    def _():
        volume[:, :, 0:2, :] = z_side[which].astype(F32)

    @pl.when(where_ref[2] == 0)
    def _():
        volume[0:2] = jnp.full((2, 20, 16, 128), outside, F32)

    @pl.when(where_ref[2] == 7)
    def _():
        volume[10:12] = jnp.full((2, 20, 16, 128), outside, F32)

    @pl.when(where_ref[3] == 0)
    def _():
        volume[:, 0:2] = jnp.full((12, 2, 16, 128), outside, F32)

    @pl.when(where_ref[3] == 7)
    def _():
        volume[:, 18:20] = jnp.full((12, 2, 16, 128), outside, F32)


def grads_kernel(
    where_ref,
    gain,
    p0, p1, p2, p3, p4, p5,
    first_hbm,
    second_hbm,
    act_ref,
    pre3_ref,
    own_ref,
    send_ref,
    cells,
    cots,
    normed3,
    masked3,
    act_t,
    normed_t,
    s0, s1, s2, s3, s4, s5,
    first,
    second_t,
    sems,
):
    core = where_ref[1]
    pieces = (s0, s1, s2, s3, s4, s5)
    copies = [
        pltpu.make_async_copy(source, target, sems.at[n])
        for n, (source, target) in enumerate(
            zip((p0, p1, p2, p3, p4, p5, first_hbm, second_hbm), (*pieces, first, second_t))
        )
    ]
    for copy in copies:
        copy.start()
    for copy in copies[:6]:
        copy.wait()
    fill(cells, 0, pieces, where_ref, OUT)
    fill(cots, 1, pieces, where_ref, 0.0)
    z_of = lax.broadcasted_iota(jnp.int32, (256, 128), 0) % 16
    inside = (z_of >= 2) & (z_of < 10)

    def prepare(x, carry):
        values = cells[x].reshape(320, 128)
        live = jnp.abs(values) < LIMIT
        held = jnp.where(live, values, 0.0)
        inverse = lax.rsqrt(jnp.mean(held * held, axis=-1, keepdims=True) + epsilon)
        normed = held * inverse * gain[...]
        normed3[x] = neighbours(normed, 1).reshape(20, 16, 384)
        masked = jnp.where(live, cots[x].reshape(320, 128), 0.0)
        masked3[x] = neighbours(masked, -1).reshape(20, 16, 384)
        return carry

    lax.fori_loop(0, 12, prepare, 0)

    def turn(x, carry):
        normed = normed3[x + 2, 2:18, :, 128:256].reshape(256, 128).astype(F32)
        columns = pl.ds(pl.multiple_of(x * 256, 256), 256)
        normed_t[:, columns] = jnp.where(inside, normed, 0.0).T.astype(BF16)
        return carry

    lax.fori_loop(0, 8, turn, 0)
    for copy in copies[6:]:
        copy.wait()

    def convolve(step, carry):
        x = step * 2
        values = cells[pl.ds(x + 1, 2), 1:19, :, :].reshape(576, 128)
        before = jnp.dot(
            gather_windows(normed3, x, 2, 18, 1), first[...], preferred_element_type=F32
        )
        before = jnp.where(jnp.abs(values) < LIMIT, before, 0.0)
        sigmoid = jax.nn.sigmoid(before)
        active = before * sigmoid
        act_ref[pl.ds(x, 2)] = active.astype(BF16).reshape(2, 18, 16, 128)
        active_grad = jnp.dot(
            gather_windows(masked3, x, 2, 18, -1), second_t[...], preferred_element_type=F32
        )
        pre = active_grad * sigmoid * (1.0 + before * (1.0 - sigmoid))
        pre = jnp.where(values > -LIMIT, pre, 0.0)
        pre3_ref[pl.ds(x, 2)] = neighbours(pre, -1).reshape(2, 18, 16, 384)
        return carry

    lax.fori_loop(0, 5, convolve, 0)

    def turn_active(x, carry):
        active = act_ref[x + 1, 1:17].reshape(256, 128).astype(F32)
        columns = pl.ds(pl.multiple_of(x * 256, 256), 256)
        act_t[:, columns] = jnp.where(inside, active, 0.0).T.astype(BF16)
        return carry

    lax.fori_loop(0, 8, turn_active, 0)

    for which, left, right, start in ((1, act_t, masked3, 3), (0, normed_t, pre3_ref, 2)):
        for target, here in ((own_ref, which), (send_ref, 1 - which)):

            @pl.when(core == here)
            def _():
                def weights(at, carry):
                    i = at // 3
                    j = at - i * 3
                    cot = window_rows(right, start - i, start - j, 8, 16)
                    total = jnp.dot(left[...], cot, preferred_element_type=F32).astype(BF16)
                    for k in range(3):
                        target[at * 3 + k] = total[:, k * 128 : (k + 1) * 128]
                    return carry

                lax.fori_loop(0, 9, weights, 0)


def grads_call(where, gain, pieces, first, second_t):
    return pl.pallas_call(
        grads_kernel,
        out_shape=(
            jax.ShapeDtypeStruct((10, 18, 16, 128), BF16),
            jax.ShapeDtypeStruct((10, 18, 16, 384), BF16),
            jax.ShapeDtypeStruct((27, 128, 128), BF16),
            jax.ShapeDtypeStruct((27, 128, 128), BF16),
        ),
        in_specs=[SM, VM] + [pl.BlockSpec(memory_space=pl.ANY)] * 8,
        out_specs=(VM,) * 4,
        scratch_shapes=[
            pltpu.VMEM((12, 20, 16, 128), F32),
            pltpu.VMEM((12, 20, 16, 128), F32),
            pltpu.VMEM((12, 20, 16, 384), BF16),
            pltpu.VMEM((12, 20, 16, 384), BF16),
            pltpu.VMEM((128, 2048), BF16),
            pltpu.VMEM((128, 2048), BF16),
            *[pltpu.VMEM(shape, BF16) for shape in PIECES],
            pltpu.VMEM((3456, 128), BF16),
            pltpu.VMEM((3456, 128), BF16),
            pltpu.SemaphoreType.DMA((8,)),
        ],
        compiler_params=pltpu.CompilerParams(vmem_limit_bytes=44 << 20),
        cost_estimate=pl.CostEstimate(flops=10 << 30, bytes_accessed=8 << 20, transcendentals=1 << 20),
    )(where, gain, *pieces, first, second_t)


def outputs_kernel(
    gain, both, act, pre3, second, first_t, block_ref, grad_ref, gain_ref, act3, spread
):
    def prepare(x, carry):
        act3[x] = neighbours(act[x].reshape(288, 128).astype(F32), 1).reshape(18, 16, 384)
        return carry

    lax.fori_loop(0, 10, prepare, 0)
    gains = gain[...]

    def convolve(step, total):
        x = step * 2
        branch = jnp.dot(
            gather_windows(act3, x, 2, 16, 1), second[...], preferred_element_type=F32
        )
        spread[...] = branch.reshape(2, 16, 16, 128)
        branch = spread[:, :, 2:10, :].reshape(256, 128)
        values = both[0, pl.ds(x, 2)].astype(F32).reshape(256, 128)
        live = values < LIMIT
        held = jnp.where(live, values, 0.0)
        block = jnp.where(live, branch, 0.0) + held
        block_ref[pl.ds(x, 2)] = block.astype(BF16).reshape(2, 16, 8, 128)
        normed_grad = jnp.dot(
            gather_windows(pre3, x, 2, 16, -1), first_t[...], preferred_element_type=F32
        )
        spread[...] = normed_grad.reshape(2, 16, 16, 128)
        normed_grad = jnp.where(live, spread[:, :, 2:10, :].reshape(256, 128), 0.0)
        inverse = lax.rsqrt(jnp.mean(held * held, axis=-1, keepdims=True) + epsilon)
        total = total + jnp.sum((normed_grad * held * inverse).reshape(32, 8, 128), axis=0)
        upstream = normed_grad * gains
        centred = jnp.mean(held * upstream, axis=-1, keepdims=True)
        extra = inverse * upstream - held * (inverse * inverse * inverse * centred)
        cot = both[1, pl.ds(x, 2)].astype(F32).reshape(256, 128)
        grad = cot + jnp.where(live, extra, 0.0)
        grad_ref[pl.ds(x, 2)] = grad.astype(BF16).reshape(2, 16, 8, 128)
        return total

    total = lax.fori_loop(0, 4, convolve, jnp.zeros((8, 128), F32))
    gain_ref[...] = total


def outputs_call(gain, both, act, pre3, second, first_t):
    return pl.pallas_call(
        outputs_kernel,
        out_shape=(
            jax.ShapeDtypeStruct((8, 16, 8, 128), BF16),
            jax.ShapeDtypeStruct((8, 16, 8, 128), BF16),
            jax.ShapeDtypeStruct((8, 128), F32),
        ),
        in_specs=[VM] * 6,
        out_specs=(VM,) * 3,
        scratch_shapes=[
            pltpu.VMEM((10, 18, 16, 384), BF16),
            pltpu.VMEM((2, 16, 16, 128), F32),
        ],
        compiler_params=pltpu.CompilerParams(vmem_limit_bytes=24 << 20),
        cost_estimate=pl.CostEstimate(flops=8 << 30, bytes_accessed=6 << 20, transcendentals=4096),
    )(gain, both, act, pre3, second, first_t)


FORWARD = [(i, i + 1) for i in range(7)]
BACKWARD = [(i + 1, i) for i in range(7)]


def edges(both, send_low, send_high):
    x_low = lax.ppermute(send_high, GX, FORWARD)
    x_high = lax.ppermute(send_low, GX, BACKWARD)
    parts = (x_low, both, x_high)
    wide_low = jnp.concatenate([part[:, :, 14:16] for part in parts], axis=1)
    wide_high = jnp.concatenate([part[:, :, 0:2] for part in parts], axis=1)
    y_low = lax.ppermute(wide_low, GY, FORWARD)
    y_high = lax.ppermute(wide_high, GY, BACKWARD)
    side = lax.axis_index(SA)

    def layer(part):
        return jnp.where(side == 0, part[:, :, :, 6:8], part[:, :, :, 0:2])

    middle = jnp.concatenate([layer(part) for part in parts], axis=1)
    sent = jnp.concatenate([layer(y_low), middle, layer(y_high)], axis=2)
    z_side = lax.ppermute(sent, SA, [(0, 1), (1, 0)])
    return both, x_low, x_high, y_low, y_high, z_side


def exchange(values, axes):
    return lax.all_to_all(values, axes, split_axis=0, concat_axis=0, tiled=True)


def local(sweep_bricks, target_rank, target_slot, conv_first, conv_second, norm_gain, out_grad):
    code = target_rank.reshape(1, 128) * 16 + target_slot.reshape(1, 128)
    arrived = exchange(place_bricks(code, sweep_bricks.reshape(128, 64, 128)), PLANE)
    gain = norm_gain.reshape(1, 128)
    first = conv_first.reshape(3456, 128)
    second = conv_second.reshape(3456, 128)
    first_t = conv_first.transpose(0, 2, 1).reshape(3456, 128)
    second_t = conv_second.transpose(0, 2, 1).reshape(3456, 128)
    pieces = edges(*sum_bricks(arrived, out_grad))
    core = lax.axis_index("c")
    where = jnp.stack([lax.axis_index(SA), core, lax.axis_index(GX), lax.axis_index(GY)])
    act, pre3, own, send = grads_call(where.astype(jnp.int32), gain, pieces, first, second_t)
    other = lax.ppermute(send, "c", [(0, 1), (1, 0)])
    pair = (own.astype(F32) + other.astype(F32)).astype(BF16).reshape(16, 216, 128)
    shares = exchange(pair, PLANE)
    block_out, grid_grad, gain_part = outputs_call(gain, pieces[0], act, pre3, second, first_t)

    def halves(row):
        high = row.astype(BF16)
        low = (row - high.astype(F32)).astype(BF16)
        return [high, low, jnp.zeros((6, 128), BF16)]

    def spread(total, row, count):
        sent = jnp.concatenate([total.astype(BF16)] + halves(row), axis=0)
        return jnp.broadcast_to(sent[None], (count, 224, 128))

    total = jnp.sum(shares.astype(F32), axis=0)
    row = jnp.sum(gain_part, axis=0, keepdims=True)
    layers = exchange(spread(total, row, 4), "z").astype(F32)
    total = jnp.sum(layers[:, :216], axis=0)
    row = jnp.sum(layers[:, 216:218], axis=(0, 1))[None]
    gathered = exchange(spread(total, row, 16), PLANE)
    swapped = lax.ppermute(gathered, "c", [(0, 1), (1, 0)])
    factor = 1.0 / math.sqrt(131072.0)

    def weights(low, high):
        picked = jnp.where(core == 0, low[:, :216], high[:, :216])
        return (picked.astype(F32) * factor).reshape(27, 128, 128)

    gains = jnp.sum(gathered[:, 216:218].astype(F32), axis=(0, 1))
    gains = gains + jnp.sum(swapped[:, 216:218].astype(F32), axis=(0, 1))
    return (
        block_out,
        grid_grad,
        weights(gathered, swapped),
        weights(swapped, gathered),
        gains * factor,
    )


def solution(mesh):
    inner = Mesh(mesh.devices.reshape(4, 2, 4, 2, 2), ("y", "xl", "z", "c", "xh"))
    in_specs = (
        P(GX, GY, SA, None, None),
        P(GX, GY, SA, None),
        P(GX, GY, SA),
        P(),
        P(),
        P(),
        P(GX, GY, SA, None),
    )
    out_specs = (P(GX, GY, SA, None), P(GX, GY, SA, None), P(), P(), P())
    return jax.shard_map(local, mesh=inner, in_specs=in_specs, out_specs=out_specs, check_vma=False)
```

```python
import math

import jax
import jax.numpy as jnp
from jax import lax
from jax.experimental import pallas as pl
from jax.experimental.pallas import tpu as pltpu
from jax.sharding import Mesh
from jax.sharding import PartitionSpec as P

epsilon = 1e-06
DEAD = 1.0e30
OUT = -1.0e30
LIMIT = 1.0e29
GX = ("y", "xl")
GY = ("z", "c")
SA = "xh"
PLANE = ("y", "xl", "xh")
F32 = jnp.float32
BF16 = jnp.bfloat16
VM = pl.BlockSpec(memory_space=pltpu.VMEM)
SM = pl.BlockSpec(memory_space=pltpu.SMEM)


def place_kernel(code_ref, rows_ref, o0, o1, o2, o3, flat, place, lift):
    @pl.when(pl.program_id(0) == 0)
    def _():
        slots = lax.broadcasted_iota(jnp.int32, (256, 128), 0)
        chosen = jnp.where(slots == code_ref[...], 1.0, 0.0)
        place[...] = chosen.astype(BF16)
        named = jnp.max(chosen, axis=1, keepdims=True)
        lift[...] = jnp.broadcast_to(jnp.where(named > 0.0, 0.0, DEAD), (256, 128))

    flat[...] = rows_ref[...].astype(F32).reshape(1024, 128)
    for voxel in range(8):
        values = flat[pl.ds(voxel, 128, stride=8), :].astype(BF16)
        summed = jnp.dot(place[...], values, preferred_element_type=F32) + lift[...]
        summed = summed.astype(BF16).reshape(4, 4, 16, 128)
        for shift, out in enumerate((o0, o1, o2, o3)):
            out[:, voxel] = summed[shift]


def place_bricks(code, rows, half):
    return pl.pallas_call(
        place_kernel,
        out_shape=(jax.ShapeDtypeStruct((4, 32, 16, 128), BF16),) * 4,
        grid=(4,),
        in_specs=[
            pl.BlockSpec((1, 128), lambda i: (0, 0)),
            pl.BlockSpec((128, 8, 128), lambda i: (0, i + 4 * half, 0)),
        ],
        out_specs=(pl.BlockSpec((4, 8, 16, 128), lambda i: (0, i, 0, 0)),) * 4,
        scratch_shapes=[
            pltpu.VMEM((1024, 128), F32),
            pltpu.VMEM((256, 128), BF16),
            pltpu.VMEM((256, 128), F32),
        ],
        compiler_params=pltpu.CompilerParams(vmem_limit_bytes=10 << 20),
        cost_estimate=pl.CostEstimate(flops=1 << 28, bytes_accessed=3 << 20, transcendentals=0),
    )(code, rows)


def added(parts):
    total = jnp.zeros(parts[0].shape, F32)
    filled = jnp.zeros(parts[0].shape[1:], jnp.bool_)
    for part in parts:
        held = part[0] < LIMIT
        filled = filled | held
        total = total + jnp.where(held, part, 0.0)
    return jnp.where(filled, total, DEAD)


def merge_kernel(p0, p1, p2, p3, o0, o1, o2, o3):
    for shift, out in enumerate((o0, o1, o2, o3)):
        parts = [part[shift].astype(F32) for part in (p0, p1, p2, p3)]
        out[...] = added(parts).astype(BF16)


def merge_bricks(parts):
    return pl.pallas_call(
        merge_kernel,
        out_shape=(jax.ShapeDtypeStruct((32, 16, 128), BF16),) * 4,
        grid=(4,),
        in_specs=[pl.BlockSpec((4, 8, 16, 128), lambda i: (0, i, 0, 0))] * 4,
        out_specs=(pl.BlockSpec((8, 16, 128), lambda i: (i, 0, 0)),) * 4,
        compiler_params=pltpu.CompilerParams(vmem_limit_bytes=10 << 20),
        cost_estimate=pl.CostEstimate(flops=4 << 20, bytes_accessed=3 << 20, transcendentals=0),
    )(*parts)


def sum_bricks_kernel(
    a0, a1, a2, a3, b0, b1, b2, b3, cot_ref, both_ref, low_ref, high_ref, sums, cells
):
    both_ref[1] = cot_ref[...]
    for half, parts in enumerate(((a0, a1, a2, a3), (b0, b1, b2, b3))):

        def block(step, carry):
            shift_x = half * 2 + step // 2
            shift_y = (step % 2) * 2
            at = pl.ds(pl.multiple_of(step * 8, 8), 8)
            sums[...] = added([part[at].astype(F32) for part in parts]).reshape(128, 128)
            for voxel in range(2):
                for bx in range(2):
                    for by in range(4):
                        slot = voxel * 64 + (bx * 4 + by) * 2
                        spot = (voxel * 2 + bx) * 4 + by
                        cells[spot, 0:4, :] = sums[pl.ds(slot, 4, stride=16), :]
                        cells[spot, 4:8, :] = sums[pl.ds(slot + 1, 4, stride=16), :]
                        both_ref[0, bx * 4 + shift_x, by * 4 + shift_y + voxel] = cells[
                            spot
                        ].astype(BF16)
            return carry

        lax.fori_loop(0, 4, block, 0)
    low_ref[...] = both_ref[:, 0:2]
    high_ref[...] = both_ref[:, 6:8]


def sum_bricks(parts, out_grad):
    return pl.pallas_call(
        sum_bricks_kernel,
        out_shape=(
            jax.ShapeDtypeStruct((2, 8, 16, 8, 128), BF16),
            jax.ShapeDtypeStruct((2, 2, 16, 8, 128), BF16),
            jax.ShapeDtypeStruct((2, 2, 16, 8, 128), BF16),
        ),
        in_specs=[VM] * 9,
        out_specs=(VM,) * 3,
        scratch_shapes=[pltpu.VMEM((128, 128), F32), pltpu.VMEM((16, 8, 128), F32)],
        compiler_params=pltpu.CompilerParams(vmem_limit_bytes=8 << 20),
        cost_estimate=pl.CostEstimate(flops=8 << 20, bytes_accessed=2 << 20, transcendentals=0),
    )(*parts, out_grad)


def ring(axes, shift, place_of):
    size = 4
    return [(place_of(i), place_of((i + shift) % size)) for i in range(size)]


def along_x(value, shift):
    return lax.ppermute(value, ("xl", "xh"), ring(0, shift, lambda i: (i % 2) * 2 + i // 2))


def along_y(value, shift):
    return lax.ppermute(value, "y", ring(0, shift, lambda i: i))


def regroup(rows, target_rank, target_slot, out_grad):
    to_x = target_rank % 2 * 2 + target_rank // 2 % 2
    shift_x = (to_x - (lax.axis_index("xh") * 2 + lax.axis_index("xl"))) & 3
    shift_y = (target_rank // 4 - lax.axis_index("y")) & 3
    code_a = (shift_x * 4 + shift_y) * 16 + target_slot
    code_b = (shift_y * 4 + shift_x) * 16 + target_slot
    placed_a = place_bricks(code_a, rows, 0)
    placed_b = place_bricks(code_b, rows, 1)
    came_a = [placed_a[0]] + [along_x(placed_a[n], n) for n in (1, 2, 3)]
    came_b = [placed_b[0]] + [along_y(placed_b[n], n) for n in (1, 2, 3)]
    merged_a = merge_bricks(came_a)
    merged_b = merge_bricks(came_b)
    came_a = [merged_a[0]] + [along_y(merged_a[n], n) for n in (1, 2, 3)]
    came_b = [merged_b[0]] + [along_x(merged_b[n], n) for n in (1, 2, 3)]
    return sum_bricks(came_a + came_b, out_grad)


def window_rows(ref, x, y, slabs, rows):
    part = ref[pl.ds(x, slabs), pl.ds(y, rows), :, :]
    return part.reshape(slabs * rows * 16, part.shape[3])


def gather_windows(ref, x, rows):
    parts = [window_rows(ref, x + i, j, 1, rows) for i in range(4) for j in range(3)]
    return jnp.concatenate(parts, axis=1)


def convolve_pair(ref, x, rows, weights):
    both = jnp.dot(gather_windows(ref, x, rows), weights[...], preferred_element_type=F32)
    return jnp.concatenate([both[:, 0:128], both[:, 128:256]], axis=0)


def pair_weights(weights):
    blocks = weights.reshape(3, 3, 384, 128)
    left = jnp.pad(blocks, ((0, 1), (0, 0), (0, 0), (0, 0)))
    right = jnp.pad(blocks, ((1, 0), (0, 0), (0, 0), (0, 0)))
    return jnp.concatenate([left, right], axis=3).reshape(4608, 256)


def turned(weights):
    return pair_weights(weights[::-1].transpose(0, 2, 1))


def neighbours(value):
    count = value.shape[0]
    order = (pltpu.roll(value, 1, 0), value, pltpu.roll(value, count - 1, 0))
    return jnp.concatenate([part.astype(BF16) for part in order], axis=1)


PIECES = (
    (2, 8, 16, 8, 128),
    (2, 2, 16, 8, 128),
    (2, 2, 16, 8, 128),
    (2, 12, 2, 8, 128),
    (2, 12, 2, 8, 128),
    (2, 12, 20, 2, 128),
)


def fill(volume, which, pieces, where_ref, outside):
    centre, x_low, x_high, y_low, y_high, z_side = pieces
    volume[...] = jnp.full(volume.shape, outside, F32)
    volume[2:10, 2:18, 2:10, :] = centre[which].astype(F32)
    volume[0:2, 2:18, 2:10, :] = x_low[which].astype(F32)
    volume[10:12, 2:18, 2:10, :] = x_high[which].astype(F32)
    volume[:, 0:2, 2:10, :] = y_low[which].astype(F32)
    volume[:, 18:20, 2:10, :] = y_high[which].astype(F32)

    @pl.when(where_ref[0] == 0)
    def _():
        volume[:, :, 10:12, :] = z_side[which].astype(F32)

    @pl.when(where_ref[0] == 1)
    def _():
        volume[:, :, 0:2, :] = z_side[which].astype(F32)

    @pl.when(where_ref[2] == 0)
    def _():
        volume[0:2] = jnp.full((2, 20, 16, 128), outside, F32)

    @pl.when(where_ref[2] == 7)
    def _():
        volume[10:12] = jnp.full((2, 20, 16, 128), outside, F32)

    @pl.when(where_ref[3] == 0)
    def _():
        volume[:, 0:2] = jnp.full((12, 2, 16, 128), outside, F32)

    @pl.when(where_ref[3] == 7)
    def _():
        volume[:, 18:20] = jnp.full((12, 2, 16, 128), outside, F32)


def grads_kernel(
    where_ref,
    gain,
    p0, p1, p2, p3, p4, p5,
    first_hbm,
    second_hbm,
    act_ref,
    pre3_ref,
    own_ref,
    send_ref,
    cells,
    cots,
    normed3,
    masked3,
    act_t,
    normed_t,
    s0, s1, s2, s3, s4, s5,
    first,
    second_t,
    sems,
):
    core = where_ref[1]
    pieces = (s0, s1, s2, s3, s4, s5)
    copies = [
        pltpu.make_async_copy(source, target, sems.at[n])
        for n, (source, target) in enumerate(
            zip((p0, p1, p2, p3, p4, p5, first_hbm, second_hbm), (*pieces, first, second_t))
        )
    ]
    for copy in copies:
        copy.start()
    for copy in copies[:6]:
        copy.wait()
    fill(cells, 0, pieces, where_ref, OUT)
    fill(cots, 1, pieces, where_ref, 0.0)
    z_of = lax.broadcasted_iota(jnp.int32, (256, 128), 0) % 16
    inside = (z_of >= 2) & (z_of < 10)

    def prepare(x, carry):
        values = cells[x].reshape(320, 128)
        live = jnp.abs(values) < LIMIT
        held = jnp.where(live, values, 0.0)
        inverse = lax.rsqrt(jnp.mean(held * held, axis=-1, keepdims=True) + epsilon)
        normed = held * inverse * gain[...]
        normed3[x] = neighbours(normed).reshape(20, 16, 384)
        masked = jnp.where(live, cots[x].reshape(320, 128), 0.0)
        masked3[x] = neighbours(masked).reshape(20, 16, 384)
        return carry

    lax.fori_loop(0, 12, prepare, 0)

    for turned_ref in (normed_t, act_t):
        turned_ref[:, 0:512] = jnp.zeros((128, 512), BF16)
        turned_ref[:, 2560:3072] = jnp.zeros((128, 512), BF16)

    def turn(x, carry):
        normed = normed3[x + 2, 2:18, :, 128:256].reshape(256, 128).astype(F32)
        columns = pl.ds(pl.multiple_of(x * 256 + 512, 256), 256)
        normed_t[:, columns] = jnp.where(inside, normed, 0.0).T.astype(BF16)
        return carry

    lax.fori_loop(0, 8, turn, 0)
    for copy in copies[6:]:
        copy.wait()

    def convolve(step, carry):
        x = step * 2
        values = cells[pl.ds(x + 1, 2), 1:19, :, :].reshape(576, 128)
        before = convolve_pair(normed3, x, 18, first)
        before = jnp.where(jnp.abs(values) < LIMIT, before, 0.0)
        sigmoid = jax.nn.sigmoid(before)
        active = before * sigmoid
        act_ref[pl.ds(x, 2)] = active.astype(BF16).reshape(2, 18, 16, 128)
        active_grad = convolve_pair(masked3, x, 18, second_t)
        pre = active_grad * sigmoid * (1.0 + before * (1.0 - sigmoid))
        pre = jnp.where(values > -LIMIT, pre, 0.0)
        pre3_ref[pl.ds(x, 2)] = neighbours(pre).reshape(2, 18, 16, 384)
        return carry

    lax.fori_loop(0, 5, convolve, 0)

    def turn_active(x, carry):
        active = act_ref[x + 1, 1:17].reshape(256, 128).astype(F32)
        columns = pl.ds(pl.multiple_of(x * 256 + 512, 256), 256)
        act_t[:, columns] = jnp.where(inside, active, 0.0).T.astype(BF16)
        return carry

    lax.fori_loop(0, 8, turn_active, 0)

    for which, left, right, start in ((1, act_t, masked3, 1), (0, normed_t, pre3_ref, 0)):
        for target, here in ((own_ref, which), (send_ref, 1 - which)):

            @pl.when(core == here)
            def _():
                def weights(j, carry):
                    cot = window_rows(right, start, start + 2 - j, 10, 16)
                    own = [left[:, 256 * (i + 0) : 256 * (i + 10)] for i in range(3)]
                    own = jnp.concatenate(own, axis=0)
                    total = jnp.dot(own, cot, preferred_element_type=F32).astype(BF16)
                    for i in range(3):
                        for k in range(3):
                            target[i * 9 + j * 3 + k] = total[
                                i * 128 : (i + 1) * 128, (2 - k) * 128 : (3 - k) * 128
                            ]
                    return carry

                lax.fori_loop(0, 3, weights, 0)


def grads_call(where, gain, pieces, first, second_t):
    return pl.pallas_call(
        grads_kernel,
        out_shape=(
            jax.ShapeDtypeStruct((10, 18, 16, 128), BF16),
            jax.ShapeDtypeStruct((10, 18, 16, 384), BF16),
            jax.ShapeDtypeStruct((27, 128, 128), BF16),
            jax.ShapeDtypeStruct((27, 128, 128), BF16),
        ),
        in_specs=[SM, VM] + [pl.BlockSpec(memory_space=pl.ANY)] * 8,
        out_specs=(VM,) * 4,
        scratch_shapes=[
            pltpu.VMEM((12, 20, 16, 128), F32),
            pltpu.VMEM((12, 20, 16, 128), F32),
            pltpu.VMEM((12, 20, 16, 384), BF16),
            pltpu.VMEM((12, 20, 16, 384), BF16),
            pltpu.VMEM((128, 3072), BF16),
            pltpu.VMEM((128, 3072), BF16),
            *[pltpu.VMEM(shape, BF16) for shape in PIECES],
            pltpu.VMEM((4608, 256), BF16),
            pltpu.VMEM((4608, 256), BF16),
            pltpu.SemaphoreType.DMA((8,)),
        ],
        compiler_params=pltpu.CompilerParams(vmem_limit_bytes=34 << 20),
        cost_estimate=pl.CostEstimate(flops=10 << 30, bytes_accessed=8 << 20, transcendentals=1 << 20),
    )(where, gain, *pieces, first, second_t)


def outputs_kernel(
    gain, both, act, pre3, second, first_t, block_ref, grad_ref, gain_ref, act3, spread
):
    def prepare(x, carry):
        act3[x] = neighbours(act[x].reshape(288, 128).astype(F32)).reshape(18, 16, 384)
        return carry

    lax.fori_loop(0, 10, prepare, 0)
    gains = gain[...]

    def convolve(step, total):
        x = step * 2
        branch = convolve_pair(act3, x, 16, second)
        spread[...] = branch.reshape(2, 16, 16, 128)
        branch = spread[:, :, 2:10, :].reshape(256, 128)
        values = both[0, pl.ds(x, 2)].astype(F32).reshape(256, 128)
        live = values < LIMIT
        held = jnp.where(live, values, 0.0)
        block = jnp.where(live, branch, 0.0) + held
        block_ref[pl.ds(x, 2)] = block.astype(BF16).reshape(2, 16, 8, 128)
        normed_grad = convolve_pair(pre3, x, 16, first_t)
        spread[...] = normed_grad.reshape(2, 16, 16, 128)
        normed_grad = jnp.where(live, spread[:, :, 2:10, :].reshape(256, 128), 0.0)
        inverse = lax.rsqrt(jnp.mean(held * held, axis=-1, keepdims=True) + epsilon)
        total = total + jnp.sum((normed_grad * held * inverse).reshape(32, 8, 128), axis=0)
        upstream = normed_grad * gains
        centred = jnp.mean(held * upstream, axis=-1, keepdims=True)
        extra = inverse * upstream - held * (inverse * inverse * inverse * centred)
        cot = both[1, pl.ds(x, 2)].astype(F32).reshape(256, 128)
        grad = cot + jnp.where(live, extra, 0.0)
        grad_ref[pl.ds(x, 2)] = grad.astype(BF16).reshape(2, 16, 8, 128)
        return total

    total = lax.fori_loop(0, 4, convolve, jnp.zeros((8, 128), F32))
    gain_ref[...] = total


def outputs_call(gain, both, act, pre3, second, first_t):
    return pl.pallas_call(
        outputs_kernel,
        out_shape=(
            jax.ShapeDtypeStruct((8, 16, 8, 128), BF16),
            jax.ShapeDtypeStruct((8, 16, 8, 128), BF16),
            jax.ShapeDtypeStruct((8, 128), F32),
        ),
        in_specs=[VM] * 6,
        out_specs=(VM,) * 3,
        scratch_shapes=[
            pltpu.VMEM((10, 18, 16, 384), BF16),
            pltpu.VMEM((2, 16, 16, 128), F32),
        ],
        compiler_params=pltpu.CompilerParams(vmem_limit_bytes=20 << 20),
        cost_estimate=pl.CostEstimate(flops=8 << 30, bytes_accessed=6 << 20, transcendentals=4096),
    )(gain, both, act, pre3, second, first_t)


FORWARD = [(i, i + 1) for i in range(7)]
BACKWARD = [(i + 1, i) for i in range(7)]


def edges(both, send_low, send_high):
    x_low = lax.ppermute(send_high, GX, FORWARD)
    x_high = lax.ppermute(send_low, GX, BACKWARD)
    parts = (x_low, both, x_high)
    wide_low = jnp.concatenate([part[:, :, 14:16] for part in parts], axis=1)
    wide_high = jnp.concatenate([part[:, :, 0:2] for part in parts], axis=1)
    y_low = lax.ppermute(wide_low, GY, FORWARD)
    y_high = lax.ppermute(wide_high, GY, BACKWARD)
    side = lax.axis_index(SA)

    def layer(part):
        return jnp.where(side == 0, part[:, :, :, 6:8], part[:, :, :, 0:2])

    middle = jnp.concatenate([layer(part) for part in parts], axis=1)
    sent = jnp.concatenate([layer(y_low), middle, layer(y_high)], axis=2)
    z_side = lax.ppermute(sent, SA, [(0, 1), (1, 0)])
    return both, x_low, x_high, y_low, y_high, z_side


def exchange(values, axes):
    return lax.all_to_all(values, axes, split_axis=0, concat_axis=0, tiled=True)


def local(sweep_bricks, target_rank, target_slot, conv_first, conv_second, norm_gain, out_grad):
    both = regroup(
        sweep_bricks.reshape(128, 64, 128),
        target_rank.reshape(1, 128),
        target_slot.reshape(1, 128),
        out_grad,
    )
    gain = norm_gain.reshape(1, 128)
    first = pair_weights(conv_first)
    second = pair_weights(conv_second)
    first_t = turned(conv_first)
    second_t = turned(conv_second)
    pieces = edges(*both)
    core = lax.axis_index("c")
    where = jnp.stack([lax.axis_index(SA), core, lax.axis_index(GX), lax.axis_index(GY)])
    act, pre3, own, send = grads_call(where.astype(jnp.int32), gain, pieces, first, second_t)
    other = lax.ppermute(send, "c", [(0, 1), (1, 0)])
    pair = (own.astype(F32) + other.astype(F32)).astype(BF16).reshape(16, 216, 128)
    shares = exchange(pair, PLANE)
    block_out, grid_grad, gain_part = outputs_call(gain, pieces[0], act, pre3, second, first_t)

    def halves(row):
        high = row.astype(BF16)
        low = (row - high.astype(F32)).astype(BF16)
        return [high, low, jnp.zeros((6, 128), BF16)]

    def spread(total, row, count):
        sent = jnp.concatenate([total.astype(BF16)] + halves(row), axis=0)
        return jnp.broadcast_to(sent[None], (count, 224, 128))

    total = jnp.sum(shares.astype(F32), axis=0)
    row = jnp.sum(gain_part, axis=0, keepdims=True)
    layers = exchange(spread(total, row, 4), "z").astype(F32)
    total = jnp.sum(layers[:, :216], axis=0)
    row = jnp.sum(layers[:, 216:218], axis=(0, 1))[None]
    gathered = exchange(spread(total, row, 16), PLANE)
    swapped = lax.ppermute(gathered, "c", [(0, 1), (1, 0)])
    factor = 1.0 / math.sqrt(131072.0)

    def weights(low, high):
        picked = jnp.where(core == 0, low[:, :216], high[:, :216])
        return (picked.astype(F32) * factor).reshape(27, 128, 128)

    gains = jnp.sum(gathered[:, 216:218].astype(F32), axis=(0, 1))
    gains = gains + jnp.sum(swapped[:, 216:218].astype(F32), axis=(0, 1))
    return (
        block_out,
        grid_grad,
        weights(gathered, swapped),
        weights(swapped, gathered),
        gains * factor,
    )


def solution(mesh):
    inner = Mesh(mesh.devices.reshape(4, 2, 4, 2, 2), ("y", "xl", "z", "c", "xh"))
    in_specs = (
        P(GX, GY, SA, None, None),
        P(GX, GY, SA, None),
        P(GX, GY, SA),
        P(),
        P(),
        P(),
        P(GX, GY, SA, None),
    )
    out_specs = (P(GX, GY, SA, None), P(GX, GY, SA, None), P(), P(), P())
    return jax.shard_map(local, mesh=inner, in_specs=in_specs, out_specs=out_specs, check_vma=False)
```

```python
import functools
import math

import jax
import jax.numpy as jnp
from jax import lax
from jax.experimental import pallas as pl
from jax.experimental.pallas import tpu as pltpu
from jax.sharding import Mesh
from jax.sharding import PartitionSpec as P

epsilon = 1e-06
DEAD = 1.0e30
OUT = -1.0e30
LIMIT = 1.0e29
GX = ("y", "xl")
GY = ("z", "c")
SA = "xh"
PLANE = ("y", "xl", "xh")
F32 = jnp.float32
BF16 = jnp.bfloat16
VM = pl.BlockSpec(memory_space=pltpu.VMEM)
SM = pl.BlockSpec(memory_space=pltpu.SMEM)
AN = pl.BlockSpec(memory_space=pl.ANY)
HB = pl.BlockSpec(memory_space=pltpu.HBM)


def place_kernel(half, code_ref, rows_hbm, o0, o1, o2, o3, fetched, flat, place, lift, sems):
    step = pl.program_id(0)

    def copy(n):
        voxels = rows_hbm.at[:, pl.ds(half * 32 + n * 8, 8), :]
        return pltpu.make_async_copy(voxels, fetched.at[n], sems.at[n])

    @pl.when(step == 0)
    def _():
        for n in range(4):
            copy(n).start()
        slots = lax.broadcasted_iota(jnp.int32, (256, 128), 0)
        chosen = jnp.where(slots == code_ref[half : half + 1, :], 1.0, 0.0)
        place[...] = chosen.astype(BF16)
        named = jnp.max(chosen, axis=1, keepdims=True)
        lift[...] = jnp.broadcast_to(jnp.where(named > 0.0, 0.0, DEAD), (256, 128))

    for n in range(4):

        @pl.when(step == n)
        def _():
            copy(n).wait()
            flat[...] = fetched[n].astype(F32).reshape(1024, 128)

    for voxel in range(8):
        values = flat[pl.ds(voxel, 128, stride=8), :].astype(BF16)
        summed = jnp.dot(place[...], values, preferred_element_type=F32) + lift[...]
        summed = summed.astype(BF16).reshape(4, 4, 16, 128)
        for shift, out in enumerate((o0, o1, o2, o3)):
            out[:, voxel] = summed[shift]


def place_bricks(code, rows, half):
    return pl.pallas_call(
        functools.partial(place_kernel, half),
        out_shape=(jax.ShapeDtypeStruct((4, 32, 16, 128), BF16),) * 4,
        grid=(4,),
        in_specs=[
            pl.BlockSpec((2, 128), lambda i: (0, 0)),
            HB,
        ],
        out_specs=(pl.BlockSpec((4, 8, 16, 128), lambda i: (0, i, 0, 0)),) * 4,
        scratch_shapes=[
            pltpu.VMEM((4, 128, 8, 128), BF16),
            pltpu.VMEM((1024, 128), F32),
            pltpu.VMEM((256, 128), BF16),
            pltpu.VMEM((256, 128), F32),
            pltpu.SemaphoreType.DMA((4,)),
        ],
        compiler_params=pltpu.CompilerParams(vmem_limit_bytes=10 << 20),
        cost_estimate=pl.CostEstimate(flops=1 << 28, bytes_accessed=3 << 20, transcendentals=0),
    )(code, rows)


def added(parts):
    total = jnp.zeros(parts[0].shape, F32)
    filled = jnp.zeros(parts[0].shape[1:], jnp.bool_)
    for part in parts:
        held = part[0] < LIMIT
        filled = filled | held
        total = total + jnp.where(held, part, 0.0)
    return jnp.where(filled, total, DEAD)


def merge_kernel(p0, p1, p2, p3, o0, o1, o2, o3):
    for shift, out in enumerate((o0, o1, o2, o3)):
        parts = [part[shift].astype(F32) for part in (p0, p1, p2, p3)]
        out[...] = added(parts).astype(BF16)


def merge_bricks(parts):
    return pl.pallas_call(
        merge_kernel,
        out_shape=(jax.ShapeDtypeStruct((32, 16, 128), BF16),) * 4,
        grid=(4,),
        in_specs=[pl.BlockSpec((4, 8, 16, 128), lambda i: (0, i, 0, 0))] * 4,
        out_specs=(pl.BlockSpec((8, 16, 128), lambda i: (i, 0, 0)),) * 4,
        compiler_params=pltpu.CompilerParams(vmem_limit_bytes=10 << 20),
        cost_estimate=pl.CostEstimate(flops=4 << 20, bytes_accessed=3 << 20, transcendentals=0),
    )(*parts)


def sum_bricks_kernel(
    where_ref,
    a0, a1, a2, a3, b0, b1, b2, b3,
    cot_ref,
    both_ref,
    low_ref,
    high_ref,
    layer_ref,
    layer_low_ref,
    layer_high_ref,
    sums,
    cells,
):
    both_ref[1] = cot_ref[...]
    for half, parts in enumerate(((a0, a1, a2, a3), (b0, b1, b2, b3))):

        def block(step, carry):
            shift_x = half * 2 + step // 2
            shift_y = (step % 2) * 2
            at = pl.ds(pl.multiple_of(step * 8, 8), 8)
            sums[...] = added([part[at].astype(F32) for part in parts]).reshape(128, 128)
            for voxel in range(2):
                for bx in range(2):
                    for by in range(4):
                        slot = voxel * 64 + (bx * 4 + by) * 2
                        spot = (voxel * 2 + bx) * 4 + by
                        cells[spot, 0:4, :] = sums[pl.ds(slot, 4, stride=16), :]
                        cells[spot, 4:8, :] = sums[pl.ds(slot + 1, 4, stride=16), :]
                        both_ref[0, bx * 4 + shift_x, by * 4 + shift_y + voxel] = cells[
                            spot
                        ].astype(BF16)
            return carry

        lax.fori_loop(0, 4, block, 0)
    low_ref[...] = both_ref[:, 0:2]
    high_ref[...] = both_ref[:, 6:8]
    for side, rows in ((0, slice(6, 8)), (1, slice(0, 2))):

        @pl.when(where_ref[0] == side)
        def _():
            for n in range(2):
                layer_ref[n] = both_ref[n].astype(F32)[:, :, rows, :].astype(BF16)

    layer_low_ref[...] = layer_ref[:, 0:2]
    layer_high_ref[...] = layer_ref[:, 6:8]


def sum_bricks(where, parts, out_grad):
    return pl.pallas_call(
        sum_bricks_kernel,
        out_shape=(
            jax.ShapeDtypeStruct((2, 8, 16, 8, 128), BF16),
            jax.ShapeDtypeStruct((2, 2, 16, 8, 128), BF16),
            jax.ShapeDtypeStruct((2, 2, 16, 8, 128), BF16),
            jax.ShapeDtypeStruct((2, 8, 16, 2, 128), BF16),
            jax.ShapeDtypeStruct((2, 2, 16, 2, 128), BF16),
            jax.ShapeDtypeStruct((2, 2, 16, 2, 128), BF16),
        ),
        in_specs=[SM] + [VM] * 9,
        out_specs=(VM,) * 6,
        scratch_shapes=[pltpu.VMEM((128, 128), F32), pltpu.VMEM((16, 8, 128), F32)],
        compiler_params=pltpu.CompilerParams(vmem_limit_bytes=8 << 20),
        cost_estimate=pl.CostEstimate(flops=8 << 20, bytes_accessed=2 << 20, transcendentals=0),
    )(where, *parts, out_grad)


def ring(axes, shift, place_of):
    size = 4
    return [(place_of(i), place_of((i + shift) % size)) for i in range(size)]


def along_x(value, shift):
    return lax.ppermute(value, ("xl", "xh"), ring(0, shift, lambda i: (i % 2) * 2 + i // 2))


def along_y(value, shift):
    return lax.ppermute(value, "y", ring(0, shift, lambda i: i))


def regroup(rows, target_rank, target_slot, out_grad, where, weights):
    to_x = target_rank % 2 * 2 + target_rank // 2 % 2
    shift_x = (to_x - (lax.axis_index("xh") * 2 + lax.axis_index("xl"))) & 3
    shift_y = (target_rank // 4 - lax.axis_index("y")) & 3
    major = jnp.concatenate([shift_x, shift_y], axis=0)
    minor = jnp.concatenate([shift_y, shift_x], axis=0)
    codes = (major * 4 + minor) * 16 + target_slot
    placed_a = place_bricks(codes, rows, 0)
    placed_b = place_bricks(codes, rows, 1)
    came_a = [placed_a[0]] + [along_x(placed_a[n], n) for n in (1, 2, 3)]
    came_b = [placed_b[0]] + [along_y(placed_b[n], n) for n in (1, 2, 3)]
    came_a, weights = lax.optimization_barrier((came_a, weights))
    merged_a = merge_bricks(came_a)
    merged_b = merge_bricks(came_b)
    came_a = [merged_a[0]] + [along_y(merged_a[n], n) for n in (1, 2, 3)]
    came_b = [merged_b[0]] + [along_x(merged_b[n], n) for n in (1, 2, 3)]
    return sum_bricks(where, came_a + came_b, out_grad), weights


def window_rows(ref, x, y, slabs, rows):
    part = ref[pl.ds(x, slabs), pl.ds(y, rows), :, :]
    return part.reshape(slabs * rows * 16, part.shape[3])


def gather_windows(ref, x, rows):
    parts = [window_rows(ref, x + i, j, 1, rows) for i in range(4) for j in range(3)]
    return jnp.concatenate(parts, axis=1)


def convolve_pair(ref, x, rows, weights):
    both = jnp.dot(gather_windows(ref, x, rows), weights[...], preferred_element_type=F32)
    return jnp.concatenate([both[:, 0:128], both[:, 128:256]], axis=0)


def pair_weights(weights):
    blocks = weights.reshape(3, 3, 384, 128)
    left = jnp.pad(blocks, ((0, 1), (0, 0), (0, 0), (0, 0)))
    right = jnp.pad(blocks, ((1, 0), (0, 0), (0, 0), (0, 0)))
    return jnp.concatenate([left, right], axis=3).reshape(4608, 256)


def turned(weights):
    return pair_weights(weights[::-1].transpose(0, 2, 1))


def neighbours(value):
    count = value.shape[0]
    order = (pltpu.roll(value, 1, 0), value, pltpu.roll(value, count - 1, 0))
    return jnp.concatenate([part.astype(BF16) for part in order], axis=1)


PIECES = (
    (2, 8, 16, 8, 128),
    (2, 2, 16, 8, 128),
    (2, 2, 16, 8, 128),
    (2, 8, 16, 2, 128),
    (2, 2, 16, 2, 128),
    (2, 2, 16, 2, 128),
    (2, 12, 2, 10, 128),
    (2, 12, 2, 10, 128),
)


def fill(volume, which, pieces, where_ref, outside):
    centre, x_low, x_high, layer, layer_low, layer_high, y_low, y_high = pieces
    volume[...] = jnp.full(volume.shape, outside, F32)
    volume[2:10, 2:18, 2:10, :] = centre[which].astype(F32)
    volume[0:2, 2:18, 2:10, :] = x_low[which].astype(F32)
    volume[10:12, 2:18, 2:10, :] = x_high[which].astype(F32)
    low = y_low[which].astype(F32)
    high = y_high[which].astype(F32)
    volume[:, 0:2, 2:10, :] = low[:, :, 0:8]
    volume[:, 18:20, 2:10, :] = high[:, :, 0:8]
    for side, rows in ((0, slice(10, 12)), (1, slice(0, 2))):

        @pl.when(where_ref[0] == side)
        def _():
            volume[2:10, 2:18, rows, :] = layer[which].astype(F32)
            volume[0:2, 2:18, rows, :] = layer_low[which].astype(F32)
            volume[10:12, 2:18, rows, :] = layer_high[which].astype(F32)
            volume[:, 0:2, rows, :] = low[:, :, 8:10]
            volume[:, 18:20, rows, :] = high[:, :, 8:10]

    @pl.when(where_ref[2] == 0)
    def _():
        volume[0:2] = jnp.full((2, 20, 16, 128), outside, F32)

    @pl.when(where_ref[2] == 7)
    def _():
        volume[10:12] = jnp.full((2, 20, 16, 128), outside, F32)

    @pl.when(where_ref[3] == 0)
    def _():
        volume[:, 0:2] = jnp.full((12, 2, 16, 128), outside, F32)

    @pl.when(where_ref[3] == 7)
    def _():
        volume[:, 18:20] = jnp.full((12, 2, 16, 128), outside, F32)


def grads_kernel(
    where_ref,
    gain,
    p0, p1, p2, p3, p4, p5, p6, p7,
    first_hbm,
    second_hbm,
    act_hbm,
    pre_hbm,
    own_ref,
    send_ref,
    cells,
    cots,
    normed3,
    masked3,
    act_t,
    normed_t,
    s0, s1, s2, s3, s4, s5, s6, s7,
    first,
    second_t,
    act_ref,
    pre_ref,
    pre3_ref,
    sems,
):
    core = where_ref[1]
    pieces = (s0, s1, s2, s3, s4, s5, s6, s7)
    copies = [
        pltpu.make_async_copy(source, target, sems.at[n])
        for n, (source, target) in enumerate(
            zip((p0, p1, p2, p3, p4, p5, p6, p7, first_hbm, second_hbm), (*pieces, first, second_t))
        )
    ]
    for copy in copies:
        copy.start()
    for copy in copies[:8]:
        copy.wait()
    fill(cells, 0, pieces, where_ref, OUT)
    fill(cots, 1, pieces, where_ref, 0.0)
    z_of = lax.broadcasted_iota(jnp.int32, (256, 128), 0) % 16
    inside = (z_of >= 2) & (z_of < 10)

    def prepare(x, carry):
        values = cells[x].reshape(320, 128)
        live = jnp.abs(values) < LIMIT
        held = jnp.where(live, values, 0.0)
        inverse = lax.rsqrt(jnp.mean(held * held, axis=-1, keepdims=True) + epsilon)
        normed = held * inverse * gain[...]
        normed3[x] = neighbours(normed).reshape(20, 16, 384)
        masked = jnp.where(live, cots[x].reshape(320, 128), 0.0)
        masked3[x] = neighbours(masked).reshape(20, 16, 384)
        return carry

    lax.fori_loop(0, 12, prepare, 0)

    for turned_ref in (normed_t, act_t):
        turned_ref[:, 0:512] = jnp.zeros((128, 512), BF16)
        turned_ref[:, 2560:3072] = jnp.zeros((128, 512), BF16)

    def turn(x, carry):
        normed = normed3[x + 2, 2:18, :, 128:256].reshape(256, 128).astype(F32)
        columns = pl.ds(pl.multiple_of(x * 256 + 512, 256), 256)
        normed_t[:, columns] = jnp.where(inside, normed, 0.0).T.astype(BF16)
        return carry

    lax.fori_loop(0, 8, turn, 0)
    for copy in copies[8:]:
        copy.wait()

    def convolve(step, carry):
        x = step * 2
        values = cells[pl.ds(x + 1, 2), 1:19, :, :].reshape(576, 128)
        before = convolve_pair(normed3, x, 18, first)
        before = jnp.where(jnp.abs(values) < LIMIT, before, 0.0)
        sigmoid = jax.nn.sigmoid(before)
        active = before * sigmoid
        act_ref[pl.ds(x, 2)] = active.astype(BF16).reshape(2, 18, 16, 128)
        active_grad = convolve_pair(masked3, x, 18, second_t)
        pre = active_grad * sigmoid * (1.0 + before * (1.0 - sigmoid))
        pre = jnp.where(values > -LIMIT, pre, 0.0)
        pre_ref[pl.ds(x, 2)] = pre.astype(BF16).reshape(2, 18, 16, 128)
        pre3_ref[pl.ds(x, 2)] = neighbours(pre).reshape(2, 18, 16, 384)
        return carry

    lax.fori_loop(0, 5, convolve, 0)
    results = [
        pltpu.make_async_copy(source, target, sems.at[n])
        for n, (source, target) in enumerate(((act_ref, act_hbm), (pre_ref, pre_hbm)))
    ]
    for copy in results:
        copy.start()

    def turn_active(x, carry):
        active = act_ref[x + 1, 1:17].reshape(256, 128).astype(F32)
        columns = pl.ds(pl.multiple_of(x * 256 + 512, 256), 256)
        act_t[:, columns] = jnp.where(inside, active, 0.0).T.astype(BF16)
        return carry

    lax.fori_loop(0, 8, turn_active, 0)

    for which, left, right, start in ((1, act_t, masked3, 1), (0, normed_t, pre3_ref, 0)):
        for target, here in ((own_ref, which), (send_ref, 1 - which)):

            @pl.when(core == here)
            def _():
                def weights(j, carry):
                    cot = window_rows(right, start, start + 2 - j, 10, 16)
                    own = [left[:, 256 * (i + 0) : 256 * (i + 10)] for i in range(3)]
                    own = jnp.concatenate(own, axis=0)
                    total = jnp.dot(own, cot, preferred_element_type=F32).astype(BF16)
                    for i in range(3):
                        for k in range(3):
                            target[i * 9 + j * 3 + k] = total[
                                i * 128 : (i + 1) * 128, (2 - k) * 128 : (3 - k) * 128
                            ]
                    return carry

                lax.fori_loop(0, 3, weights, 0)

    for copy in results:
        copy.wait()


def grads_call(where, gain, pieces, first, second_t):
    return pl.pallas_call(
        grads_kernel,
        out_shape=(
            jax.ShapeDtypeStruct((10, 18, 16, 128), BF16),
            jax.ShapeDtypeStruct((10, 18, 16, 128), BF16),
            jax.ShapeDtypeStruct((27, 128, 128), BF16),
            jax.ShapeDtypeStruct((27, 128, 128), BF16),
        ),
        in_specs=[SM, VM] + [AN] * 8 + [HB] * 2,
        out_specs=(HB, HB, VM, VM),
        scratch_shapes=[
            pltpu.VMEM((12, 20, 16, 128), F32),
            pltpu.VMEM((12, 20, 16, 128), F32),
            pltpu.VMEM((12, 20, 16, 384), BF16),
            pltpu.VMEM((12, 20, 16, 384), BF16),
            pltpu.VMEM((128, 3072), BF16),
            pltpu.VMEM((128, 3072), BF16),
            *[pltpu.VMEM(shape, BF16) for shape in PIECES],
            pltpu.VMEM((4608, 256), BF16),
            pltpu.VMEM((4608, 256), BF16),
            pltpu.VMEM((10, 18, 16, 128), BF16),
            pltpu.VMEM((10, 18, 16, 128), BF16),
            pltpu.VMEM((10, 18, 16, 384), BF16),
            pltpu.SemaphoreType.DMA((10,)),
        ],
        compiler_params=pltpu.CompilerParams(vmem_limit_bytes=34 << 20),
        cost_estimate=pl.CostEstimate(flops=10 << 30, bytes_accessed=8 << 20, transcendentals=1 << 20),
    )(where, gain, *pieces, first, second_t)


def outputs_kernel(
    gain,
    both_hbm,
    act_hbm,
    pre_hbm,
    second_hbm,
    first_hbm,
    block_ref,
    grad_ref,
    gain_ref,
    both,
    act,
    pre,
    second,
    first_t,
    act3,
    pre3,
    spread,
    sems,
):
    copies = [
        pltpu.make_async_copy(source, target, sems.at[n])
        for n, (source, target) in enumerate(
            (
                (act_hbm, act),
                (pre_hbm, pre),
                (both_hbm, both),
                (second_hbm, second),
                (first_hbm, first_t),
            )
        )
    ]
    for copy in copies:
        copy.start()
    for copy, source, target in ((copies[0], act, act3), (copies[1], pre, pre3)):
        copy.wait()

        def prepare(x, carry):
            values = source[x].reshape(288, 128).astype(F32)
            target[x] = neighbours(values).reshape(18, 16, 384)
            return carry

        lax.fori_loop(0, 10, prepare, 0)

    for copy in copies[2:]:
        copy.wait()
    gains = gain[...]

    def convolve(step, total):
        x = step * 2
        branch = convolve_pair(act3, x, 16, second)
        spread[...] = branch.reshape(2, 16, 16, 128)
        branch = spread[:, :, 2:10, :].reshape(256, 128)
        values = both[0, pl.ds(x, 2)].astype(F32).reshape(256, 128)
        live = values < LIMIT
        held = jnp.where(live, values, 0.0)
        block = jnp.where(live, branch, 0.0) + held
        block_ref[pl.ds(x, 2)] = block.astype(BF16).reshape(2, 16, 8, 128)
        normed_grad = convolve_pair(pre3, x, 16, first_t)
        spread[...] = normed_grad.reshape(2, 16, 16, 128)
        normed_grad = jnp.where(live, spread[:, :, 2:10, :].reshape(256, 128), 0.0)
        inverse = lax.rsqrt(jnp.mean(held * held, axis=-1, keepdims=True) + epsilon)
        total = total + jnp.sum((normed_grad * held * inverse).reshape(32, 8, 128), axis=0)
        upstream = normed_grad * gains
        centred = jnp.mean(held * upstream, axis=-1, keepdims=True)
        extra = inverse * upstream - held * (inverse * inverse * inverse * centred)
        cot = both[1, pl.ds(x, 2)].astype(F32).reshape(256, 128)
        grad = cot + jnp.where(live, extra, 0.0)
        grad_ref[pl.ds(x, 2)] = grad.astype(BF16).reshape(2, 16, 8, 128)
        return total

    total = lax.fori_loop(0, 4, convolve, jnp.zeros((8, 128), F32))
    gain_ref[...] = total


def outputs_call(gain, both, act, pre, second, first_t):
    return pl.pallas_call(
        outputs_kernel,
        out_shape=(
            jax.ShapeDtypeStruct((8, 16, 8, 128), BF16),
            jax.ShapeDtypeStruct((8, 16, 8, 128), BF16),
            jax.ShapeDtypeStruct((8, 128), F32),
        ),
        in_specs=[VM, AN, HB, HB, HB, HB],
        out_specs=(VM,) * 3,
        scratch_shapes=[
            pltpu.VMEM((2, 8, 16, 8, 128), BF16),
            pltpu.VMEM((10, 18, 16, 128), BF16),
            pltpu.VMEM((10, 18, 16, 128), BF16),
            pltpu.VMEM((4608, 256), BF16),
            pltpu.VMEM((4608, 256), BF16),
            pltpu.VMEM((10, 18, 16, 384), BF16),
            pltpu.VMEM((10, 18, 16, 384), BF16),
            pltpu.VMEM((2, 16, 16, 128), F32),
            pltpu.SemaphoreType.DMA((5,)),
        ],
        compiler_params=pltpu.CompilerParams(vmem_limit_bytes=20 << 20),
        cost_estimate=pl.CostEstimate(flops=8 << 30, bytes_accessed=6 << 20, transcendentals=4096),
    )(gain, both, act, pre, second, first_t)


def add_kernel(own_ref, other_ref, out_ref):
    out_ref[...] = (own_ref[...].astype(F32) + other_ref[...].astype(F32)).astype(BF16)


def add_pair(own, other):
    spec = pl.BlockSpec((9, 128, 128), lambda i: (i, 0, 0))
    return pl.pallas_call(
        add_kernel,
        out_shape=jax.ShapeDtypeStruct((27, 128, 128), BF16),
        grid=(3,),
        in_specs=[spec, spec],
        out_specs=spec,
        compiler_params=pltpu.CompilerParams(vmem_limit_bytes=6 << 20),
        cost_estimate=pl.CostEstimate(flops=1 << 19, bytes_accessed=3 << 20, transcendentals=0),
    )(own, other)


FORWARD = [(i, i + 1) for i in range(7)]
BACKWARD = [(i + 1, i) for i in range(7)]


def edges(both, send_low, send_high, layer, layer_low, layer_high):
    far = [(a * 2 + s, b * 2 + 1 - s) for a, b in FORWARD for s in range(2)]
    near = [(a * 2 + s, b * 2 + 1 - s) for a, b in BACKWARD for s in range(2)]
    x_low = lax.ppermute(send_high, GX, FORWARD)
    x_high = lax.ppermute(send_low, GX, BACKWARD)
    came = lax.ppermute(layer, SA, [(0, 1), (1, 0)])
    came_low = lax.ppermute(layer_high, PLANE, far)
    came_high = lax.ppermute(layer_low, PLANE, near)

    def wide(rows):
        inner = jnp.concatenate([part[:, :, rows] for part in (x_low, both, x_high)], axis=1)
        outer = jnp.concatenate([part[:, :, rows] for part in (came_low, came, came_high)], axis=1)
        return jnp.concatenate([inner, outer], axis=3)

    y_low = lax.ppermute(wide(slice(14, 16)), GY, FORWARD)
    y_high = lax.ppermute(wide(slice(0, 2)), GY, BACKWARD)
    return both, x_low, x_high, came, came_low, came_high, y_low, y_high


def exchange(values, axes):
    return lax.all_to_all(values, axes, split_axis=0, concat_axis=0, tiled=True)


def local(sweep_bricks, target_rank, target_slot, conv_first, conv_second, norm_gain, out_grad):
    gain = norm_gain.reshape(1, 128)
    core = lax.axis_index("c")
    where = jnp.stack([lax.axis_index(SA), core, lax.axis_index(GX), lax.axis_index(GY)])
    where = where.astype(jnp.int32)
    both, (first, second, first_t, second_t) = regroup(
        sweep_bricks.reshape(128, 64, 128),
        target_rank.reshape(1, 128),
        target_slot.reshape(1, 128),
        out_grad,
        where,
        (
            pair_weights(conv_first),
            pair_weights(conv_second),
            turned(conv_first),
            turned(conv_second),
        ),
    )
    pieces = edges(*both)
    act, pre, own, send = grads_call(where, gain, pieces, first, second_t)
    other = lax.ppermute(send, "c", [(0, 1), (1, 0)])
    shares = exchange(add_pair(own, other).reshape(16, 216, 128), PLANE)
    block_out, grid_grad, gain_part = outputs_call(gain, pieces[0], act, pre, second, first_t)

    def halves(row):
        high = row.astype(BF16)
        low = (row - high.astype(F32)).astype(BF16)
        return [high, low, jnp.zeros((6, 128), BF16)]

    def joined(total, row):
        return jnp.concatenate([total.astype(BF16)] + halves(row), axis=0)

    total = jnp.sum(shares.astype(F32), axis=0)
    sent = joined(total, jnp.sum(gain_part, axis=0, keepdims=True))
    parts = [sent] + [
        lax.ppermute(sent, "z", [(i, (i + shift) % 4) for i in range(4)]) for shift in (1, 2, 3)
    ]
    parts = [part.astype(F32) for part in parts]
    layers = (parts[0] + parts[2]) + (parts[1] + parts[3])
    sent = joined(layers[:216], layers[216:217] + layers[217:218])
    gathered = exchange(jnp.broadcast_to(sent[None], (16, 224, 128)), PLANE)
    swapped = lax.ppermute(gathered, "c", [(0, 1), (1, 0)])
    factor = 1.0 / math.sqrt(131072.0)

    def weights(low, high):
        picked = jnp.where(core == 0, low[:, :216], high[:, :216])
        return (picked.astype(F32) * factor).reshape(27, 128, 128)

    gains = jnp.sum(gathered[:, 216:218].astype(F32), axis=(0, 1))
    gains = gains + jnp.sum(swapped[:, 216:218].astype(F32), axis=(0, 1))
    return (
        block_out,
        grid_grad,
        weights(gathered, swapped),
        weights(swapped, gathered),
        gains * factor,
    )


def solution(mesh):
    inner = Mesh(mesh.devices.reshape(4, 2, 4, 2, 2), ("y", "xl", "z", "c", "xh"))
    in_specs = (
        P(GX, GY, SA, None, None),
        P(GX, GY, SA, None),
        P(GX, GY, SA),
        P(),
        P(),
        P(),
        P(GX, GY, SA, None),
    )
    out_specs = (P(GX, GY, SA, None), P(GX, GY, SA, None), P(), P(), P())
    return jax.shard_map(local, mesh=inner, in_specs=in_specs, out_specs=out_specs, check_vma=False)
```

```python
import functools
import math

import jax
import jax.numpy as jnp
from jax import lax
from jax.experimental import pallas as pl
from jax.experimental.pallas import tpu as pltpu
from jax.sharding import Mesh
from jax.sharding import PartitionSpec as P

epsilon = 1e-06
DEAD = 1.0e30
OUT = -1.0e30
LIMIT = 1.0e29
GX = ("y", "xl")
GY = ("z", "c")
SA = "xh"
PLANE = ("y", "xl", "xh")
F32 = jnp.float32
BF16 = jnp.bfloat16
VM = pl.BlockSpec(memory_space=pltpu.VMEM)
SM = pl.BlockSpec(memory_space=pltpu.SMEM)
AN = pl.BlockSpec(memory_space=pl.ANY)
HB = pl.BlockSpec(memory_space=pltpu.HBM)


def place_kernel(half, code_ref, rows_hbm, o0, o1, o2, o3, fetched, flat, place, lift, sems):
    step = pl.program_id(0)

    def copy(n):
        voxels = rows_hbm.at[:, pl.ds(half * 32 + n * 8, 8), :]
        return pltpu.make_async_copy(voxels, fetched.at[n], sems.at[n])

    @pl.when(step == 0)
    def _():
        for n in range(4):
            copy(n).start()
        slots = lax.broadcasted_iota(jnp.int32, (256, 128), 0)
        chosen = jnp.where(slots == code_ref[half : half + 1, :], 1.0, 0.0)
        place[...] = chosen.astype(BF16)
        named = jnp.max(chosen, axis=1, keepdims=True)
        lift[...] = jnp.broadcast_to(jnp.where(named > 0.0, 0.0, DEAD), (256, 128))

    for n in range(4):

        @pl.when(step == n)
        def _():
            copy(n).wait()
            flat[...] = fetched[n].astype(F32).reshape(1024, 128)

    for voxel in range(8):
        values = flat[pl.ds(voxel, 128, stride=8), :].astype(BF16)
        summed = jnp.dot(place[...], values, preferred_element_type=F32) + lift[...]
        summed = summed.astype(BF16).reshape(4, 4, 16, 128)
        for shift, out in enumerate((o0, o1, o2, o3)):
            out[:, voxel] = summed[shift]


def place_bricks(code, rows, half):
    return pl.pallas_call(
        functools.partial(place_kernel, half),
        out_shape=(jax.ShapeDtypeStruct((4, 32, 16, 128), BF16),) * 4,
        grid=(4,),
        in_specs=[
            pl.BlockSpec((2, 128), lambda i: (0, 0)),
            HB,
        ],
        out_specs=(pl.BlockSpec((4, 8, 16, 128), lambda i: (0, i, 0, 0)),) * 4,
        scratch_shapes=[
            pltpu.VMEM((4, 128, 8, 128), BF16),
            pltpu.VMEM((1024, 128), F32),
            pltpu.VMEM((256, 128), BF16),
            pltpu.VMEM((256, 128), F32),
            pltpu.SemaphoreType.DMA((4,)),
        ],
        compiler_params=pltpu.CompilerParams(vmem_limit_bytes=10 << 20),
        cost_estimate=pl.CostEstimate(flops=1 << 28, bytes_accessed=3 << 20, transcendentals=0),
    )(code, rows)


def added(parts):
    total = jnp.zeros(parts[0].shape, F32)
    filled = jnp.zeros(parts[0].shape[1:], jnp.bool_)
    for part in parts:
        held = part[0] < LIMIT
        filled = filled | held
        total = total + jnp.where(held, part, 0.0)
    return jnp.where(filled, total, DEAD)


def merge_kernel(p0, p1, p2, p3, o0, o1, o2, o3):
    for shift, out in enumerate((o0, o1, o2, o3)):
        parts = [part[shift].astype(F32) for part in (p0, p1, p2, p3)]
        out[...] = added(parts).astype(BF16)


def merge_bricks(parts):
    return pl.pallas_call(
        merge_kernel,
        out_shape=(jax.ShapeDtypeStruct((32, 16, 128), BF16),) * 4,
        grid=(4,),
        in_specs=[pl.BlockSpec((4, 8, 16, 128), lambda i: (0, i, 0, 0))] * 4,
        out_specs=(pl.BlockSpec((8, 16, 128), lambda i: (i, 0, 0)),) * 4,
        compiler_params=pltpu.CompilerParams(vmem_limit_bytes=10 << 20),
        cost_estimate=pl.CostEstimate(flops=4 << 20, bytes_accessed=3 << 20, transcendentals=0),
    )(*parts)


def send_rows(place, top):
    odd = place % 2
    return top - top * odd, top * odd


def sum_bricks_kernel(
    where_ref,
    a0, a1, a2, a3, b0, b1, b2, b3,
    cot_ref,
    both_ref,
    one_ref,
    two_ref,
    layer_ref,
    layer_one_ref,
    layer_two_ref,
    sums,
    cells,
):
    both_ref[1] = cot_ref[...]
    for half, parts in enumerate(((a0, a1, a2, a3), (b0, b1, b2, b3))):

        def block(step, carry):
            shift_x = half * 2 + step // 2
            shift_y = (step % 2) * 2
            at = pl.ds(pl.multiple_of(step * 8, 8), 8)
            sums[...] = added([part[at].astype(F32) for part in parts]).reshape(128, 128)
            for voxel in range(2):
                for bx in range(2):
                    for by in range(4):
                        slot = voxel * 64 + (bx * 4 + by) * 2
                        spot = (voxel * 2 + bx) * 4 + by
                        cells[spot, 0:4, :] = sums[pl.ds(slot, 4, stride=16), :]
                        cells[spot, 4:8, :] = sums[pl.ds(slot + 1, 4, stride=16), :]
                        both_ref[0, bx * 4 + shift_x, by * 4 + shift_y + voxel] = cells[
                            spot
                        ].astype(BF16)
            return carry

        lax.fori_loop(0, 4, block, 0)
    first_x, second_x = send_rows(where_ref[2], 6)
    one_ref[...] = both_ref[:, pl.ds(first_x, 2)]
    two_ref[...] = both_ref[:, pl.ds(second_x, 2)]
    for side, rows in ((0, slice(6, 8)), (1, slice(0, 2))):

        @pl.when(where_ref[0] == side)
        def _():
            for n in range(2):
                layer_ref[n] = both_ref[n].astype(F32)[:, :, rows, :].astype(BF16)

    layer_one_ref[...] = layer_ref[:, pl.ds(first_x, 2)]
    layer_two_ref[...] = layer_ref[:, pl.ds(second_x, 2)]


def sum_bricks(where, parts, out_grad):
    return pl.pallas_call(
        sum_bricks_kernel,
        out_shape=(
            jax.ShapeDtypeStruct((2, 8, 16, 8, 128), BF16),
            jax.ShapeDtypeStruct((2, 2, 16, 8, 128), BF16),
            jax.ShapeDtypeStruct((2, 2, 16, 8, 128), BF16),
            jax.ShapeDtypeStruct((2, 8, 16, 2, 128), BF16),
            jax.ShapeDtypeStruct((2, 2, 16, 2, 128), BF16),
            jax.ShapeDtypeStruct((2, 2, 16, 2, 128), BF16),
        ),
        in_specs=[SM] + [VM] * 9,
        out_specs=(VM,) * 6,
        scratch_shapes=[pltpu.VMEM((128, 128), F32), pltpu.VMEM((16, 8, 128), F32)],
        compiler_params=pltpu.CompilerParams(vmem_limit_bytes=8 << 20),
        cost_estimate=pl.CostEstimate(flops=8 << 20, bytes_accessed=2 << 20, transcendentals=0),
    )(where, *parts, out_grad)


def along_x(value, shift):
    def place(chip):
        return chip % 2 * 2 + chip // 2

    pairs = [(place(chip), place((chip + shift) % 4)) for chip in range(4)]
    return lax.ppermute(value, ("xl", "xh"), pairs)


def along(axis, value, shift):
    return lax.ppermute(value, axis, [(i, (i + shift) % 4) for i in range(4)])


def regroup(rows, target_rank, target_slot, out_grad, where, weights):
    to_x = target_rank % 2 * 2 + target_rank // 2 % 2
    shift_x = (to_x - (lax.axis_index("xh") * 2 + lax.axis_index("xl"))) & 3
    shift_y = (target_rank // 4 - lax.axis_index("y")) & 3
    major = jnp.concatenate([shift_x, shift_y], axis=0)
    minor = jnp.concatenate([shift_y, shift_x], axis=0)
    codes = (major * 4 + minor) * 16 + target_slot
    placed_a = place_bricks(codes, rows, 0)
    placed_b = place_bricks(codes, rows, 1)
    came_a = [placed_a[0]] + [along_x(placed_a[n], n) for n in (1, 2, 3)]
    came_b = [placed_b[0]] + [along("y", placed_b[n], n) for n in (1, 2, 3)]
    came_a, weights = lax.optimization_barrier((came_a, weights))
    merged_a = merge_bricks(came_a)
    merged_b = merge_bricks(came_b)
    came_a = [merged_a[0]] + [along("y", merged_a[n], n) for n in (1, 2, 3)]
    came_b = [merged_b[0]] + [along_x(merged_b[n], n) for n in (1, 2, 3)]
    return sum_bricks(where, came_a + came_b, out_grad), weights


def window_rows(ref, x, y, slabs, rows):
    part = ref[pl.ds(x, slabs), pl.ds(y, rows), :, :]
    return part.reshape(slabs * rows * 16, part.shape[3])


def gather_windows(ref, x, rows):
    parts = [window_rows(ref, x + i, j, 1, rows) for i in range(4) for j in range(3)]
    return jnp.concatenate(parts, axis=1)


def convolve_pair(ref, x, rows, weights):
    both = jnp.dot(gather_windows(ref, x, rows), weights[...], preferred_element_type=F32)
    return jnp.concatenate([both[:, 0:128], both[:, 128:256]], axis=0)


def pair_weights(weights):
    blocks = weights.reshape(3, 3, 384, 128)
    left = jnp.pad(blocks, ((0, 1), (0, 0), (0, 0), (0, 0)))
    right = jnp.pad(blocks, ((1, 0), (0, 0), (0, 0), (0, 0)))
    return jnp.concatenate([left, right], axis=3).reshape(4608, 256)


def turned(weights):
    return pair_weights(weights[::-1].transpose(0, 2, 1))


def neighbours(value):
    count = value.shape[0]
    order = (pltpu.roll(value, 1, 0), value, pltpu.roll(value, count - 1, 0))
    return jnp.concatenate([part.astype(BF16) for part in order], axis=1)


PIECES = (
    (2, 8, 16, 8, 128),
    (2, 2, 16, 8, 128),
    (2, 2, 16, 8, 128),
    (2, 8, 16, 2, 128),
    (2, 2, 16, 2, 128),
    (2, 2, 16, 2, 128),
    (2, 12, 2, 10, 128),
    (2, 12, 2, 10, 128),
)


def fill(volume, which, pieces, where_ref, outside):
    centre, x_one, x_two, layer, layer_one, layer_two, y_one, y_two = pieces
    first_x, second_x = send_rows(where_ref[2], 10)
    first_y, second_y = send_rows(where_ref[3], 18)
    at_one = pl.ds(first_x, 2)
    at_two = pl.ds(second_x, 2)
    volume[...] = jnp.full(volume.shape, outside, F32)
    volume[2:10, 2:18, 2:10, :] = centre[which].astype(F32)
    volume[at_one, 2:18, 2:10, :] = x_one[which].astype(F32)
    volume[at_two, 2:18, 2:10, :] = x_two[which].astype(F32)
    sides = ((y_one, pl.ds(first_y, 2)), (y_two, pl.ds(second_y, 2)))
    spans = ((at_one, slice(0, 2)), (slice(2, 10), slice(2, 10)), (at_two, slice(10, 12)))
    for came, at_y in sides:
        values = came[which].astype(F32)
        for at_x, rows in spans:
            volume[at_x, at_y, 2:10, :] = values[rows, :, 0:8]
    for side, at_z in ((0, slice(10, 12)), (1, slice(0, 2))):

        @pl.when(where_ref[0] == side)
        def _():
            volume[2:10, 2:18, at_z, :] = layer[which].astype(F32)
            volume[at_one, 2:18, at_z, :] = layer_one[which].astype(F32)
            volume[at_two, 2:18, at_z, :] = layer_two[which].astype(F32)
            for came, at_y in sides:
                values = came[which].astype(F32)
                for at_x, rows in spans:
                    volume[at_x, at_y, at_z, :] = values[rows, :, 8:10]

    @pl.when(where_ref[2] == 0)
    def _():
        volume[0:2] = jnp.full((2, 20, 16, 128), outside, F32)

    @pl.when(where_ref[2] == 7)
    def _():
        volume[10:12] = jnp.full((2, 20, 16, 128), outside, F32)

    @pl.when(where_ref[3] == 0)
    def _():
        volume[:, 0:2] = jnp.full((12, 2, 16, 128), outside, F32)

    @pl.when(where_ref[3] == 7)
    def _():
        volume[:, 18:20] = jnp.full((12, 2, 16, 128), outside, F32)


def grads_kernel(
    where_ref,
    gain,
    p0, p1, p2, p3, p4, p5, p6, p7,
    first_hbm,
    second_hbm,
    act_hbm,
    pre_hbm,
    own_ref,
    send_ref,
    cells,
    cots,
    normed3,
    masked3,
    act_t,
    normed_t,
    s0, s1, s2, s3, s4, s5, s6, s7,
    first,
    second_t,
    act_ref,
    pre_ref,
    pre3_ref,
    sems,
):
    core = where_ref[1]
    pieces = (s0, s1, s2, s3, s4, s5, s6, s7)
    copies = [
        pltpu.make_async_copy(source, target, sems.at[n])
        for n, (source, target) in enumerate(
            zip((p0, p1, p2, p3, p4, p5, p6, p7, first_hbm, second_hbm), (*pieces, first, second_t))
        )
    ]
    for copy in copies:
        copy.start()
    for copy in copies[:8]:
        copy.wait()
    fill(cells, 0, pieces, where_ref, OUT)
    fill(cots, 1, pieces, where_ref, 0.0)
    z_of = lax.broadcasted_iota(jnp.int32, (256, 128), 0) % 16
    inside = (z_of >= 2) & (z_of < 10)

    def prepare(x, carry):
        values = cells[x].reshape(320, 128)
        live = jnp.abs(values) < LIMIT
        held = jnp.where(live, values, 0.0)
        inverse = lax.rsqrt(jnp.mean(held * held, axis=-1, keepdims=True) + epsilon)
        normed = held * inverse * gain[...]
        normed3[x] = neighbours(normed).reshape(20, 16, 384)
        masked = jnp.where(live, cots[x].reshape(320, 128), 0.0)
        masked3[x] = neighbours(masked).reshape(20, 16, 384)
        return carry

    lax.fori_loop(0, 12, prepare, 0)

    for turned_ref in (normed_t, act_t):
        turned_ref[:, 0:512] = jnp.zeros((128, 512), BF16)
        turned_ref[:, 2560:3072] = jnp.zeros((128, 512), BF16)

    def turn(x, carry):
        normed = normed3[x + 2, 2:18, :, 128:256].reshape(256, 128).astype(F32)
        columns = pl.ds(pl.multiple_of(x * 256 + 512, 256), 256)
        normed_t[:, columns] = jnp.where(inside, normed, 0.0).T.astype(BF16)
        return carry

    lax.fori_loop(0, 8, turn, 0)
    for copy in copies[8:]:
        copy.wait()

    def convolve(step, carry):
        x = step * 2
        values = cells[pl.ds(x + 1, 2), 1:19, :, :].reshape(576, 128)
        before = convolve_pair(normed3, x, 18, first)
        before = jnp.where(jnp.abs(values) < LIMIT, before, 0.0)
        sigmoid = jax.nn.sigmoid(before)
        active = before * sigmoid
        act_ref[pl.ds(x, 2)] = active.astype(BF16).reshape(2, 18, 16, 128)
        active_grad = convolve_pair(masked3, x, 18, second_t)
        pre = active_grad * sigmoid * (1.0 + before * (1.0 - sigmoid))
        pre = jnp.where(values > -LIMIT, pre, 0.0)
        pre_ref[pl.ds(x, 2)] = pre.astype(BF16).reshape(2, 18, 16, 128)
        pre3_ref[pl.ds(x, 2)] = neighbours(pre).reshape(2, 18, 16, 384)
        return carry

    lax.fori_loop(0, 5, convolve, 0)
    results = [
        pltpu.make_async_copy(source, target, sems.at[n])
        for n, (source, target) in enumerate(((act_ref, act_hbm), (pre_ref, pre_hbm)))
    ]
    for copy in results:
        copy.start()

    def turn_active(x, carry):
        active = act_ref[x + 1, 1:17].reshape(256, 128).astype(F32)
        columns = pl.ds(pl.multiple_of(x * 256 + 512, 256), 256)
        act_t[:, columns] = jnp.where(inside, active, 0.0).T.astype(BF16)
        return carry

    lax.fori_loop(0, 8, turn_active, 0)

    for which, left, right, start in ((1, act_t, masked3, 1), (0, normed_t, pre3_ref, 0)):
        for target, here in ((own_ref, which), (send_ref, 1 - which)):

            @pl.when(core == here)
            def _():
                def weights(j, carry):
                    cot = window_rows(right, start, start + 2 - j, 10, 16)
                    own = [left[:, 256 * (i + 0) : 256 * (i + 10)] for i in range(3)]
                    own = jnp.concatenate(own, axis=0)
                    total = jnp.dot(own, cot, preferred_element_type=F32).astype(BF16)
                    for i in range(3):
                        for k in range(3):
                            target[i * 9 + j * 3 + k] = total[
                                i * 128 : (i + 1) * 128, (2 - k) * 128 : (3 - k) * 128
                            ]
                    return carry

                lax.fori_loop(0, 3, weights, 0)

    for copy in results:
        copy.wait()


def grads_call(where, gain, pieces, first, second_t):
    return pl.pallas_call(
        grads_kernel,
        out_shape=(
            jax.ShapeDtypeStruct((10, 18, 16, 128), BF16),
            jax.ShapeDtypeStruct((10, 18, 16, 128), BF16),
            jax.ShapeDtypeStruct((27, 128, 128), BF16),
            jax.ShapeDtypeStruct((27, 128, 128), BF16),
        ),
        in_specs=[SM, VM] + [AN] * 8 + [HB] * 2,
        out_specs=(HB, HB, VM, VM),
        scratch_shapes=[
            pltpu.VMEM((12, 20, 16, 128), F32),
            pltpu.VMEM((12, 20, 16, 128), F32),
            pltpu.VMEM((12, 20, 16, 384), BF16),
            pltpu.VMEM((12, 20, 16, 384), BF16),
            pltpu.VMEM((128, 3072), BF16),
            pltpu.VMEM((128, 3072), BF16),
            *[pltpu.VMEM(shape, BF16) for shape in PIECES],
            pltpu.VMEM((4608, 256), BF16),
            pltpu.VMEM((4608, 256), BF16),
            pltpu.VMEM((10, 18, 16, 128), BF16),
            pltpu.VMEM((10, 18, 16, 128), BF16),
            pltpu.VMEM((10, 18, 16, 384), BF16),
            pltpu.SemaphoreType.DMA((10,)),
        ],
        compiler_params=pltpu.CompilerParams(vmem_limit_bytes=34 << 20),
        cost_estimate=pl.CostEstimate(flops=10 << 30, bytes_accessed=8 << 20, transcendentals=1 << 20),
    )(where, gain, *pieces, first, second_t)


def outputs_kernel(
    gain,
    both_hbm,
    act_hbm,
    pre_hbm,
    second_hbm,
    first_hbm,
    block_ref,
    grad_ref,
    gain_ref,
    both,
    act,
    pre,
    second,
    first_t,
    act3,
    pre3,
    spread,
    sems,
):
    copies = [
        pltpu.make_async_copy(source, target, sems.at[n])
        for n, (source, target) in enumerate(
            (
                (act_hbm, act),
                (pre_hbm, pre),
                (both_hbm, both),
                (second_hbm, second),
                (first_hbm, first_t),
            )
        )
    ]
    for copy in copies:
        copy.start()
    for copy, source, target in ((copies[0], act, act3), (copies[1], pre, pre3)):
        copy.wait()

        def prepare(x, carry):
            values = source[x].reshape(288, 128).astype(F32)
            target[x] = neighbours(values).reshape(18, 16, 384)
            return carry

        lax.fori_loop(0, 10, prepare, 0)

    for copy in copies[2:]:
        copy.wait()
    gains = gain[...]

    def convolve(step, total):
        x = step * 2
        branch = convolve_pair(act3, x, 16, second)
        spread[...] = branch.reshape(2, 16, 16, 128)
        branch = spread[:, :, 2:10, :].reshape(256, 128)
        values = both[0, pl.ds(x, 2)].astype(F32).reshape(256, 128)
        live = values < LIMIT
        held = jnp.where(live, values, 0.0)
        block = jnp.where(live, branch, 0.0) + held
        block_ref[pl.ds(x, 2)] = block.astype(BF16).reshape(2, 16, 8, 128)
        normed_grad = convolve_pair(pre3, x, 16, first_t)
        spread[...] = normed_grad.reshape(2, 16, 16, 128)
        normed_grad = jnp.where(live, spread[:, :, 2:10, :].reshape(256, 128), 0.0)
        inverse = lax.rsqrt(jnp.mean(held * held, axis=-1, keepdims=True) + epsilon)
        total = total + jnp.sum((normed_grad * held * inverse).reshape(32, 8, 128), axis=0)
        upstream = normed_grad * gains
        centred = jnp.mean(held * upstream, axis=-1, keepdims=True)
        extra = inverse * upstream - held * (inverse * inverse * inverse * centred)
        cot = both[1, pl.ds(x, 2)].astype(F32).reshape(256, 128)
        grad = cot + jnp.where(live, extra, 0.0)
        grad_ref[pl.ds(x, 2)] = grad.astype(BF16).reshape(2, 16, 8, 128)
        return total

    total = lax.fori_loop(0, 4, convolve, jnp.zeros((8, 128), F32))
    gain_ref[...] = total


def outputs_call(gain, both, act, pre, second, first_t):
    return pl.pallas_call(
        outputs_kernel,
        out_shape=(
            jax.ShapeDtypeStruct((8, 16, 8, 128), BF16),
            jax.ShapeDtypeStruct((8, 16, 8, 128), BF16),
            jax.ShapeDtypeStruct((8, 128), F32),
        ),
        in_specs=[VM, AN, HB, HB, HB, HB],
        out_specs=(VM,) * 3,
        scratch_shapes=[
            pltpu.VMEM((2, 8, 16, 8, 128), BF16),
            pltpu.VMEM((10, 18, 16, 128), BF16),
            pltpu.VMEM((10, 18, 16, 128), BF16),
            pltpu.VMEM((4608, 256), BF16),
            pltpu.VMEM((4608, 256), BF16),
            pltpu.VMEM((10, 18, 16, 384), BF16),
            pltpu.VMEM((10, 18, 16, 384), BF16),
            pltpu.VMEM((2, 16, 16, 128), F32),
            pltpu.SemaphoreType.DMA((5,)),
        ],
        compiler_params=pltpu.CompilerParams(vmem_limit_bytes=20 << 20),
        cost_estimate=pl.CostEstimate(flops=8 << 30, bytes_accessed=6 << 20, transcendentals=4096),
    )(gain, both, act, pre, second, first_t)


def add_kernel(own_ref, other_ref, out_ref):
    out_ref[...] = (own_ref[...].astype(F32) + other_ref[...].astype(F32)).astype(BF16)


def add_pair(own, other):
    spec = pl.BlockSpec((9, 128, 128), lambda i: (i, 0, 0))
    return pl.pallas_call(
        add_kernel,
        out_shape=jax.ShapeDtypeStruct((27, 128, 128), BF16),
        grid=(3,),
        in_specs=[spec, spec],
        out_specs=spec,
        compiler_params=pltpu.CompilerParams(vmem_limit_bytes=6 << 20),
        cost_estimate=pl.CostEstimate(flops=1 << 19, bytes_accessed=3 << 20, transcendentals=0),
    )(own, other)


FIRST = [(i, i ^ 1) for i in range(8)]
SECOND = [(i, i - 1 if i % 2 == 0 else i + 1) for i in range(1, 7)]


def across(pairs):
    return [(a * 2 + s, b * 2 + 1 - s) for a, b in pairs for s in range(2)]


def edges(both, send_one, send_two, layer, layer_one, layer_two):
    x_one = lax.ppermute(send_one, GX, FIRST)
    x_two = lax.ppermute(send_two, GX, SECOND)
    came = lax.ppermute(layer, SA, [(0, 1), (1, 0)])
    came_one = lax.ppermute(layer_one, PLANE, across(FIRST))
    came_two = lax.ppermute(layer_two, PLANE, across(SECOND))

    def wide(start):
        def rows(part):
            return lax.dynamic_slice_in_dim(part, start, 2, axis=2)

        inner = jnp.concatenate([rows(part) for part in (x_one, both, x_two)], axis=1)
        outer = jnp.concatenate([rows(part) for part in (came_one, came, came_two)], axis=1)
        return jnp.concatenate([inner, outer], axis=3)

    first_y, second_y = send_rows(lax.axis_index(GY), 14)
    y_one = lax.ppermute(wide(first_y), GY, FIRST)
    y_two = lax.ppermute(wide(second_y), GY, SECOND)
    return both, x_one, x_two, came, came_one, came_two, y_one, y_two


def exchange(values, axes):
    return lax.all_to_all(values, axes, split_axis=0, concat_axis=0, tiled=True)


def local(sweep_bricks, target_rank, target_slot, conv_first, conv_second, norm_gain, out_grad):
    gain = norm_gain.reshape(1, 128)
    core = lax.axis_index("c")
    where = jnp.stack([lax.axis_index(SA), core, lax.axis_index(GX), lax.axis_index(GY)])
    where = where.astype(jnp.int32)
    both, (first, second, first_t, second_t) = regroup(
        sweep_bricks.reshape(128, 64, 128),
        target_rank.reshape(1, 128),
        target_slot.reshape(1, 128),
        out_grad,
        where,
        (
            pair_weights(conv_first),
            pair_weights(conv_second),
            turned(conv_first),
            turned(conv_second),
        ),
    )
    pieces = edges(*both)
    act, pre, own, send = grads_call(where, gain, pieces, first, second_t)
    other = lax.ppermute(send, "c", [(0, 1), (1, 0)])
    shares = exchange(add_pair(own, other).reshape(16, 216, 128), PLANE)
    block_out, grid_grad, gain_part = outputs_call(gain, pieces[0], act, pre, second, first_t)

    def halves(row):
        high = row.astype(BF16)
        low = (row - high.astype(F32)).astype(BF16)
        return [high, low, jnp.zeros((6, 128), BF16)]

    def joined(total, row):
        return jnp.concatenate([total.astype(BF16)] + halves(row), axis=0)

    total = jnp.sum(shares.astype(F32), axis=0)
    sent = joined(total, jnp.sum(gain_part, axis=0, keepdims=True))
    parts = [sent] + [along("z", sent, shift) for shift in (1, 2, 3)]
    parts = [part.astype(F32) for part in parts]
    layers = (parts[0] + parts[2]) + (parts[1] + parts[3])
    sent = joined(layers[:216], layers[216:217] + layers[217:218])
    gathered = exchange(jnp.broadcast_to(sent[None], (16, 224, 128)), PLANE)
    swapped = lax.ppermute(gathered, "c", [(0, 1), (1, 0)])
    factor = 1.0 / math.sqrt(131072.0)

    def weights(low, high):
        picked = jnp.where(core == 0, low[:, :216], high[:, :216])
        return (picked.astype(F32) * factor).reshape(27, 128, 128)

    gains = jnp.sum(gathered[:, 216:218].astype(F32), axis=(0, 1))
    gains = gains + jnp.sum(swapped[:, 216:218].astype(F32), axis=(0, 1))
    return (
        block_out,
        grid_grad,
        weights(gathered, swapped),
        weights(swapped, gathered),
        gains * factor,
    )


def solution(mesh):
    inner = Mesh(mesh.devices.reshape(4, 2, 4, 2, 2), ("y", "xl", "z", "c", "xh"))
    in_specs = (
        P(GX, GY, SA, None, None),
        P(GX, GY, SA, None),
        P(GX, GY, SA),
        P(),
        P(),
        P(),
        P(GX, GY, SA, None),
    )
    out_specs = (P(GX, GY, SA, None), P(GX, GY, SA, None), P(), P(), P())
    return jax.shard_map(local, mesh=inner, in_specs=in_specs, out_specs=out_specs, check_vma=False)
```

```python
import functools
import math

import jax
import jax.numpy as jnp
from jax import lax
from jax.experimental import pallas as pl
from jax.experimental.pallas import tpu as pltpu
from jax.sharding import Mesh
from jax.sharding import PartitionSpec as P

epsilon = 1e-06
DEAD = 1.0e30
OUT = -1.0e30
LIMIT = 1.0e29
GX = ("y", "xl")
GY = ("z", "c")
SA = "xh"
PLANE = ("y", "xl", "xh")
F32 = jnp.float32
BF16 = jnp.bfloat16
VM = pl.BlockSpec(memory_space=pltpu.VMEM)
SM = pl.BlockSpec(memory_space=pltpu.SMEM)
AN = pl.BlockSpec(memory_space=pl.ANY)
HB = pl.BlockSpec(memory_space=pltpu.HBM)


def place_kernel(half, code_ref, rows_hbm, o0, o1, o2, o3, fetched, flat, place, lift, sems):
    step = pl.program_id(0)

    def copy(n):
        voxels = rows_hbm.at[:, pl.ds(half * 32 + n * 8, 8), :]
        return pltpu.make_async_copy(voxels, fetched.at[n], sems.at[n])

    @pl.when(step == 0)
    def _():
        for n in range(4):
            copy(n).start()
        slots = lax.broadcasted_iota(jnp.int32, (256, 128), 0)
        chosen = jnp.where(slots == code_ref[half : half + 1, :], 1.0, 0.0)
        place[...] = chosen.astype(BF16)
        named = jnp.max(chosen, axis=1, keepdims=True)
        lift[...] = jnp.broadcast_to(jnp.where(named > 0.0, 0.0, DEAD), (256, 128))

    for n in range(4):

        @pl.when(step == n)
        def _():
            copy(n).wait()
            flat[...] = fetched[n].astype(F32).reshape(1024, 128)

    for voxel in range(8):
        values = flat[pl.ds(voxel, 128, stride=8), :].astype(BF16)
        summed = jnp.dot(place[...], values, preferred_element_type=F32) + lift[...]
        summed = summed.astype(BF16).reshape(4, 4, 16, 128)
        for shift, out in enumerate((o0, o1, o2, o3)):
            out[:, voxel] = summed[shift]


def place_bricks(code, rows, half):
    return pl.pallas_call(
        functools.partial(place_kernel, half),
        out_shape=(jax.ShapeDtypeStruct((4, 32, 16, 128), BF16),) * 4,
        grid=(4,),
        in_specs=[
            pl.BlockSpec((2, 128), lambda i: (0, 0)),
            HB,
        ],
        out_specs=(pl.BlockSpec((4, 8, 16, 128), lambda i: (0, i, 0, 0)),) * 4,
        scratch_shapes=[
            pltpu.VMEM((4, 128, 8, 128), BF16),
            pltpu.VMEM((1024, 128), F32),
            pltpu.VMEM((256, 128), BF16),
            pltpu.VMEM((256, 128), F32),
            pltpu.SemaphoreType.DMA((4,)),
        ],
        compiler_params=pltpu.CompilerParams(vmem_limit_bytes=10 << 20),
        cost_estimate=pl.CostEstimate(flops=1 << 28, bytes_accessed=3 << 20, transcendentals=0),
    )(code, rows)


def added(parts):
    total = jnp.zeros(parts[0].shape, F32)
    filled = jnp.zeros(parts[0].shape[1:], jnp.bool_)
    for part in parts:
        held = part[0] < LIMIT
        filled = filled | held
        total = total + jnp.where(held, part, 0.0)
    return jnp.where(filled, total, DEAD)


def merge_kernel(p0, p1, p2, p3, o0, o1, o2, o3, fetched, sums, sems):
    sources = (p0, p1, p2, p3)
    copies = [
        [
            pltpu.make_async_copy(part.at[shift], fetched.at[shift, n], sems.at[shift, n])
            for n, part in enumerate(sources)
        ]
        for shift in range(4)
    ]
    for shift in (1, 2, 3, 0):
        for copy in copies[shift]:
            copy.start()
    stores = []
    for shift, out in ((1, o1), (2, o2), (3, o3), (0, o0)):
        for copy in copies[shift]:
            copy.wait()

        def block(step, carry):
            at = pl.ds(pl.multiple_of(step * 8, 8), 8)
            parts = [fetched[shift, n, at].astype(F32) for n in range(4)]
            sums[shift, at] = added(parts).astype(BF16)
            return carry

        lax.fori_loop(0, 4, block, 0)
        stores.append(pltpu.make_async_copy(sums.at[shift], out, sems.at[4, shift]))
        stores[-1].start()
    for store in stores:
        store.wait()


def merge_bricks(parts):
    return pl.pallas_call(
        merge_kernel,
        out_shape=(jax.ShapeDtypeStruct((32, 16, 128), BF16),) * 4,
        in_specs=[AN] * 4,
        out_specs=(AN,) * 4,
        scratch_shapes=[
            pltpu.VMEM((4, 4, 32, 16, 128), BF16),
            pltpu.VMEM((4, 32, 16, 128), BF16),
            pltpu.SemaphoreType.DMA((5, 4)),
        ],
        compiler_params=pltpu.CompilerParams(vmem_limit_bytes=60 << 20),
        cost_estimate=pl.CostEstimate(flops=4 << 20, bytes_accessed=3 << 20, transcendentals=0),
    )(*parts)


def send_rows(place, top):
    odd = place % 2
    return top - top * odd, top * odd


def sum_bricks_kernel(
    where_ref,
    a0, a1, a2, a3, b0, b1, b2, b3,
    cot_ref,
    both_ref,
    one_ref,
    two_ref,
    layer_ref,
    layer_one_ref,
    layer_two_ref,
    sums,
    cells,
):
    both_ref[1] = cot_ref[...]
    for half, parts in enumerate(((a0, a1, a2, a3), (b0, b1, b2, b3))):

        def block(step, carry):
            shift_x = half * 2 + step // 2
            shift_y = (step % 2) * 2
            at = pl.ds(pl.multiple_of(step * 8, 8), 8)
            sums[...] = added([part[at].astype(F32) for part in parts]).reshape(128, 128)
            for voxel in range(2):
                for bx in range(2):
                    for by in range(4):
                        slot = voxel * 64 + (bx * 4 + by) * 2
                        spot = (voxel * 2 + bx) * 4 + by
                        cells[spot, 0:4, :] = sums[pl.ds(slot, 4, stride=16), :]
                        cells[spot, 4:8, :] = sums[pl.ds(slot + 1, 4, stride=16), :]
                        both_ref[0, bx * 4 + shift_x, by * 4 + shift_y + voxel] = cells[
                            spot
                        ].astype(BF16)
            return carry

        lax.fori_loop(0, 4, block, 0)
    first_x, second_x = send_rows(where_ref[2], 6)
    one_ref[...] = both_ref[:, pl.ds(first_x, 2)]
    two_ref[...] = both_ref[:, pl.ds(second_x, 2)]
    for side, rows in ((0, slice(6, 8)), (1, slice(0, 2))):

        @pl.when(where_ref[0] == side)
        def _():
            for n in range(2):
                layer_ref[n] = both_ref[n].astype(F32)[:, :, rows, :].astype(BF16)

    layer_one_ref[...] = layer_ref[:, pl.ds(first_x, 2)]
    layer_two_ref[...] = layer_ref[:, pl.ds(second_x, 2)]


def sum_bricks(where, parts, out_grad):
    return pl.pallas_call(
        sum_bricks_kernel,
        out_shape=(
            jax.ShapeDtypeStruct((2, 8, 16, 8, 128), BF16),
            jax.ShapeDtypeStruct((2, 2, 16, 8, 128), BF16),
            jax.ShapeDtypeStruct((2, 2, 16, 8, 128), BF16),
            jax.ShapeDtypeStruct((2, 8, 16, 2, 128), BF16),
            jax.ShapeDtypeStruct((2, 2, 16, 2, 128), BF16),
            jax.ShapeDtypeStruct((2, 2, 16, 2, 128), BF16),
        ),
        in_specs=[SM] + [VM] * 9,
        out_specs=(VM,) * 6,
        scratch_shapes=[pltpu.VMEM((128, 128), F32), pltpu.VMEM((16, 8, 128), F32)],
        compiler_params=pltpu.CompilerParams(vmem_limit_bytes=60 << 20),
        cost_estimate=pl.CostEstimate(flops=8 << 20, bytes_accessed=2 << 20, transcendentals=0),
    )(where, *parts, out_grad)


def along_x(value, shift):
    def place(chip):
        return chip % 2 * 2 + chip // 2

    pairs = [(place(chip), place((chip + shift) % 4)) for chip in range(4)]
    return lax.ppermute(value, ("xl", "xh"), pairs)


def along(axis, value, shift):
    return lax.ppermute(value, axis, [(i, (i + shift) % 4) for i in range(4)])


def regroup(rows, target_rank, target_slot, out_grad, where, weights):
    to_x = target_rank % 2 * 2 + target_rank // 2 % 2
    shift_x = (to_x - (lax.axis_index("xh") * 2 + lax.axis_index("xl"))) & 3
    shift_y = (target_rank // 4 - lax.axis_index("y")) & 3
    major = jnp.concatenate([shift_x, shift_y], axis=0)
    minor = jnp.concatenate([shift_y, shift_x], axis=0)
    codes = (major * 4 + minor) * 16 + target_slot
    placed_a = place_bricks(codes, rows, 0)
    placed_b = place_bricks(codes, rows, 1)
    came_a = [placed_a[0]] + [along_x(placed_a[n], n) for n in (1, 2, 3)]
    came_b = [placed_b[0]] + [along("y", placed_b[n], n) for n in (1, 2, 3)]
    came_a, weights = lax.optimization_barrier((came_a, weights))
    merged_a = merge_bricks(came_a)
    merged_b = merge_bricks(came_b)
    came_a = [merged_a[0]] + [along("y", merged_a[n], n) for n in (1, 2, 3)]
    came_b = [merged_b[0]] + [along_x(merged_b[n], n) for n in (1, 2, 3)]
    return sum_bricks(where, came_a + came_b, out_grad), weights


def window_rows(ref, x, y, slabs, rows):
    part = ref[pl.ds(x, slabs), pl.ds(y, rows), :, :]
    return part.reshape(slabs * rows * 16, part.shape[3])


def gather_windows(ref, x, rows):
    parts = [window_rows(ref, x + i, j, 1, rows) for i in range(4) for j in range(3)]
    return jnp.concatenate(parts, axis=1)


def convolve_pair(ref, x, rows, weights):
    both = jnp.dot(gather_windows(ref, x, rows), weights[...], preferred_element_type=F32)
    return jnp.concatenate([both[:, 0:128], both[:, 128:256]], axis=0)


def pair_weights(weights):
    blocks = weights.reshape(3, 3, 384, 128)
    left = jnp.pad(blocks, ((0, 1), (0, 0), (0, 0), (0, 0)))
    right = jnp.pad(blocks, ((1, 0), (0, 0), (0, 0), (0, 0)))
    return jnp.concatenate([left, right], axis=3).reshape(4608, 256)


def turned(weights):
    return pair_weights(weights[::-1].transpose(0, 2, 1))


def neighbours(value):
    count = value.shape[0]
    order = (pltpu.roll(value, 1, 0), value, pltpu.roll(value, count - 1, 0))
    return jnp.concatenate([part.astype(BF16) for part in order], axis=1)


PIECES = (
    (2, 8, 16, 8, 128),
    (2, 2, 16, 8, 128),
    (2, 2, 16, 8, 128),
    (2, 8, 16, 2, 128),
    (2, 2, 16, 2, 128),
    (2, 2, 16, 2, 128),
    (2, 12, 2, 10, 128),
    (2, 12, 2, 10, 128),
)


def fill(volume, which, pieces, where_ref, outside):
    centre, x_one, x_two, layer, layer_one, layer_two, y_one, y_two = pieces
    first_x, second_x = send_rows(where_ref[2], 10)
    first_y, second_y = send_rows(where_ref[3], 18)
    at_one = pl.ds(first_x, 2)
    at_two = pl.ds(second_x, 2)
    volume[...] = jnp.full(volume.shape, outside, F32)
    volume[2:10, 2:18, 2:10, :] = centre[which].astype(F32)
    volume[at_one, 2:18, 2:10, :] = x_one[which].astype(F32)
    volume[at_two, 2:18, 2:10, :] = x_two[which].astype(F32)
    sides = ((y_one, pl.ds(first_y, 2)), (y_two, pl.ds(second_y, 2)))
    spans = ((at_one, slice(0, 2)), (slice(2, 10), slice(2, 10)), (at_two, slice(10, 12)))
    for came, at_y in sides:
        values = came[which].astype(F32)
        for at_x, rows in spans:
            volume[at_x, at_y, 2:10, :] = values[rows, :, 0:8]
    for side, at_z in ((0, slice(10, 12)), (1, slice(0, 2))):

        @pl.when(where_ref[0] == side)
        def _():
            volume[2:10, 2:18, at_z, :] = layer[which].astype(F32)
            volume[at_one, 2:18, at_z, :] = layer_one[which].astype(F32)
            volume[at_two, 2:18, at_z, :] = layer_two[which].astype(F32)
            for came, at_y in sides:
                values = came[which].astype(F32)
                for at_x, rows in spans:
                    volume[at_x, at_y, at_z, :] = values[rows, :, 8:10]

    @pl.when(where_ref[2] == 0)
    def _():
        volume[0:2] = jnp.full((2, 20, 16, 128), outside, F32)

    @pl.when(where_ref[2] == 7)
    def _():
        volume[10:12] = jnp.full((2, 20, 16, 128), outside, F32)

    @pl.when(where_ref[3] == 0)
    def _():
        volume[:, 0:2] = jnp.full((12, 2, 16, 128), outside, F32)

    @pl.when(where_ref[3] == 7)
    def _():
        volume[:, 18:20] = jnp.full((12, 2, 16, 128), outside, F32)


def grads_kernel(
    where_ref,
    gain,
    p0, p1, p2, p3, p4, p5, p6, p7,
    first_hbm,
    second_hbm,
    act_hbm,
    pre_hbm,
    own_hbm,
    send_hbm,
    cells,
    cots,
    normed3,
    masked3,
    act_t,
    normed_t,
    row_cells,
    pair_cells,
    masked_even,
    masked_odd,
    pre_even,
    pre_odd,
    found,
    s0, s1, s2, s3, s4, s5, s6, s7,
    first,
    second_t,
    act_ref,
    pre_ref,
    sems,
):
    core = where_ref[1]
    pieces = (s0, s1, s2, s3, s4, s5, s6, s7)
    copies = [
        pltpu.make_async_copy(source, target, sems.at[n])
        for n, (source, target) in enumerate(
            zip((p0, p1, p2, p3, p4, p5, p6, p7, first_hbm, second_hbm), (*pieces, first, second_t))
        )
    ]
    for copy in copies:
        copy.start()
    for copy in copies[:8]:
        copy.wait()
    fill(cells, 0, pieces, where_ref, OUT)
    fill(cots, 1, pieces, where_ref, 0.0)
    act_t[:, 0:128] = jnp.zeros((128, 128), BF16)
    act_t[:, 1408:1536] = jnp.zeros((128, 128), BF16)

    def turned_columns(target, x, values):
        inner = jnp.where((x >= 2) & (x < 10), values, 0.0).astype(BF16)
        target[:, pl.ds(pl.multiple_of(x * 128, 128), 128)] = inner.T

    def prepare(x, carry):
        values = cells[x].reshape(320, 128)
        live = jnp.abs(values) < LIMIT
        held = jnp.where(live, values, 0.0)
        inverse = lax.rsqrt(jnp.mean(held * held, axis=-1, keepdims=True) + epsilon)
        normed = held * inverse * gain[...]
        normed3[x] = neighbours(normed).reshape(20, 16, 384)
        row_cells[...] = normed.reshape(20, 16, 128)
        turned_columns(normed_t, x, row_cells[2:18, 2:10, :].reshape(128, 128))
        masked = jnp.where(live, cots[x].reshape(320, 128), 0.0)
        masked3[x] = neighbours(masked).reshape(20, 16, 384)
        cots[x] = masked.reshape(20, 16, 128)
        parts = [cots[x, :, 1 + k : 9 + k, :].reshape(160, 128) for k in range(3)]
        masked_even[x] = jnp.concatenate([part.astype(BF16) for part in parts], axis=1)
        masked_odd[x] = jnp.concatenate([part[8:152].astype(BF16) for part in parts], axis=1)
        return carry

    lax.fori_loop(0, 12, prepare, 0)
    for copy in copies[8:]:
        copy.wait()

    def convolve(step, carry):
        x = step * 2
        values = cells[pl.ds(x + 1, 2), 1:19, :, :].reshape(576, 128)
        before = convolve_pair(normed3, x, 18, first)
        before = jnp.where(jnp.abs(values) < LIMIT, before, 0.0)
        sigmoid = jax.nn.sigmoid(before)
        active = before * sigmoid
        act_ref[pl.ds(x, 2)] = active.astype(BF16).reshape(2, 18, 16, 128)
        pair_cells[...] = active.reshape(2, 18, 16, 128)
        for n in range(2):
            inner = pair_cells[n, 1:17, 2:10, :].reshape(128, 128)
            turned_columns(act_t, x + 1 + n, inner)
        active_grad = convolve_pair(masked3, x, 18, second_t)
        pre = active_grad * sigmoid * (1.0 + before * (1.0 - sigmoid))
        pre = jnp.where(values > -LIMIT, pre, 0.0)
        pre_ref[pl.ds(x, 2)] = pre.astype(BF16).reshape(2, 18, 16, 128)
        pair_cells[...] = pre.reshape(2, 18, 16, 128)
        for n in range(2):
            parts = [pair_cells[n, :, 1 + k : 9 + k, :].reshape(144, 128) for k in range(3)]
            pre_even[x + n] = jnp.concatenate([part.astype(BF16) for part in parts], axis=1)
            pre_odd[x + n] = jnp.concatenate([part[8:136].astype(BF16) for part in parts], axis=1)
        return carry

    lax.fori_loop(0, 5, convolve, 0)
    results = [
        pltpu.make_async_copy(source, target, sems.at[n])
        for n, (source, target) in enumerate(((act_ref, act_hbm), (pre_ref, pre_hbm)))
    ]
    for copy in results:
        copy.start()

    for which, left, sides in (
        (1, act_t, ((masked_odd, 16), (masked_even, 16), (masked_odd, 0))),
        (0, normed_t, ((pre_even, 16), (pre_odd, 0), (pre_even, 0))),
    ):
        own = jnp.concatenate([left[:, 128 * i : 128 * (i + 10)] for i in range(3)], axis=0)
        for j, (cots_at, row) in enumerate(sides):
            start = which
            cot = cots_at[start : start + 10, row : row + 128, :].reshape(1280, 384)
            total = jnp.dot(own, cot, preferred_element_type=F32).astype(BF16)
            for i in range(3):
                for k in range(3):
                    found[which, i * 9 + j * 3 + k] = total[
                        i * 128 : (i + 1) * 128, (2 - k) * 128 : (3 - k) * 128
                    ]

    results += [
        pltpu.make_async_copy(found.at[core], own_hbm, sems.at[2]),
        pltpu.make_async_copy(found.at[1 - core], send_hbm, sems.at[3]),
    ]
    for copy in results[2:]:
        copy.start()
    for copy in results:
        copy.wait()


def grads_call(where, gain, pieces, first, second_t):
    return pl.pallas_call(
        grads_kernel,
        out_shape=(
            jax.ShapeDtypeStruct((10, 18, 16, 128), BF16),
            jax.ShapeDtypeStruct((10, 18, 16, 128), BF16),
            jax.ShapeDtypeStruct((27, 128, 128), BF16),
            jax.ShapeDtypeStruct((27, 128, 128), BF16),
        ),
        in_specs=[SM, VM] + [AN] * 8 + [HB] * 2,
        out_specs=(HB, HB, HB, HB),
        scratch_shapes=[
            pltpu.VMEM((12, 20, 16, 128), F32),
            pltpu.VMEM((12, 20, 16, 128), F32),
            pltpu.VMEM((12, 20, 16, 384), BF16),
            pltpu.VMEM((12, 20, 16, 384), BF16),
            pltpu.VMEM((128, 1536), BF16),
            pltpu.VMEM((128, 1536), BF16),
            pltpu.VMEM((20, 16, 128), F32),
            pltpu.VMEM((2, 18, 16, 128), F32),
            pltpu.VMEM((12, 160, 384), BF16),
            pltpu.VMEM((12, 144, 384), BF16),
            pltpu.VMEM((10, 144, 384), BF16),
            pltpu.VMEM((10, 128, 384), BF16),
            pltpu.VMEM((2, 27, 128, 128), BF16),
            *[pltpu.VMEM(shape, BF16) for shape in PIECES],
            pltpu.VMEM((4608, 256), BF16),
            pltpu.VMEM((4608, 256), BF16),
            pltpu.VMEM((10, 18, 16, 128), BF16),
            pltpu.VMEM((10, 18, 16, 128), BF16),
            pltpu.SemaphoreType.DMA((10,)),
        ],
        compiler_params=pltpu.CompilerParams(vmem_limit_bytes=60 << 20),
        cost_estimate=pl.CostEstimate(flops=10 << 30, bytes_accessed=8 << 20, transcendentals=1 << 20),
    )(where, gain, *pieces, first, second_t)


def outputs_kernel(
    gain,
    both_hbm,
    act_hbm,
    pre_hbm,
    second_hbm,
    first_hbm,
    block_ref,
    grad_ref,
    gain_ref,
    both,
    act,
    pre,
    second,
    first_t,
    act3,
    pre3,
    spread,
    sems,
):
    copies = [
        pltpu.make_async_copy(source, target, sems.at[n])
        for n, (source, target) in enumerate(
            (
                (act_hbm, act),
                (pre_hbm, pre),
                (both_hbm, both),
                (second_hbm, second),
                (first_hbm, first_t),
            )
        )
    ]
    for copy in copies:
        copy.start()
    for copy, source, target in ((copies[0], act, act3), (copies[1], pre, pre3)):
        copy.wait()

        def prepare(x, carry):
            values = source[x].reshape(288, 128).astype(F32)
            target[x] = neighbours(values).reshape(18, 16, 384)
            return carry

        lax.fori_loop(0, 10, prepare, 0)

    for copy in copies[2:]:
        copy.wait()
    gains = gain[...]

    def convolve(step, total):
        x = step * 2
        branch = convolve_pair(act3, x, 16, second)
        spread[...] = branch.reshape(2, 16, 16, 128)
        branch = spread[:, :, 2:10, :].reshape(256, 128)
        values = both[0, pl.ds(x, 2)].astype(F32).reshape(256, 128)
        live = values < LIMIT
        held = jnp.where(live, values, 0.0)
        block = jnp.where(live, branch, 0.0) + held
        block_ref[pl.ds(x, 2)] = block.astype(BF16).reshape(2, 16, 8, 128)
        normed_grad = convolve_pair(pre3, x, 16, first_t)
        spread[...] = normed_grad.reshape(2, 16, 16, 128)
        normed_grad = jnp.where(live, spread[:, :, 2:10, :].reshape(256, 128), 0.0)
        inverse = lax.rsqrt(jnp.mean(held * held, axis=-1, keepdims=True) + epsilon)
        total = total + jnp.sum((normed_grad * held * inverse).reshape(32, 8, 128), axis=0)
        upstream = normed_grad * gains
        centred = jnp.mean(held * upstream, axis=-1, keepdims=True)
        extra = inverse * upstream - held * (inverse * inverse * inverse * centred)
        cot = both[1, pl.ds(x, 2)].astype(F32).reshape(256, 128)
        grad = cot + jnp.where(live, extra, 0.0)
        grad_ref[pl.ds(x, 2)] = grad.astype(BF16).reshape(2, 16, 8, 128)
        return total

    total = lax.fori_loop(0, 4, convolve, jnp.zeros((8, 128), F32))
    gain_ref[...] = total


def outputs_call(gain, both, act, pre, second, first_t):
    return pl.pallas_call(
        outputs_kernel,
        out_shape=(
            jax.ShapeDtypeStruct((8, 16, 8, 128), BF16),
            jax.ShapeDtypeStruct((8, 16, 8, 128), BF16),
            jax.ShapeDtypeStruct((8, 128), F32),
        ),
        in_specs=[VM, AN, HB, HB, HB, HB],
        out_specs=(VM,) * 3,
        scratch_shapes=[
            pltpu.VMEM((2, 8, 16, 8, 128), BF16),
            pltpu.VMEM((10, 18, 16, 128), BF16),
            pltpu.VMEM((10, 18, 16, 128), BF16),
            pltpu.VMEM((4608, 256), BF16),
            pltpu.VMEM((4608, 256), BF16),
            pltpu.VMEM((10, 18, 16, 384), BF16),
            pltpu.VMEM((10, 18, 16, 384), BF16),
            pltpu.VMEM((2, 16, 16, 128), F32),
            pltpu.SemaphoreType.DMA((5,)),
        ],
        compiler_params=pltpu.CompilerParams(vmem_limit_bytes=60 << 20),
        cost_estimate=pl.CostEstimate(flops=8 << 30, bytes_accessed=6 << 20, transcendentals=4096),
    )(gain, both, act, pre, second, first_t)


def add_kernel(own_ref, other_ref, out_ref):
    out_ref[...] = (own_ref[...].astype(F32) + other_ref[...].astype(F32)).astype(BF16)


def add_pair(own, other):
    return pl.pallas_call(
        add_kernel,
        out_shape=jax.ShapeDtypeStruct((27, 128, 128), BF16),
        in_specs=[VM, VM],
        out_specs=VM,
        compiler_params=pltpu.CompilerParams(vmem_limit_bytes=6 << 20),
        cost_estimate=pl.CostEstimate(flops=1 << 19, bytes_accessed=3 << 20, transcendentals=0),
    )(own, other)


FIRST = [(i, i ^ 1) for i in range(8)]
SECOND = [(i, i - 1 if i % 2 == 0 else i + 1) for i in range(1, 7)]


def across(pairs):
    return [(a * 2 + s, b * 2 + 1 - s) for a, b in pairs for s in range(2)]


def edges(both, send_one, send_two, layer, layer_one, layer_two):
    x_one = lax.ppermute(send_one, GX, FIRST)
    x_two = lax.ppermute(send_two, GX, SECOND)
    came = lax.ppermute(layer, SA, [(0, 1), (1, 0)])
    came_one = lax.ppermute(layer_one, PLANE, across(FIRST))
    came_two = lax.ppermute(layer_two, PLANE, across(SECOND))

    def wide(start):
        def rows(part):
            return lax.dynamic_slice_in_dim(part, start, 2, axis=2)

        inner = jnp.concatenate([rows(part) for part in (x_one, both, x_two)], axis=1)
        outer = jnp.concatenate([rows(part) for part in (came_one, came, came_two)], axis=1)
        return jnp.concatenate([inner, outer], axis=3)

    first_y, second_y = send_rows(lax.axis_index(GY), 14)
    y_one = lax.ppermute(wide(first_y), GY, FIRST)
    y_two = lax.ppermute(wide(second_y), GY, SECOND)
    return both, x_one, x_two, came, came_one, came_two, y_one, y_two


def exchange(values, axes):
    return lax.all_to_all(values, axes, split_axis=0, concat_axis=0, tiled=True)


def local(sweep_bricks, target_rank, target_slot, conv_first, conv_second, norm_gain, out_grad):
    gain = norm_gain.reshape(1, 128)
    core = lax.axis_index("c")
    where = jnp.stack([lax.axis_index(SA), core, lax.axis_index(GX), lax.axis_index(GY)])
    where = where.astype(jnp.int32)
    both, (first, second, first_t, second_t) = regroup(
        sweep_bricks.reshape(128, 64, 128),
        target_rank.reshape(1, 128),
        target_slot.reshape(1, 128),
        out_grad,
        where,
        (
            pair_weights(conv_first),
            pair_weights(conv_second),
            turned(conv_first),
            turned(conv_second),
        ),
    )
    pieces = edges(*both)
    act, pre, own, send = grads_call(where, gain, pieces, first, second_t)
    other = lax.ppermute(send, "c", [(0, 1), (1, 0)])
    shares = exchange(add_pair(own, other).reshape(16, 216, 128), PLANE)
    block_out, grid_grad, gain_part = outputs_call(gain, pieces[0], act, pre, second, first_t)

    def halves(row):
        high = row.astype(BF16)
        low = (row - high.astype(F32)).astype(BF16)
        return [high, low, jnp.zeros((6, 128), BF16)]

    def joined(total, row):
        return jnp.concatenate([total.astype(BF16)] + halves(row), axis=0)

    total = jnp.sum(shares.astype(F32), axis=0)
    sent = joined(total, jnp.sum(gain_part, axis=0, keepdims=True))
    parts = [sent] + [along("z", sent, shift) for shift in (1, 2, 3)]
    parts = [part.astype(F32) for part in parts]
    layers = (parts[0] + parts[2]) + (parts[1] + parts[3])
    sent = joined(layers[:216], layers[216:217] + layers[217:218])
    gathered = exchange(jnp.broadcast_to(sent[None], (16, 224, 128)), PLANE)
    swapped = lax.ppermute(gathered, "c", [(0, 1), (1, 0)])
    factor = 1.0 / math.sqrt(131072.0)

    def weights(low, high):
        picked = jnp.where(core == 0, low[:, :216], high[:, :216])
        return (picked.astype(F32) * factor).reshape(27, 128, 128)

    gains = jnp.sum(gathered[:, 216:218].astype(F32), axis=(0, 1))
    gains = gains + jnp.sum(swapped[:, 216:218].astype(F32), axis=(0, 1))
    return (
        block_out,
        grid_grad,
        weights(gathered, swapped),
        weights(swapped, gathered),
        gains * factor,
    )


def solution(mesh):
    inner = Mesh(mesh.devices.reshape(4, 2, 4, 2, 2), ("y", "xl", "z", "c", "xh"))
    in_specs = (
        P(GX, GY, SA, None, None),
        P(GX, GY, SA, None),
        P(GX, GY, SA),
        P(),
        P(),
        P(),
        P(GX, GY, SA, None),
    )
    out_specs = (P(GX, GY, SA, None), P(GX, GY, SA, None), P(), P(), P())
    return jax.shard_map(local, mesh=inner, in_specs=in_specs, out_specs=out_specs, check_vma=False)
```

```python
import functools
import math

import jax
import jax.numpy as jnp
from jax import lax
from jax.experimental import pallas as pl
from jax.experimental.pallas import tpu as pltpu
from jax.sharding import Mesh
from jax.sharding import PartitionSpec as P

epsilon = 1e-06
DEAD = 1.0e30
OUT = -1.0e30
LIMIT = 1.0e29
GX = ("y", "xl")
GY = ("z", "c")
SA = "xh"
PLANE = ("y", "xl", "xh")
F32 = jnp.float32
BF16 = jnp.bfloat16
VM = pl.BlockSpec(memory_space=pltpu.VMEM)
SM = pl.BlockSpec(memory_space=pltpu.SMEM)
AN = pl.BlockSpec(memory_space=pl.ANY)
HB = pl.BlockSpec(memory_space=pltpu.HBM)


def place_kernel(half, code_ref, rows_hbm, o0, o1, o2, o3, fetched, flat, place, lift, sems):
    step = pl.program_id(0)

    def copy(n):
        voxels = rows_hbm.at[:, pl.ds(half * 32 + n * 8, 8), :]
        return pltpu.make_async_copy(voxels, fetched.at[n], sems.at[n])

    @pl.when(step == 0)
    def _():
        for n in range(4):
            copy(n).start()
        slots = lax.broadcasted_iota(jnp.int32, (256, 128), 0)
        chosen = jnp.where(slots == code_ref[half : half + 1, :], 1.0, 0.0)
        place[...] = chosen.astype(BF16)
        named = jnp.max(chosen, axis=1, keepdims=True)
        lift[...] = jnp.broadcast_to(jnp.where(named > 0.0, 0.0, DEAD), (256, 128))

    for n in range(4):

        @pl.when(step == n)
        def _():
            copy(n).wait()
            flat[...] = fetched[n].astype(F32).reshape(1024, 128)

    for voxel in range(8):
        values = flat[pl.ds(voxel, 128, stride=8), :].astype(BF16)
        summed = jnp.dot(place[...], values, preferred_element_type=F32) + lift[...]
        summed = summed.astype(BF16).reshape(4, 4, 16, 128)
        for shift, out in enumerate((o0, o1, o2, o3)):
            out[:, voxel] = summed[shift]


def place_bricks(code, rows, half):
    return pl.pallas_call(
        functools.partial(place_kernel, half),
        out_shape=(jax.ShapeDtypeStruct((4, 32, 16, 128), BF16),) * 4,
        grid=(4,),
        in_specs=[
            pl.BlockSpec((2, 128), lambda i: (0, 0)),
            HB,
        ],
        out_specs=(pl.BlockSpec((4, 8, 16, 128), lambda i: (0, i, 0, 0)),) * 4,
        scratch_shapes=[
            pltpu.VMEM((4, 128, 8, 128), BF16),
            pltpu.VMEM((1024, 128), F32),
            pltpu.VMEM((256, 128), BF16),
            pltpu.VMEM((256, 128), F32),
            pltpu.SemaphoreType.DMA((4,)),
        ],
        compiler_params=pltpu.CompilerParams(vmem_limit_bytes=10 << 20),
        cost_estimate=pl.CostEstimate(flops=1 << 28, bytes_accessed=3 << 20, transcendentals=0),
    )(code, rows)


def added(parts):
    total = jnp.zeros(parts[0].shape, F32)
    filled = jnp.zeros(parts[0].shape[1:], jnp.bool_)
    for part in parts:
        held = part[0] < LIMIT
        filled = filled | held
        total = total + jnp.where(held, part, 0.0)
    return jnp.where(filled, total, DEAD)


def merge_kernel(p0, p1, p2, p3, o0, o1, o2, o3, fetched, sums, sems):
    sources = (p0, p1, p2, p3)
    copies = [
        [
            pltpu.make_async_copy(part.at[shift], fetched.at[shift, n], sems.at[shift, n])
            for n, part in enumerate(sources)
        ]
        for shift in range(4)
    ]
    for shift in (1, 2, 3, 0):
        for copy in copies[shift]:
            copy.start()
    stores = []
    for shift, out in ((1, o1), (2, o2), (3, o3), (0, o0)):
        for copy in copies[shift]:
            copy.wait()

        def block(step, carry):
            at = pl.ds(pl.multiple_of(step * 8, 8), 8)
            parts = [fetched[shift, n, at].astype(F32) for n in range(4)]
            sums[shift, at] = added(parts).astype(BF16)
            return carry

        lax.fori_loop(0, 4, block, 0)
        stores.append(pltpu.make_async_copy(sums.at[shift], out, sems.at[4, shift]))
        stores[-1].start()
    for store in stores:
        store.wait()


def merge_bricks(parts):
    return pl.pallas_call(
        merge_kernel,
        out_shape=(jax.ShapeDtypeStruct((32, 16, 128), BF16),) * 4,
        in_specs=[AN] * 4,
        out_specs=(AN,) * 4,
        scratch_shapes=[
            pltpu.VMEM((4, 4, 32, 16, 128), BF16),
            pltpu.VMEM((4, 32, 16, 128), BF16),
            pltpu.SemaphoreType.DMA((5, 4)),
        ],
        compiler_params=pltpu.CompilerParams(vmem_limit_bytes=60 << 20),
        cost_estimate=pl.CostEstimate(flops=4 << 20, bytes_accessed=3 << 20, transcendentals=0),
    )(*parts)


def send_rows(place, top):
    odd = place % 2
    return top - top * odd, top * odd


def sum_bricks_kernel(
    where_ref,
    a0, a1, a2, a3, b0, b1, b2, b3,
    cot_ref,
    both_ref,
    one_ref,
    two_ref,
    layer_ref,
    layer_one_ref,
    layer_two_ref,
    sums,
    cells,
):
    both_ref[1] = cot_ref[...]
    for half, parts in enumerate(((a0, a1, a2, a3), (b0, b1, b2, b3))):

        def block(step, carry):
            shift_x = half * 2 + step // 2
            shift_y = (step % 2) * 2
            at = pl.ds(pl.multiple_of(step * 8, 8), 8)
            sums[...] = added([part[at].astype(F32) for part in parts]).reshape(128, 128)
            for voxel in range(2):
                for bx in range(2):
                    for by in range(4):
                        slot = voxel * 64 + (bx * 4 + by) * 2
                        spot = (voxel * 2 + bx) * 4 + by
                        cells[spot, 0:4, :] = sums[pl.ds(slot, 4, stride=16), :]
                        cells[spot, 4:8, :] = sums[pl.ds(slot + 1, 4, stride=16), :]
                        both_ref[0, bx * 4 + shift_x, by * 4 + shift_y + voxel] = cells[
                            spot
                        ].astype(BF16)
            return carry

        lax.fori_loop(0, 4, block, 0)
    first_x, second_x = send_rows(where_ref[2], 6)
    one_ref[...] = both_ref[:, pl.ds(first_x, 2)]
    two_ref[...] = both_ref[:, pl.ds(second_x, 2)]
    for side, rows in ((0, slice(6, 8)), (1, slice(0, 2))):

        @pl.when(where_ref[0] == side)
        def _():
            for n in range(2):
                layer_ref[n] = both_ref[n].astype(F32)[:, :, rows, :].astype(BF16)

    layer_one_ref[...] = layer_ref[:, pl.ds(first_x, 2)]
    layer_two_ref[...] = layer_ref[:, pl.ds(second_x, 2)]


def sum_bricks(where, parts, out_grad):
    return pl.pallas_call(
        sum_bricks_kernel,
        out_shape=(
            jax.ShapeDtypeStruct((2, 8, 16, 8, 128), BF16),
            jax.ShapeDtypeStruct((2, 2, 16, 8, 128), BF16),
            jax.ShapeDtypeStruct((2, 2, 16, 8, 128), BF16),
            jax.ShapeDtypeStruct((2, 8, 16, 2, 128), BF16),
            jax.ShapeDtypeStruct((2, 2, 16, 2, 128), BF16),
            jax.ShapeDtypeStruct((2, 2, 16, 2, 128), BF16),
        ),
        in_specs=[SM] + [VM] * 9,
        out_specs=(VM,) * 6,
        scratch_shapes=[pltpu.VMEM((128, 128), F32), pltpu.VMEM((16, 8, 128), F32)],
        compiler_params=pltpu.CompilerParams(vmem_limit_bytes=60 << 20),
        cost_estimate=pl.CostEstimate(flops=8 << 20, bytes_accessed=2 << 20, transcendentals=0),
    )(where, *parts, out_grad)


def along_x(value, shift):
    def place(chip):
        return chip % 2 * 2 + chip // 2

    pairs = [(place(chip), place((chip + shift) % 4)) for chip in range(4)]
    return lax.ppermute(value, ("xl", "xh"), pairs)


def along(axis, value, shift):
    return lax.ppermute(value, axis, [(i, (i + shift) % 4) for i in range(4)])


def regroup(rows, target_rank, target_slot, out_grad, where, weights):
    to_x = target_rank % 2 * 2 + target_rank // 2 % 2
    shift_x = (to_x - (lax.axis_index("xh") * 2 + lax.axis_index("xl"))) & 3
    shift_y = (target_rank // 4 - lax.axis_index("y")) & 3
    major = jnp.concatenate([shift_x, shift_y], axis=0)
    minor = jnp.concatenate([shift_y, shift_x], axis=0)
    codes = (major * 4 + minor) * 16 + target_slot
    placed_a = place_bricks(codes, rows, 0)
    placed_b = place_bricks(codes, rows, 1)
    came_a = [placed_a[0]] + [along_x(placed_a[n], n) for n in (1, 2, 3)]
    came_b = [placed_b[0]] + [along("y", placed_b[n], n) for n in (1, 2, 3)]
    came_a, weights, where = lax.optimization_barrier((came_a, weights, where))
    merged_a = merge_bricks(came_a)
    merged_b = merge_bricks(came_b)
    came_a = [merged_a[0]] + [along("y", merged_a[n], n) for n in (1, 2, 3)]
    came_b = [merged_b[0]] + [along_x(merged_b[n], n) for n in (1, 2, 3)]
    return sum_bricks(where, came_a + came_b, out_grad), weights, where


def window_rows(ref, x, y, slabs, rows):
    part = ref[pl.ds(x, slabs), pl.ds(y, rows), :, :]
    return part.reshape(slabs * rows * 16, part.shape[3])


def gather_windows(ref, x, rows):
    parts = [window_rows(ref, x + i, j, 1, rows) for i in range(4) for j in range(3)]
    return jnp.concatenate(parts, axis=1)


def convolve_pair(ref, x, rows, weights):
    both = jnp.dot(gather_windows(ref, x, rows), weights[...], preferred_element_type=F32)
    return jnp.concatenate([both[:, 0:128], both[:, 128:256]], axis=0)


def pair_kernel(weights_ref, plain_ref, turned_ref):
    a = pl.program_id(0)
    for j in range(3):
        for k in range(3):
            rows = slice(k * 128, (k + 1) * 128)
            for side in range(2):
                x = a - side
                kept = (x >= 0) & (x < 3)
                at = jnp.clip(x, 0, 2) * 9 + j * 3 + k
                columns = slice(side * 128, (side + 1) * 128)
                zero = jnp.zeros((128, 128), BF16)
                plain_ref[0, j, rows, columns] = jnp.where(kept, weights_ref[at], zero)
                turned_ref[0, j, rows, columns] = jnp.where(kept, weights_ref[26 - at].T, zero)


def pair_weights(weights):
    out = jax.ShapeDtypeStruct((4, 3, 384, 256), BF16)
    spec = pl.BlockSpec((1, 3, 384, 256), lambda a: (a, 0, 0, 0))
    plain, turned = pl.pallas_call(
        pair_kernel,
        out_shape=(out, out),
        grid=(4,),
        in_specs=[pl.BlockSpec((27, 128, 128), lambda a: (0, 0, 0))],
        out_specs=(spec, spec),
        compiler_params=pltpu.CompilerParams(vmem_limit_bytes=60 << 20),
        cost_estimate=pl.CostEstimate(flops=1 << 20, bytes_accessed=6 << 20, transcendentals=0),
    )(weights)
    return plain.reshape(4608, 256), turned.reshape(4608, 256)


def neighbours(value):
    count = value.shape[0]
    order = (pltpu.roll(value, 1, 0), value, pltpu.roll(value, count - 1, 0))
    return jnp.concatenate([part.astype(BF16) for part in order], axis=1)


PIECES = (
    (2, 8, 16, 8, 128),
    (2, 2, 16, 8, 128),
    (2, 2, 16, 8, 128),
    (2, 8, 16, 2, 128),
    (2, 2, 16, 2, 128),
    (2, 2, 16, 2, 128),
    (2, 12, 2, 10, 128),
    (2, 12, 2, 10, 128),
)


def fill(volume, which, pieces, where_ref, outside):
    centre, x_one, x_two, layer, layer_one, layer_two, y_one, y_two = pieces
    first_x, second_x = send_rows(where_ref[2], 10)
    first_y, second_y = send_rows(where_ref[3], 18)
    at_one = pl.ds(first_x, 2)
    at_two = pl.ds(second_x, 2)
    volume[...] = jnp.full(volume.shape, outside, F32)
    volume[2:10, 2:18, 2:10, :] = centre[which].astype(F32)
    volume[at_one, 2:18, 2:10, :] = x_one[which].astype(F32)
    volume[at_two, 2:18, 2:10, :] = x_two[which].astype(F32)
    sides = ((y_one, pl.ds(first_y, 2)), (y_two, pl.ds(second_y, 2)))
    spans = ((at_one, slice(0, 2)), (slice(2, 10), slice(2, 10)), (at_two, slice(10, 12)))
    for came, at_y in sides:
        values = came[which].astype(F32)
        for at_x, rows in spans:
            volume[at_x, at_y, 2:10, :] = values[rows, :, 0:8]
    for side, at_z in ((0, slice(10, 12)), (1, slice(0, 2))):

        @pl.when(where_ref[0] == side)
        def _():
            volume[2:10, 2:18, at_z, :] = layer[which].astype(F32)
            volume[at_one, 2:18, at_z, :] = layer_one[which].astype(F32)
            volume[at_two, 2:18, at_z, :] = layer_two[which].astype(F32)
            for came, at_y in sides:
                values = came[which].astype(F32)
                for at_x, rows in spans:
                    volume[at_x, at_y, at_z, :] = values[rows, :, 8:10]

    @pl.when(where_ref[2] == 0)
    def _():
        volume[0:2] = jnp.full((2, 20, 16, 128), outside, F32)

    @pl.when(where_ref[2] == 7)
    def _():
        volume[10:12] = jnp.full((2, 20, 16, 128), outside, F32)

    @pl.when(where_ref[3] == 0)
    def _():
        volume[:, 0:2] = jnp.full((12, 2, 16, 128), outside, F32)

    @pl.when(where_ref[3] == 7)
    def _():
        volume[:, 18:20] = jnp.full((12, 2, 16, 128), outside, F32)


def grads_kernel(
    where_ref,
    gain,
    p0, p1, p2, p3, p4, p5, p6, p7,
    first_hbm,
    second_hbm,
    act_hbm,
    pre_hbm,
    own_hbm,
    send_hbm,
    cells,
    cots,
    normed3,
    masked3,
    act_t,
    normed_t,
    row_cells,
    pair_cells,
    masked_even,
    masked_odd,
    pre_even,
    pre_odd,
    found,
    s0, s1, s2, s3, s4, s5, s6, s7,
    first,
    second_t,
    act_ref,
    pre_ref,
    sems,
):
    core = where_ref[1]
    pieces = (s0, s1, s2, s3, s4, s5, s6, s7)
    copies = [
        pltpu.make_async_copy(source, target, sems.at[n])
        for n, (source, target) in enumerate(
            zip((p0, p1, p2, p3, p4, p5, p6, p7, first_hbm, second_hbm), (*pieces, first, second_t))
        )
    ]
    for copy in copies:
        copy.start()
    for copy in copies[:8]:
        copy.wait()
    fill(cells, 0, pieces, where_ref, OUT)
    fill(cots, 1, pieces, where_ref, 0.0)
    act_t[:, 0:128] = jnp.zeros((128, 128), BF16)
    act_t[:, 1408:1536] = jnp.zeros((128, 128), BF16)

    def turned_columns(target, x, values):
        inner = jnp.where((x >= 2) & (x < 10), values, 0.0).astype(BF16)
        target[:, pl.ds(pl.multiple_of(x * 128, 128), 128)] = inner.T

    def prepare(x, carry):
        values = cells[x].reshape(320, 128)
        live = jnp.abs(values) < LIMIT
        held = jnp.where(live, values, 0.0)
        inverse = lax.rsqrt(jnp.mean(held * held, axis=-1, keepdims=True) + epsilon)
        normed = held * inverse * gain[...]
        normed3[x] = neighbours(normed).reshape(20, 16, 384)
        row_cells[...] = normed.reshape(20, 16, 128)
        turned_columns(normed_t, x, row_cells[2:18, 2:10, :].reshape(128, 128))
        masked = jnp.where(live, cots[x].reshape(320, 128), 0.0)
        masked3[x] = neighbours(masked).reshape(20, 16, 384)
        cots[x] = masked.reshape(20, 16, 128)
        parts = [cots[x, :, 1 + k : 9 + k, :].reshape(160, 128) for k in range(3)]
        masked_even[x] = jnp.concatenate([part.astype(BF16) for part in parts], axis=1)
        masked_odd[x] = jnp.concatenate([part[8:152].astype(BF16) for part in parts], axis=1)
        return carry

    lax.fori_loop(0, 12, prepare, 0)
    for copy in copies[8:]:
        copy.wait()

    def convolve(step, carry):
        x = step * 2
        values = cells[pl.ds(x + 1, 2), 1:19, :, :].reshape(576, 128)
        before = convolve_pair(normed3, x, 18, first)
        before = jnp.where(jnp.abs(values) < LIMIT, before, 0.0)
        sigmoid = jax.nn.sigmoid(before)
        active = before * sigmoid
        act_ref[pl.ds(x, 2)] = active.astype(BF16).reshape(2, 18, 16, 128)
        pair_cells[...] = active.reshape(2, 18, 16, 128)
        for n in range(2):
            inner = pair_cells[n, 1:17, 2:10, :].reshape(128, 128)
            turned_columns(act_t, x + 1 + n, inner)
        active_grad = convolve_pair(masked3, x, 18, second_t)
        pre = active_grad * sigmoid * (1.0 + before * (1.0 - sigmoid))
        pre = jnp.where(values > -LIMIT, pre, 0.0)
        pre_ref[pl.ds(x, 2)] = pre.astype(BF16).reshape(2, 18, 16, 128)
        pair_cells[...] = pre.reshape(2, 18, 16, 128)
        for n in range(2):
            parts = [pair_cells[n, :, 1 + k : 9 + k, :].reshape(144, 128) for k in range(3)]
            pre_even[x + n] = jnp.concatenate([part.astype(BF16) for part in parts], axis=1)
            pre_odd[x + n] = jnp.concatenate([part[8:136].astype(BF16) for part in parts], axis=1)
        return carry

    lax.fori_loop(0, 5, convolve, 0)
    results = [
        pltpu.make_async_copy(source, target, sems.at[n])
        for n, (source, target) in enumerate(((act_ref, act_hbm), (pre_ref, pre_hbm)))
    ]
    for copy in results:
        copy.start()

    for which, left, sides in (
        (1, act_t, ((masked_odd, 16), (masked_even, 16), (masked_odd, 0))),
        (0, normed_t, ((pre_even, 16), (pre_odd, 0), (pre_even, 0))),
    ):
        own = jnp.concatenate([left[:, 128 * i : 128 * (i + 10)] for i in range(3)], axis=0)
        for j, (cots_at, row) in enumerate(sides):
            start = which
            cot = cots_at[start : start + 10, row : row + 128, :].reshape(1280, 384)
            total = jnp.dot(own, cot, preferred_element_type=F32).astype(BF16)
            for i in range(3):
                for k in range(3):
                    found[which, i * 9 + j * 3 + k] = total[
                        i * 128 : (i + 1) * 128, (2 - k) * 128 : (3 - k) * 128
                    ]

    results += [
        pltpu.make_async_copy(found.at[core], own_hbm, sems.at[2]),
        pltpu.make_async_copy(found.at[1 - core], send_hbm, sems.at[3]),
    ]
    for copy in results[2:]:
        copy.start()
    for copy in results:
        copy.wait()


def grads_call(where, gain, pieces, first, second_t):
    return pl.pallas_call(
        grads_kernel,
        out_shape=(
            jax.ShapeDtypeStruct((10, 18, 16, 128), BF16),
            jax.ShapeDtypeStruct((10, 18, 16, 128), BF16),
            jax.ShapeDtypeStruct((27, 128, 128), BF16),
            jax.ShapeDtypeStruct((27, 128, 128), BF16),
        ),
        in_specs=[SM, VM] + [AN] * 8 + [HB] * 2,
        out_specs=(HB, HB, HB, HB),
        scratch_shapes=[
            pltpu.VMEM((12, 20, 16, 128), F32),
            pltpu.VMEM((12, 20, 16, 128), F32),
            pltpu.VMEM((12, 20, 16, 384), BF16),
            pltpu.VMEM((12, 20, 16, 384), BF16),
            pltpu.VMEM((128, 1536), BF16),
            pltpu.VMEM((128, 1536), BF16),
            pltpu.VMEM((20, 16, 128), F32),
            pltpu.VMEM((2, 18, 16, 128), F32),
            pltpu.VMEM((12, 160, 384), BF16),
            pltpu.VMEM((12, 144, 384), BF16),
            pltpu.VMEM((10, 144, 384), BF16),
            pltpu.VMEM((10, 128, 384), BF16),
            pltpu.VMEM((2, 27, 128, 128), BF16),
            *[pltpu.VMEM(shape, BF16) for shape in PIECES],
            pltpu.VMEM((4608, 256), BF16),
            pltpu.VMEM((4608, 256), BF16),
            pltpu.VMEM((10, 18, 16, 128), BF16),
            pltpu.VMEM((10, 18, 16, 128), BF16),
            pltpu.SemaphoreType.DMA((10,)),
        ],
        compiler_params=pltpu.CompilerParams(vmem_limit_bytes=60 << 20),
        cost_estimate=pl.CostEstimate(flops=10 << 30, bytes_accessed=8 << 20, transcendentals=1 << 20),
    )(where, gain, *pieces, first, second_t)


def outputs_kernel(
    gain,
    both_hbm,
    act_hbm,
    pre_hbm,
    second_hbm,
    first_hbm,
    block_ref,
    grad_ref,
    gain_ref,
    both,
    act,
    pre,
    second,
    first_t,
    act3,
    pre3,
    spread,
    sems,
):
    copies = [
        pltpu.make_async_copy(source, target, sems.at[n])
        for n, (source, target) in enumerate(
            (
                (act_hbm, act),
                (pre_hbm, pre),
                (both_hbm, both),
                (second_hbm, second),
                (first_hbm, first_t),
            )
        )
    ]
    for copy in copies:
        copy.start()
    for copy, source, target in ((copies[0], act, act3), (copies[1], pre, pre3)):
        copy.wait()

        def prepare(x, carry):
            values = source[x].reshape(288, 128).astype(F32)
            target[x] = neighbours(values).reshape(18, 16, 384)
            return carry

        lax.fori_loop(0, 10, prepare, 0)

    for copy in copies[2:]:
        copy.wait()
    gains = gain[...]

    def convolve(step, total):
        x = step * 2
        branch = convolve_pair(act3, x, 16, second)
        spread[...] = branch.reshape(2, 16, 16, 128)
        branch = spread[:, :, 2:10, :].reshape(256, 128)
        values = both[0, pl.ds(x, 2)].astype(F32).reshape(256, 128)
        live = values < LIMIT
        held = jnp.where(live, values, 0.0)
        block = jnp.where(live, branch, 0.0) + held
        block_ref[pl.ds(x, 2)] = block.astype(BF16).reshape(2, 16, 8, 128)
        normed_grad = convolve_pair(pre3, x, 16, first_t)
        spread[...] = normed_grad.reshape(2, 16, 16, 128)
        normed_grad = jnp.where(live, spread[:, :, 2:10, :].reshape(256, 128), 0.0)
        inverse = lax.rsqrt(jnp.mean(held * held, axis=-1, keepdims=True) + epsilon)
        total = total + jnp.sum((normed_grad * held * inverse).reshape(32, 8, 128), axis=0)
        upstream = normed_grad * gains
        centred = jnp.mean(held * upstream, axis=-1, keepdims=True)
        extra = inverse * upstream - held * (inverse * inverse * inverse * centred)
        cot = both[1, pl.ds(x, 2)].astype(F32).reshape(256, 128)
        grad = cot + jnp.where(live, extra, 0.0)
        grad_ref[pl.ds(x, 2)] = grad.astype(BF16).reshape(2, 16, 8, 128)
        return total

    total = lax.fori_loop(0, 4, convolve, jnp.zeros((8, 128), F32))
    gain_ref[...] = total


def outputs_call(gain, both, act, pre, second, first_t):
    return pl.pallas_call(
        outputs_kernel,
        out_shape=(
            jax.ShapeDtypeStruct((8, 16, 8, 128), BF16),
            jax.ShapeDtypeStruct((8, 16, 8, 128), BF16),
            jax.ShapeDtypeStruct((8, 128), F32),
        ),
        in_specs=[VM, AN, HB, HB, HB, HB],
        out_specs=(VM,) * 3,
        scratch_shapes=[
            pltpu.VMEM((2, 8, 16, 8, 128), BF16),
            pltpu.VMEM((10, 18, 16, 128), BF16),
            pltpu.VMEM((10, 18, 16, 128), BF16),
            pltpu.VMEM((4608, 256), BF16),
            pltpu.VMEM((4608, 256), BF16),
            pltpu.VMEM((10, 18, 16, 384), BF16),
            pltpu.VMEM((10, 18, 16, 384), BF16),
            pltpu.VMEM((2, 16, 16, 128), F32),
            pltpu.SemaphoreType.DMA((5,)),
        ],
        compiler_params=pltpu.CompilerParams(vmem_limit_bytes=60 << 20),
        cost_estimate=pl.CostEstimate(flops=8 << 30, bytes_accessed=6 << 20, transcendentals=4096),
    )(gain, both, act, pre, second, first_t)


def add_kernel(own_ref, other_ref, out_ref):
    out_ref[...] = (own_ref[...].astype(F32) + other_ref[...].astype(F32)).astype(BF16)


def add_pair(own, other):
    return pl.pallas_call(
        add_kernel,
        out_shape=jax.ShapeDtypeStruct((27, 128, 128), BF16),
        in_specs=[VM, VM],
        out_specs=VM,
        compiler_params=pltpu.CompilerParams(vmem_limit_bytes=6 << 20),
        cost_estimate=pl.CostEstimate(flops=1 << 19, bytes_accessed=3 << 20, transcendentals=0),
    )(own, other)


FIRST = [(i, i ^ 1) for i in range(8)]
SECOND = [(i, i - 1 if i % 2 == 0 else i + 1) for i in range(1, 7)]


def across(pairs):
    return [(a * 2 + s, b * 2 + 1 - s) for a, b in pairs for s in range(2)]


def edges(both, send_one, send_two, layer, layer_one, layer_two):
    x_one = lax.ppermute(send_one, GX, FIRST)
    x_two = lax.ppermute(send_two, GX, SECOND)
    came = lax.ppermute(layer, SA, [(0, 1), (1, 0)])
    came_one = lax.ppermute(layer_one, PLANE, across(FIRST))
    came_two = lax.ppermute(layer_two, PLANE, across(SECOND))

    def wide(start):
        def rows(part):
            return lax.dynamic_slice_in_dim(part, start, 2, axis=2)

        inner = jnp.concatenate([rows(part) for part in (x_one, both, x_two)], axis=1)
        outer = jnp.concatenate([rows(part) for part in (came_one, came, came_two)], axis=1)
        return jnp.concatenate([inner, outer], axis=3)

    first_y, second_y = send_rows(lax.axis_index(GY), 14)
    y_one = lax.ppermute(wide(first_y), GY, FIRST)
    y_two = lax.ppermute(wide(second_y), GY, SECOND)
    return both, x_one, x_two, came, came_one, came_two, y_one, y_two


def exchange(values, axes):
    return lax.all_to_all(values, axes, split_axis=0, concat_axis=0, tiled=True)


def local(sweep_bricks, target_rank, target_slot, conv_first, conv_second, norm_gain, out_grad):
    gain = norm_gain.reshape(1, 128)
    core = lax.axis_index("c")
    where = jnp.stack([lax.axis_index(SA), core, lax.axis_index(GX), lax.axis_index(GY)])
    where = where.astype(jnp.int32)
    both, ((first, first_t), (second, second_t)), where = regroup(
        sweep_bricks.reshape(128, 64, 128),
        target_rank.reshape(1, 128),
        target_slot.reshape(1, 128),
        out_grad,
        where,
        (pair_weights(conv_first), pair_weights(conv_second)),
    )
    pieces = edges(*both)
    act, pre, own, send = grads_call(where, gain, pieces, first, second_t)
    other = lax.ppermute(send, "c", [(0, 1), (1, 0)])
    shares = exchange(add_pair(own, other).reshape(16, 216, 128), PLANE)
    block_out, grid_grad, gain_part = outputs_call(gain, pieces[0], act, pre, second, first_t)

    def halves(row):
        high = row.astype(BF16)
        low = (row - high.astype(F32)).astype(BF16)
        return [high, low, jnp.zeros((6, 128), BF16)]

    def joined(total, row):
        return jnp.concatenate([total.astype(BF16)] + halves(row), axis=0)

    total = jnp.sum(shares.astype(F32), axis=0)
    sent = joined(total, jnp.sum(gain_part, axis=0, keepdims=True))
    parts = [sent] + [along("z", sent, shift) for shift in (1, 2, 3)]
    parts = [part.astype(F32) for part in parts]
    layers = (parts[0] + parts[2]) + (parts[1] + parts[3])
    sent = joined(layers[:216], layers[216:217] + layers[217:218])
    gathered = exchange(jnp.broadcast_to(sent[None], (16, 224, 128)), PLANE)
    swapped = lax.ppermute(gathered, "c", [(0, 1), (1, 0)])
    factor = 1.0 / math.sqrt(131072.0)

    def weights(low, high):
        picked = jnp.where(core == 0, low[:, :216], high[:, :216])
        return (picked.astype(F32) * factor).reshape(27, 128, 128)

    gains = jnp.sum(gathered[:, 216:218].astype(F32), axis=(0, 1))
    gains = gains + jnp.sum(swapped[:, 216:218].astype(F32), axis=(0, 1))
    return (
        block_out,
        grid_grad,
        weights(gathered, swapped),
        weights(swapped, gathered),
        gains * factor,
    )


def solution(mesh):
    inner = Mesh(mesh.devices.reshape(4, 2, 4, 2, 2), ("y", "xl", "z", "c", "xh"))
    in_specs = (
        P(GX, GY, SA, None, None),
        P(GX, GY, SA, None),
        P(GX, GY, SA),
        P(),
        P(),
        P(),
        P(GX, GY, SA, None),
    )
    out_specs = (P(GX, GY, SA, None), P(GX, GY, SA, None), P(), P(), P())
    return jax.shard_map(local, mesh=inner, in_specs=in_specs, out_specs=out_specs, check_vma=False)
```

```python
import functools
import math

import jax
import jax.numpy as jnp
from jax import lax
from jax.experimental import pallas as pl
from jax.experimental.pallas import tpu as pltpu
from jax.sharding import Mesh
from jax.sharding import PartitionSpec as P

epsilon = 1e-06
DEAD = 1.0e30
OUT = -1.0e30
LIMIT = 1.0e29
GX = ("y", "xl")
GY = ("z", "c")
SA = "xh"
PLANE = ("y", "xl", "xh")
F32 = jnp.float32
BF16 = jnp.bfloat16
VM = pl.BlockSpec(memory_space=pltpu.VMEM)
SM = pl.BlockSpec(memory_space=pltpu.SMEM)
AN = pl.BlockSpec(memory_space=pl.ANY)
HB = pl.BlockSpec(memory_space=pltpu.HBM)


def place_kernel(half, code_ref, rows_hbm, o0, o1, o2, o3, fetched, flat, place, lift, sems):
    step = pl.program_id(0)

    def copy(n):
        voxels = rows_hbm.at[:, pl.ds(half * 32 + n * 8, 8), :]
        return pltpu.make_async_copy(voxels, fetched.at[n], sems.at[n])

    @pl.when(step == 0)
    def _():
        for n in range(4):
            copy(n).start()
        slots = lax.broadcasted_iota(jnp.int32, (256, 128), 0)
        chosen = jnp.where(slots == code_ref[half : half + 1, :], 1.0, 0.0)
        place[...] = chosen.astype(BF16)
        named = jnp.max(chosen, axis=1, keepdims=True)
        lift[...] = jnp.broadcast_to(jnp.where(named > 0.0, 0.0, DEAD), (256, 128))

    for n in range(4):

        @pl.when(step == n)
        def _():
            copy(n).wait()
            flat[...] = fetched[n].astype(F32).reshape(1024, 128)

    for voxel in range(8):
        values = flat[pl.ds(voxel, 128, stride=8), :].astype(BF16)
        summed = jnp.dot(place[...], values, preferred_element_type=F32) + lift[...]
        summed = summed.astype(BF16).reshape(4, 4, 16, 128)
        for shift, out in enumerate((o0, o1, o2, o3)):
            out[:, voxel] = summed[shift]


def place_bricks(code, rows, half):
    return pl.pallas_call(
        functools.partial(place_kernel, half),
        out_shape=(jax.ShapeDtypeStruct((4, 32, 16, 128), BF16),) * 4,
        grid=(4,),
        in_specs=[
            pl.BlockSpec((2, 128), lambda i: (0, 0)),
            HB,
        ],
        out_specs=(pl.BlockSpec((4, 8, 16, 128), lambda i: (0, i, 0, 0)),) * 4,
        scratch_shapes=[
            pltpu.VMEM((4, 128, 8, 128), BF16),
            pltpu.VMEM((1024, 128), F32),
            pltpu.VMEM((256, 128), BF16),
            pltpu.VMEM((256, 128), F32),
            pltpu.SemaphoreType.DMA((4,)),
        ],
        compiler_params=pltpu.CompilerParams(vmem_limit_bytes=10 << 20),
        cost_estimate=pl.CostEstimate(flops=1 << 28, bytes_accessed=3 << 20, transcendentals=0),
    )(code, rows)


def added(parts):
    total = jnp.zeros(parts[0].shape, F32)
    filled = jnp.zeros(parts[0].shape[1:], jnp.bool_)
    for part in parts:
        held = part[0] < LIMIT
        filled = filled | held
        total = total + jnp.where(held, part, 0.0)
    return jnp.where(filled, total, DEAD)


def merge_kernel(p0, p1, p2, p3, o0, o1, o2, o3, fetched, sums, sems):
    sources = (p0, p1, p2, p3)
    copies = [
        [
            pltpu.make_async_copy(part.at[shift], fetched.at[shift, n], sems.at[shift, n])
            for n, part in enumerate(sources)
        ]
        for shift in range(4)
    ]
    for shift in (1, 2, 3, 0):
        for copy in copies[shift]:
            copy.start()
    stores = []
    for shift, out in ((1, o1), (2, o2), (3, o3), (0, o0)):
        for copy in copies[shift]:
            copy.wait()

        def block(step, carry):
            at = pl.ds(pl.multiple_of(step * 8, 8), 8)
            parts = [fetched[shift, n, at].astype(F32) for n in range(4)]
            sums[shift, at] = added(parts).astype(BF16)
            return carry

        lax.fori_loop(0, 4, block, 0)
        stores.append(pltpu.make_async_copy(sums.at[shift], out, sems.at[4, shift]))
        stores[-1].start()
    for store in stores:
        store.wait()


def merge_bricks(parts):
    return pl.pallas_call(
        merge_kernel,
        out_shape=(jax.ShapeDtypeStruct((32, 16, 128), BF16),) * 4,
        in_specs=[AN] * 4,
        out_specs=(AN,) * 4,
        scratch_shapes=[
            pltpu.VMEM((4, 4, 32, 16, 128), BF16),
            pltpu.VMEM((4, 32, 16, 128), BF16),
            pltpu.SemaphoreType.DMA((5, 4)),
        ],
        compiler_params=pltpu.CompilerParams(vmem_limit_bytes=60 << 20),
        cost_estimate=pl.CostEstimate(flops=4 << 20, bytes_accessed=3 << 20, transcendentals=0),
    )(*parts)


def send_rows(place, top):
    odd = place % 2
    return top - top * odd, top * odd


def sum_bricks_kernel(
    where_ref,
    a0, a1, a2, a3, b0, b1, b2, b3,
    cot_ref,
    both_ref,
    one_ref,
    two_ref,
    layer_ref,
    layer_one_ref,
    layer_two_ref,
    sums,
    cells,
):
    both_ref[1] = cot_ref[...]
    for half, parts in enumerate(((a0, a1, a2, a3), (b0, b1, b2, b3))):

        def block(step, carry):
            shift_x = half * 2 + step // 2
            shift_y = (step % 2) * 2
            at = pl.ds(pl.multiple_of(step * 8, 8), 8)
            sums[...] = added([part[at].astype(F32) for part in parts]).reshape(128, 128)
            for voxel in range(2):
                for bx in range(2):
                    for by in range(4):
                        slot = voxel * 64 + (bx * 4 + by) * 2
                        spot = (voxel * 2 + bx) * 4 + by
                        cells[spot, 0:4, :] = sums[pl.ds(slot, 4, stride=16), :]
                        cells[spot, 4:8, :] = sums[pl.ds(slot + 1, 4, stride=16), :]
                        both_ref[0, bx * 4 + shift_x, by * 4 + shift_y + voxel] = cells[
                            spot
                        ].astype(BF16)
            return carry

        lax.fori_loop(0, 4, block, 0)
    first_x, second_x = send_rows(where_ref[2], 6)
    one_ref[...] = both_ref[:, pl.ds(first_x, 2)]
    two_ref[...] = both_ref[:, pl.ds(second_x, 2)]
    for side, rows in ((0, slice(6, 8)), (1, slice(0, 2))):

        @pl.when(where_ref[0] == side)
        def _():
            for n in range(2):
                layer_ref[n] = both_ref[n].astype(F32)[:, :, rows, :].astype(BF16)

    layer_one_ref[...] = layer_ref[:, pl.ds(first_x, 2)]
    layer_two_ref[...] = layer_ref[:, pl.ds(second_x, 2)]


def sum_bricks(where, parts, out_grad):
    return pl.pallas_call(
        sum_bricks_kernel,
        out_shape=(
            jax.ShapeDtypeStruct((2, 8, 16, 8, 128), BF16),
            jax.ShapeDtypeStruct((2, 2, 16, 8, 128), BF16),
            jax.ShapeDtypeStruct((2, 2, 16, 8, 128), BF16),
            jax.ShapeDtypeStruct((2, 8, 16, 2, 128), BF16),
            jax.ShapeDtypeStruct((2, 2, 16, 2, 128), BF16),
            jax.ShapeDtypeStruct((2, 2, 16, 2, 128), BF16),
        ),
        in_specs=[SM] + [VM] * 9,
        out_specs=(VM,) * 6,
        scratch_shapes=[pltpu.VMEM((128, 128), F32), pltpu.VMEM((16, 8, 128), F32)],
        compiler_params=pltpu.CompilerParams(vmem_limit_bytes=8 << 20),
        cost_estimate=pl.CostEstimate(flops=8 << 20, bytes_accessed=2 << 20, transcendentals=0),
    )(where, *parts, out_grad)


def along_x(value, shift):
    def place(chip):
        return chip % 2 * 2 + chip // 2

    pairs = [(place(chip), place((chip + shift) % 4)) for chip in range(4)]
    return lax.ppermute(value, ("xl", "xh"), pairs)


def along(axis, value, shift):
    return lax.ppermute(value, axis, [(i, (i + shift) % 4) for i in range(4)])


def regroup(rows, target_rank, target_slot, out_grad, where, weights):
    to_x = target_rank % 2 * 2 + target_rank // 2 % 2
    shift_x = (to_x - (lax.axis_index("xh") * 2 + lax.axis_index("xl"))) & 3
    shift_y = (target_rank // 4 - lax.axis_index("y")) & 3
    major = jnp.concatenate([shift_x, shift_y], axis=0)
    minor = jnp.concatenate([shift_y, shift_x], axis=0)
    codes = (major * 4 + minor) * 16 + target_slot
    placed_a = place_bricks(codes, rows, 0)
    placed_b = place_bricks(codes, rows, 1)
    came_a = [placed_a[0]] + [along_x(placed_a[n], n) for n in (1, 2, 3)]
    came_b = [placed_b[0]] + [along("y", placed_b[n], n) for n in (1, 2, 3)]
    came_a, weights, where = lax.optimization_barrier((came_a, weights, where))
    merged_a = merge_bricks(came_a)
    merged_b = merge_bricks(came_b)
    came_a = [merged_a[0]] + [along("y", merged_a[n], n) for n in (1, 2, 3)]
    came_b = [merged_b[0]] + [along_x(merged_b[n], n) for n in (1, 2, 3)]
    return sum_bricks(where, came_a + came_b, out_grad), weights, where


def window_rows(ref, x, y, slabs, rows):
    part = ref[pl.ds(x, slabs), pl.ds(y, rows), :, :]
    return part.reshape(slabs * rows * 16, part.shape[3])


def gather_windows(ref, x, rows):
    parts = [window_rows(ref, x + i, j, 1, rows) for i in range(4) for j in range(3)]
    return jnp.concatenate(parts, axis=1)


def convolve_pair(ref, x, rows, weights):
    both = jnp.dot(gather_windows(ref, x, rows), weights[...], preferred_element_type=F32)
    return jnp.concatenate([both[:, 0:128], both[:, 128:256]], axis=0)


def pair_kernel(weights_ref, plain_ref, turned_ref):
    a = pl.program_id(0)
    for j in range(3):
        for k in range(3):
            rows = slice(k * 128, (k + 1) * 128)
            for side in range(2):
                x = a - side
                kept = (x >= 0) & (x < 3)
                at = jnp.clip(x, 0, 2) * 9 + j * 3 + k
                columns = slice(side * 128, (side + 1) * 128)
                zero = jnp.zeros((128, 128), BF16)
                plain_ref[0, j, rows, columns] = jnp.where(kept, weights_ref[at], zero)
                turned_ref[0, j, rows, columns] = jnp.where(kept, weights_ref[26 - at].T, zero)


def pair_weights(weights):
    out = jax.ShapeDtypeStruct((4, 3, 384, 256), BF16)
    spec = pl.BlockSpec((1, 3, 384, 256), lambda a: (a, 0, 0, 0))
    plain, turned = pl.pallas_call(
        pair_kernel,
        out_shape=(out, out),
        grid=(4,),
        in_specs=[pl.BlockSpec((27, 128, 128), lambda a: (0, 0, 0))],
        out_specs=(spec, spec),
        compiler_params=pltpu.CompilerParams(vmem_limit_bytes=60 << 20),
        cost_estimate=pl.CostEstimate(flops=1 << 20, bytes_accessed=6 << 20, transcendentals=0),
    )(weights)
    return plain.reshape(4608, 256), turned.reshape(4608, 256)


def neighbours(value):
    count = value.shape[0]
    order = (pltpu.roll(value, 1, 0), value, pltpu.roll(value, count - 1, 0))
    return jnp.concatenate([part.astype(BF16) for part in order], axis=1)


PIECES = (
    (2, 8, 16, 8, 128),
    (2, 2, 16, 8, 128),
    (2, 2, 16, 8, 128),
    (2, 8, 16, 2, 128),
    (2, 2, 16, 2, 128),
    (2, 2, 16, 2, 128),
    (2, 12, 2, 10, 128),
    (2, 12, 2, 10, 128),
)


def fill(volume, which, pieces, where_ref, outside):
    centre, x_one, x_two, layer, layer_one, layer_two, y_one, y_two = pieces
    first_x, second_x = send_rows(where_ref[2], 10)
    first_y, second_y = send_rows(where_ref[3], 18)
    at_one = pl.ds(first_x, 2)
    at_two = pl.ds(second_x, 2)
    volume[...] = jnp.full(volume.shape, outside, F32)
    volume[2:10, 2:18, 2:10, :] = centre[which].astype(F32)
    volume[at_one, 2:18, 2:10, :] = x_one[which].astype(F32)
    volume[at_two, 2:18, 2:10, :] = x_two[which].astype(F32)
    sides = ((y_one, pl.ds(first_y, 2)), (y_two, pl.ds(second_y, 2)))
    spans = ((at_one, slice(0, 2)), (slice(2, 10), slice(2, 10)), (at_two, slice(10, 12)))
    for came, at_y in sides:
        values = came[which].astype(F32)
        for at_x, rows in spans:
            volume[at_x, at_y, 2:10, :] = values[rows, :, 0:8]
    for side, at_z in ((0, slice(10, 12)), (1, slice(0, 2))):

        @pl.when(where_ref[0] == side)
        def _():
            volume[2:10, 2:18, at_z, :] = layer[which].astype(F32)
            volume[at_one, 2:18, at_z, :] = layer_one[which].astype(F32)
            volume[at_two, 2:18, at_z, :] = layer_two[which].astype(F32)
            for came, at_y in sides:
                values = came[which].astype(F32)
                for at_x, rows in spans:
                    volume[at_x, at_y, at_z, :] = values[rows, :, 8:10]

    @pl.when(where_ref[2] == 0)
    def _():
        volume[0:2] = jnp.full((2, 20, 16, 128), outside, F32)

    @pl.when(where_ref[2] == 7)
    def _():
        volume[10:12] = jnp.full((2, 20, 16, 128), outside, F32)

    @pl.when(where_ref[3] == 0)
    def _():
        volume[:, 0:2] = jnp.full((12, 2, 16, 128), outside, F32)

    @pl.when(where_ref[3] == 7)
    def _():
        volume[:, 18:20] = jnp.full((12, 2, 16, 128), outside, F32)


def grads_kernel(
    where_ref,
    gain,
    p0, p1, p2, p3, p4, p5, p6, p7,
    first_hbm,
    second_hbm,
    act_hbm,
    pre_hbm,
    own_hbm,
    send_hbm,
    cells,
    cots,
    normed3,
    masked3,
    act_t,
    normed_t,
    row_cells,
    pair_cells,
    masked_even,
    masked_odd,
    pre_even,
    pre_odd,
    found,
    s0, s1, s2, s3, s4, s5, s6, s7,
    first,
    second_t,
    act_ref,
    pre_ref,
    sems,
):
    core = where_ref[1]
    pieces = (s0, s1, s2, s3, s4, s5, s6, s7)
    copies = [
        pltpu.make_async_copy(source, target, sems.at[n])
        for n, (source, target) in enumerate(
            zip((p0, p1, p2, p3, p4, p5, p6, p7, first_hbm, second_hbm), (*pieces, first, second_t))
        )
    ]
    for copy in copies:
        copy.start()
    for copy in copies[:8]:
        copy.wait()
    fill(cells, 0, pieces, where_ref, OUT)
    fill(cots, 1, pieces, where_ref, 0.0)
    act_t[:, 0:128] = jnp.zeros((128, 128), BF16)
    act_t[:, 1408:1536] = jnp.zeros((128, 128), BF16)

    def turned_columns(target, x, values):
        inner = jnp.where((x >= 2) & (x < 10), values, 0.0).astype(BF16)
        target[:, pl.ds(pl.multiple_of(x * 128, 128), 128)] = inner.T

    def prepare(x, carry):
        values = cells[x].reshape(320, 128)
        live = jnp.abs(values) < LIMIT
        held = jnp.where(live, values, 0.0)
        inverse = lax.rsqrt(jnp.mean(held * held, axis=-1, keepdims=True) + epsilon)
        normed = held * inverse * gain[...]
        normed3[x] = neighbours(normed).reshape(20, 16, 384)
        row_cells[...] = normed.reshape(20, 16, 128)
        turned_columns(normed_t, x, row_cells[2:18, 2:10, :].reshape(128, 128))
        masked = jnp.where(live, cots[x].reshape(320, 128), 0.0)
        masked3[x] = neighbours(masked).reshape(20, 16, 384)
        cots[x] = masked.reshape(20, 16, 128)
        parts = [cots[x, :, 1 + k : 9 + k, :].reshape(160, 128) for k in range(3)]
        masked_even[x] = jnp.concatenate([part.astype(BF16) for part in parts], axis=1)
        masked_odd[x] = jnp.concatenate([part[8:152].astype(BF16) for part in parts], axis=1)
        return carry

    lax.fori_loop(0, 12, prepare, 0)
    for copy in copies[8:]:
        copy.wait()

    def convolve(step, carry):
        x = step * 2
        values = cells[pl.ds(x + 1, 2), 1:19, :, :].reshape(576, 128)
        before = convolve_pair(normed3, x, 18, first)
        before = jnp.where(jnp.abs(values) < LIMIT, before, 0.0)
        sigmoid = jax.nn.sigmoid(before)
        active = before * sigmoid
        act_ref[pl.ds(x, 2)] = active.astype(BF16).reshape(2, 18, 16, 128)
        pair_cells[...] = active.reshape(2, 18, 16, 128)
        for n in range(2):
            inner = pair_cells[n, 1:17, 2:10, :].reshape(128, 128)
            turned_columns(act_t, x + 1 + n, inner)
        active_grad = convolve_pair(masked3, x, 18, second_t)
        pre = active_grad * sigmoid * (1.0 + before * (1.0 - sigmoid))
        pre = jnp.where(values > -LIMIT, pre, 0.0)
        pre_ref[pl.ds(x, 2)] = pre.astype(BF16).reshape(2, 18, 16, 128)
        pair_cells[...] = pre.reshape(2, 18, 16, 128)
        for n in range(2):
            parts = [pair_cells[n, :, 1 + k : 9 + k, :].reshape(144, 128) for k in range(3)]
            pre_even[x + n] = jnp.concatenate([part.astype(BF16) for part in parts], axis=1)
            pre_odd[x + n] = jnp.concatenate([part[8:136].astype(BF16) for part in parts], axis=1)
        return carry

    lax.fori_loop(0, 5, convolve, 0)
    results = [
        pltpu.make_async_copy(source, target, sems.at[n])
        for n, (source, target) in enumerate(((act_ref, act_hbm), (pre_ref, pre_hbm)))
    ]
    for copy in results:
        copy.start()

    for which, left, sides in (
        (1, act_t, ((masked_odd, 16), (masked_even, 16), (masked_odd, 0))),
        (0, normed_t, ((pre_even, 16), (pre_odd, 0), (pre_even, 0))),
    ):
        own = jnp.concatenate([left[:, 128 * i : 128 * (i + 10)] for i in range(3)], axis=0)
        for j, (cots_at, row) in enumerate(sides):
            start = which
            cot = cots_at[start : start + 10, row : row + 128, :].reshape(1280, 384)
            total = jnp.dot(own, cot, preferred_element_type=F32).astype(BF16)
            for i in range(3):
                for k in range(3):
                    found[which, i * 9 + j * 3 + k] = total[
                        i * 128 : (i + 1) * 128, (2 - k) * 128 : (3 - k) * 128
                    ]

    results += [
        pltpu.make_async_copy(found.at[core], own_hbm, sems.at[2]),
        pltpu.make_async_copy(found.at[1 - core], send_hbm, sems.at[3]),
    ]
    for copy in results[2:]:
        copy.start()
    for copy in results:
        copy.wait()


def grads_call(where, gain, pieces, first, second_t):
    return pl.pallas_call(
        grads_kernel,
        out_shape=(
            jax.ShapeDtypeStruct((10, 18, 16, 128), BF16),
            jax.ShapeDtypeStruct((10, 18, 16, 128), BF16),
            jax.ShapeDtypeStruct((27, 128, 128), BF16),
            jax.ShapeDtypeStruct((27, 128, 128), BF16),
        ),
        in_specs=[SM, VM] + [AN] * 8 + [HB] * 2,
        out_specs=(HB, HB, HB, HB),
        scratch_shapes=[
            pltpu.VMEM((12, 20, 16, 128), F32),
            pltpu.VMEM((12, 20, 16, 128), F32),
            pltpu.VMEM((12, 20, 16, 384), BF16),
            pltpu.VMEM((12, 20, 16, 384), BF16),
            pltpu.VMEM((128, 1536), BF16),
            pltpu.VMEM((128, 1536), BF16),
            pltpu.VMEM((20, 16, 128), F32),
            pltpu.VMEM((2, 18, 16, 128), F32),
            pltpu.VMEM((12, 160, 384), BF16),
            pltpu.VMEM((12, 144, 384), BF16),
            pltpu.VMEM((10, 144, 384), BF16),
            pltpu.VMEM((10, 128, 384), BF16),
            pltpu.VMEM((2, 27, 128, 128), BF16),
            *[pltpu.VMEM(shape, BF16) for shape in PIECES],
            pltpu.VMEM((4608, 256), BF16),
            pltpu.VMEM((4608, 256), BF16),
            pltpu.VMEM((10, 18, 16, 128), BF16),
            pltpu.VMEM((10, 18, 16, 128), BF16),
            pltpu.SemaphoreType.DMA((10,)),
        ],
        compiler_params=pltpu.CompilerParams(vmem_limit_bytes=60 << 20),
        cost_estimate=pl.CostEstimate(flops=10 << 30, bytes_accessed=8 << 20, transcendentals=1 << 20),
    )(where, gain, *pieces, first, second_t)


def outputs_kernel(
    gain,
    both_hbm,
    act_hbm,
    pre_hbm,
    second_hbm,
    first_hbm,
    block_ref,
    grad_ref,
    gain_ref,
    both,
    act,
    pre,
    second,
    first_t,
    act3,
    pre3,
    spread,
    sems,
):
    copies = [
        pltpu.make_async_copy(source, target, sems.at[n])
        for n, (source, target) in enumerate(
            (
                (act_hbm, act),
                (pre_hbm, pre),
                (both_hbm, both),
                (second_hbm, second),
                (first_hbm, first_t),
            )
        )
    ]
    for copy in copies:
        copy.start()
    for copy, source, target in ((copies[0], act, act3), (copies[1], pre, pre3)):
        copy.wait()

        def prepare(x, carry):
            values = source[x].reshape(288, 128).astype(F32)
            target[x] = neighbours(values).reshape(18, 16, 384)
            return carry

        lax.fori_loop(0, 10, prepare, 0)

    for copy in copies[2:]:
        copy.wait()
    gains = gain[...]

    def convolve(step, total):
        x = step * 2
        branch = convolve_pair(act3, x, 16, second)
        spread[...] = branch.reshape(2, 16, 16, 128)
        branch = spread[:, :, 2:10, :].reshape(256, 128)
        values = both[0, pl.ds(x, 2)].astype(F32).reshape(256, 128)
        live = values < LIMIT
        held = jnp.where(live, values, 0.0)
        block = jnp.where(live, branch, 0.0) + held
        block_ref[pl.ds(x, 2)] = block.astype(BF16).reshape(2, 16, 8, 128)
        normed_grad = convolve_pair(pre3, x, 16, first_t)
        spread[...] = normed_grad.reshape(2, 16, 16, 128)
        normed_grad = jnp.where(live, spread[:, :, 2:10, :].reshape(256, 128), 0.0)
        inverse = lax.rsqrt(jnp.mean(held * held, axis=-1, keepdims=True) + epsilon)
        total = total + jnp.sum((normed_grad * held * inverse).reshape(32, 8, 128), axis=0)
        upstream = normed_grad * gains
        centred = jnp.mean(held * upstream, axis=-1, keepdims=True)
        extra = inverse * upstream - held * (inverse * inverse * inverse * centred)
        cot = both[1, pl.ds(x, 2)].astype(F32).reshape(256, 128)
        grad = cot + jnp.where(live, extra, 0.0)
        grad_ref[pl.ds(x, 2)] = grad.astype(BF16).reshape(2, 16, 8, 128)
        return total

    total = lax.fori_loop(0, 4, convolve, jnp.zeros((8, 128), F32))
    gain_ref[...] = total


def outputs_call(gain, both, act, pre, second, first_t):
    return pl.pallas_call(
        outputs_kernel,
        out_shape=(
            jax.ShapeDtypeStruct((8, 16, 8, 128), BF16),
            jax.ShapeDtypeStruct((8, 16, 8, 128), BF16),
            jax.ShapeDtypeStruct((8, 128), F32),
        ),
        in_specs=[VM, AN, HB, HB, HB, HB],
        out_specs=(VM,) * 3,
        scratch_shapes=[
            pltpu.VMEM((2, 8, 16, 8, 128), BF16),
            pltpu.VMEM((10, 18, 16, 128), BF16),
            pltpu.VMEM((10, 18, 16, 128), BF16),
            pltpu.VMEM((4608, 256), BF16),
            pltpu.VMEM((4608, 256), BF16),
            pltpu.VMEM((10, 18, 16, 384), BF16),
            pltpu.VMEM((10, 18, 16, 384), BF16),
            pltpu.VMEM((2, 16, 16, 128), F32),
            pltpu.SemaphoreType.DMA((5,)),
        ],
        compiler_params=pltpu.CompilerParams(vmem_limit_bytes=60 << 20),
        cost_estimate=pl.CostEstimate(flops=8 << 30, bytes_accessed=6 << 20, transcendentals=4096),
    )(gain, both, act, pre, second, first_t)


def add_kernel(own_ref, other_ref, out_ref):
    out_ref[...] = (own_ref[...].astype(F32) + other_ref[...].astype(F32)).astype(BF16)


def add_pair(own, other):
    return pl.pallas_call(
        add_kernel,
        out_shape=jax.ShapeDtypeStruct((27, 128, 128), BF16),
        in_specs=[VM, VM],
        out_specs=VM,
        compiler_params=pltpu.CompilerParams(vmem_limit_bytes=6 << 20),
        cost_estimate=pl.CostEstimate(flops=1 << 19, bytes_accessed=3 << 20, transcendentals=0),
    )(own, other)


FIRST = [(i, i ^ 1) for i in range(8)]
SECOND = [(i, i - 1 if i % 2 == 0 else i + 1) for i in range(1, 7)]


def across(pairs):
    return [(a * 2 + s, b * 2 + 1 - s) for a, b in pairs for s in range(2)]


def edges(both, send_one, send_two, layer, layer_one, layer_two):
    x_one = lax.ppermute(send_one, GX, FIRST)
    x_two = lax.ppermute(send_two, GX, SECOND)
    came = lax.ppermute(layer, SA, [(0, 1), (1, 0)])
    came_one = lax.ppermute(layer_one, PLANE, across(FIRST))
    came_two = lax.ppermute(layer_two, PLANE, across(SECOND))

    def wide(start):
        def rows(part):
            return lax.dynamic_slice_in_dim(part, start, 2, axis=2)

        inner = jnp.concatenate([rows(part) for part in (x_one, both, x_two)], axis=1)
        outer = jnp.concatenate([rows(part) for part in (came_one, came, came_two)], axis=1)
        return jnp.concatenate([inner, outer], axis=3)

    first_y, second_y = send_rows(lax.axis_index(GY), 14)
    y_one = lax.ppermute(wide(first_y), GY, FIRST)
    y_two = lax.ppermute(wide(second_y), GY, SECOND)
    return both, x_one, x_two, came, came_one, came_two, y_one, y_two


def exchange(values, axes):
    return lax.all_to_all(values, axes, split_axis=0, concat_axis=0, tiled=True)


def local(sweep_bricks, target_rank, target_slot, conv_first, conv_second, norm_gain, out_grad):
    gain = norm_gain.reshape(1, 128)
    core = lax.axis_index("c")
    where = jnp.stack([lax.axis_index(SA), core, lax.axis_index(GX), lax.axis_index(GY)])
    where = where.astype(jnp.int32)
    both, ((first, first_t), (second, second_t)), where = regroup(
        sweep_bricks.reshape(128, 64, 128),
        target_rank.reshape(1, 128),
        target_slot.reshape(1, 128),
        out_grad,
        where,
        (pair_weights(conv_first), pair_weights(conv_second)),
    )
    pieces = edges(*both)
    act, pre, own, send = grads_call(where, gain, pieces, first, second_t)
    other = lax.ppermute(send, "c", [(0, 1), (1, 0)])
    shares = exchange(add_pair(own, other).reshape(16, 216, 128), PLANE)
    block_out, grid_grad, gain_part = outputs_call(gain, pieces[0], act, pre, second, first_t)

    def halves(row):
        high = row.astype(BF16)
        low = (row - high.astype(F32)).astype(BF16)
        return [high, low, jnp.zeros((6, 128), BF16)]

    def joined(total, row):
        return jnp.concatenate([total.astype(BF16)] + halves(row), axis=0)

    total = jnp.sum(shares.astype(F32), axis=0)
    sent = joined(total, jnp.sum(gain_part, axis=0, keepdims=True))
    parts = [sent] + [along("z", sent, shift) for shift in (1, 2, 3)]
    parts = [part.astype(F32) for part in parts]
    layers = (parts[0] + parts[2]) + (parts[1] + parts[3])
    sent = joined(layers[:216], layers[216:217] + layers[217:218])
    gathered = exchange(jnp.broadcast_to(sent[None], (16, 224, 128)), PLANE)
    swapped = lax.ppermute(gathered, "c", [(0, 1), (1, 0)])
    factor = 1.0 / math.sqrt(131072.0)

    def weights(low, high):
        picked = jnp.where(core == 0, low[:, :216], high[:, :216])
        return (picked.astype(F32) * factor).reshape(27, 128, 128)

    gains = jnp.sum(gathered[:, 216:218].astype(F32), axis=(0, 1))
    gains = gains + jnp.sum(swapped[:, 216:218].astype(F32), axis=(0, 1))
    return (
        block_out,
        grid_grad,
        weights(gathered, swapped),
        weights(swapped, gathered),
        gains * factor,
    )


def solution(mesh):
    inner = Mesh(mesh.devices.reshape(4, 2, 4, 2, 2), ("y", "xl", "z", "c", "xh"))
    in_specs = (
        P(GX, GY, SA, None, None),
        P(GX, GY, SA, None),
        P(GX, GY, SA),
        P(),
        P(),
        P(),
        P(GX, GY, SA, None),
    )
    out_specs = (P(GX, GY, SA, None), P(GX, GY, SA, None), P(), P(), P())
    return jax.shard_map(local, mesh=inner, in_specs=in_specs, out_specs=out_specs, check_vma=False)
```

```python
import functools
import math

import jax
import jax.numpy as jnp
from jax import lax
from jax.experimental import pallas as pl
from jax.experimental.pallas import tpu as pltpu
from jax.sharding import Mesh
from jax.sharding import PartitionSpec as P

epsilon = 1e-06
DEAD = 1.0e30
OUT = -1.0e30
LIMIT = 1.0e29
GX = ("y", "xl")
GY = ("z", "c")
SA = "xh"
PLANE = ("y", "xl", "xh")
F32 = jnp.float32
BF16 = jnp.bfloat16
VM = pl.BlockSpec(memory_space=pltpu.VMEM)
SM = pl.BlockSpec(memory_space=pltpu.SMEM)
AN = pl.BlockSpec(memory_space=pl.ANY)
HB = pl.BlockSpec(memory_space=pltpu.HBM)


def place_kernel(half, code_ref, rows_hbm, o0, o1, o2, o3, fetched, flat, place, lift, sems):
    step = pl.program_id(0)

    def copy(n):
        voxels = rows_hbm.at[:, pl.ds(half * 32 + n * 8, 8), :]
        return pltpu.make_async_copy(voxels, fetched.at[n], sems.at[n])

    @pl.when(step == 0)
    def _():
        for n in range(4):
            copy(n).start()
        slots = lax.broadcasted_iota(jnp.int32, (256, 128), 0)
        chosen = jnp.where(slots == code_ref[half : half + 1, :], 1.0, 0.0)
        place[...] = chosen.astype(BF16)
        named = jnp.max(chosen, axis=1, keepdims=True)
        lift[...] = jnp.broadcast_to(jnp.where(named > 0.0, 0.0, DEAD), (256, 128))

    for n in range(4):

        @pl.when(step == n)
        def _():
            copy(n).wait()
            flat[...] = fetched[n].astype(F32).reshape(1024, 128)

    for voxel in range(8):
        values = flat[pl.ds(voxel, 128, stride=8), :].astype(BF16)
        summed = jnp.dot(place[...], values, preferred_element_type=F32) + lift[...]
        summed = summed.astype(BF16).reshape(4, 4, 16, 128)
        for shift, out in enumerate((o0, o1, o2, o3)):
            out[:, voxel] = summed[shift]


def place_bricks(code, rows, half):
    return pl.pallas_call(
        functools.partial(place_kernel, half),
        out_shape=(jax.ShapeDtypeStruct((4, 32, 16, 128), BF16),) * 4,
        grid=(4,),
        in_specs=[
            pl.BlockSpec((2, 128), lambda i: (0, 0)),
            HB,
        ],
        out_specs=(pl.BlockSpec((4, 8, 16, 128), lambda i: (0, i, 0, 0)),) * 4,
        scratch_shapes=[
            pltpu.VMEM((4, 128, 8, 128), BF16),
            pltpu.VMEM((1024, 128), F32),
            pltpu.VMEM((256, 128), BF16),
            pltpu.VMEM((256, 128), F32),
            pltpu.SemaphoreType.DMA((4,)),
        ],
        compiler_params=pltpu.CompilerParams(vmem_limit_bytes=10 << 20),
        cost_estimate=pl.CostEstimate(flops=1 << 28, bytes_accessed=3 << 20, transcendentals=0),
    )(code, rows)


def added(parts):
    total = jnp.zeros(parts[0].shape, F32)
    filled = jnp.zeros(parts[0].shape[1:], jnp.bool_)
    for part in parts:
        held = part[0] < LIMIT
        filled = filled | held
        total = total + jnp.where(held, part, 0.0)
    return jnp.where(filled, total, DEAD)


def merge_kernel(p0, p1, p2, p3, o0, o1, o2, o3, fetched, sums, sems):
    sources = (p0, p1, p2, p3)
    copies = [
        [
            pltpu.make_async_copy(part.at[shift], fetched.at[shift, n], sems.at[shift, n])
            for n, part in enumerate(sources)
        ]
        for shift in range(4)
    ]
    for shift in (1, 2, 3, 0):
        for copy in copies[shift]:
            copy.start()
    stores = []
    for shift, out in ((1, o1), (2, o2), (3, o3), (0, o0)):
        for copy in copies[shift]:
            copy.wait()

        def block(step, carry):
            at = pl.ds(pl.multiple_of(step * 8, 8), 8)
            parts = [fetched[shift, n, at].astype(F32) for n in range(4)]
            sums[shift, at] = added(parts).astype(BF16)
            return carry

        lax.fori_loop(0, 4, block, 0)
        stores.append(pltpu.make_async_copy(sums.at[shift], out, sems.at[4, shift]))
        stores[-1].start()
    for store in stores:
        store.wait()


def merge_bricks(parts):
    return pl.pallas_call(
        merge_kernel,
        out_shape=(jax.ShapeDtypeStruct((32, 16, 128), BF16),) * 4,
        in_specs=[AN] * 4,
        out_specs=(AN,) * 4,
        scratch_shapes=[
            pltpu.VMEM((4, 4, 32, 16, 128), BF16),
            pltpu.VMEM((4, 32, 16, 128), BF16),
            pltpu.SemaphoreType.DMA((5, 4)),
        ],
        compiler_params=pltpu.CompilerParams(vmem_limit_bytes=60 << 20),
        cost_estimate=pl.CostEstimate(flops=4 << 20, bytes_accessed=3 << 20, transcendentals=0),
    )(*parts)


def send_rows(place, top):
    odd = place % 2
    return top - top * odd, top * odd


def sum_bricks_kernel(
    where_ref,
    a0, a1, a2, a3, b0, b1, b2, b3,
    cot_ref,
    both_ref,
    one_ref,
    two_ref,
    layer_ref,
    layer_one_ref,
    layer_two_ref,
    sums,
    cells,
):
    both_ref[1] = cot_ref[...]
    for half, parts in enumerate(((a0, a1, a2, a3), (b0, b1, b2, b3))):

        def block(step, carry):
            shift_x = half * 2 + step // 2
            shift_y = (step % 2) * 2
            at = pl.ds(pl.multiple_of(step * 8, 8), 8)
            sums[...] = added([part[at].astype(F32) for part in parts]).reshape(128, 128)
            for voxel in range(2):
                for bx in range(2):
                    for by in range(4):
                        slot = voxel * 64 + (bx * 4 + by) * 2
                        spot = (voxel * 2 + bx) * 4 + by
                        cells[spot, 0:4, :] = sums[pl.ds(slot, 4, stride=16), :]
                        cells[spot, 4:8, :] = sums[pl.ds(slot + 1, 4, stride=16), :]
                        both_ref[0, bx * 4 + shift_x, by * 4 + shift_y + voxel] = cells[
                            spot
                        ].astype(BF16)
            return carry

        lax.fori_loop(0, 4, block, 0)
    first_x, second_x = send_rows(where_ref[2], 6)
    one_ref[...] = both_ref[:, pl.ds(first_x, 2)]
    two_ref[...] = both_ref[:, pl.ds(second_x, 2)]
    for side, rows in ((0, slice(6, 8)), (1, slice(0, 2))):

        @pl.when(where_ref[0] == side)
        def _():
            for n in range(2):
                layer_ref[n] = both_ref[n].astype(F32)[:, :, rows, :].astype(BF16)

    layer_one_ref[...] = layer_ref[:, pl.ds(first_x, 2)]
    layer_two_ref[...] = layer_ref[:, pl.ds(second_x, 2)]


def sum_bricks(where, parts, out_grad):
    return pl.pallas_call(
        sum_bricks_kernel,
        out_shape=(
            jax.ShapeDtypeStruct((2, 8, 16, 8, 128), BF16),
            jax.ShapeDtypeStruct((2, 2, 16, 8, 128), BF16),
            jax.ShapeDtypeStruct((2, 2, 16, 8, 128), BF16),
            jax.ShapeDtypeStruct((2, 8, 16, 2, 128), BF16),
            jax.ShapeDtypeStruct((2, 2, 16, 2, 128), BF16),
            jax.ShapeDtypeStruct((2, 2, 16, 2, 128), BF16),
        ),
        in_specs=[SM] + [VM] * 9,
        out_specs=(VM,) * 6,
        scratch_shapes=[pltpu.VMEM((128, 128), F32), pltpu.VMEM((16, 8, 128), F32)],
        compiler_params=pltpu.CompilerParams(vmem_limit_bytes=8 << 20),
        cost_estimate=pl.CostEstimate(flops=8 << 20, bytes_accessed=2 << 20, transcendentals=0),
    )(where, *parts, out_grad)


def along_x(value, shift):
    def place(chip):
        return chip % 2 * 2 + chip // 2

    pairs = [(place(chip), place((chip + shift) % 4)) for chip in range(4)]
    return lax.ppermute(value, ("xl", "xh"), pairs)


def along(axis, value, shift):
    return lax.ppermute(value, axis, [(i, (i + shift) % 4) for i in range(4)])


def regroup(rows, target_rank, target_slot, out_grad, where, weights):
    to_x = target_rank % 2 * 2 + target_rank // 2 % 2
    shift_x = (to_x - (lax.axis_index("xh") * 2 + lax.axis_index("xl"))) & 3
    shift_y = (target_rank // 4 - lax.axis_index("y")) & 3
    major = jnp.concatenate([shift_x, shift_y], axis=0)
    minor = jnp.concatenate([shift_y, shift_x], axis=0)
    codes = (major * 4 + minor) * 16 + target_slot
    placed_a = place_bricks(codes, rows, 0)
    placed_b = place_bricks(codes, rows, 1)
    came_a = [placed_a[0]] + [along_x(placed_a[n], n) for n in (1, 2, 3)]
    came_b = [placed_b[0]] + [along("y", placed_b[n], n) for n in (1, 2, 3)]
    came_a, weights, where = lax.optimization_barrier((came_a, weights, where))
    merged_a = merge_bricks(came_a)
    merged_b = merge_bricks(came_b)
    came_a = [merged_a[0]] + [along("y", merged_a[n], n) for n in (1, 2, 3)]
    came_b = [merged_b[0]] + [along_x(merged_b[n], n) for n in (1, 2, 3)]
    return sum_bricks(where, came_a + came_b, out_grad), weights, where


def window_rows(ref, x, y, slabs, rows):
    part = ref[pl.ds(x, slabs), pl.ds(y, rows), :, :]
    return part.reshape(slabs * rows * 16, part.shape[3])


def gather_windows(ref, x, rows):
    parts = [window_rows(ref, x + i, j, 1, rows) for i in range(4) for j in range(3)]
    return jnp.concatenate(parts, axis=1)


def convolve_pair(ref, x, rows, weights):
    both = jnp.dot(gather_windows(ref, x, rows), weights[...], preferred_element_type=F32)
    return jnp.concatenate([both[:, 0:128], both[:, 128:256]], axis=0)


def pair_kernel(weights_ref, plain_ref, turned_ref):
    a = pl.program_id(0)
    for j in range(3):
        for k in range(3):
            rows = slice(k * 128, (k + 1) * 128)
            for side in range(2):
                x = a - side
                kept = (x >= 0) & (x < 3)
                at = jnp.clip(x, 0, 2) * 9 + j * 3 + k
                columns = slice(side * 128, (side + 1) * 128)
                zero = jnp.zeros((128, 128), BF16)
                plain_ref[0, j, rows, columns] = jnp.where(kept, weights_ref[at], zero)
                turned_ref[0, j, rows, columns] = jnp.where(kept, weights_ref[26 - at].T, zero)


def pair_weights(weights):
    out = jax.ShapeDtypeStruct((4, 3, 384, 256), BF16)
    spec = pl.BlockSpec((1, 3, 384, 256), lambda a: (a, 0, 0, 0))
    plain, turned = pl.pallas_call(
        pair_kernel,
        out_shape=(out, out),
        grid=(4,),
        in_specs=[pl.BlockSpec((27, 128, 128), lambda a: (0, 0, 0))],
        out_specs=(spec, spec),
        compiler_params=pltpu.CompilerParams(vmem_limit_bytes=60 << 20),
        cost_estimate=pl.CostEstimate(flops=1 << 20, bytes_accessed=6 << 20, transcendentals=0),
    )(weights)
    return plain.reshape(4608, 256), turned.reshape(4608, 256)


def neighbours(value):
    count = value.shape[0]
    order = (pltpu.roll(value, 1, 0), value, pltpu.roll(value, count - 1, 0))
    return jnp.concatenate([part.astype(BF16) for part in order], axis=1)


PIECES = (
    (2, 8, 16, 8, 128),
    (2, 2, 16, 8, 128),
    (2, 2, 16, 8, 128),
    (2, 8, 16, 2, 128),
    (2, 2, 16, 2, 128),
    (2, 2, 16, 2, 128),
    (2, 12, 2, 10, 128),
    (2, 12, 2, 10, 128),
)


def fill(volume, which, pieces, where_ref, outside):
    centre, x_one, x_two, layer, layer_one, layer_two, y_one, y_two = pieces
    first_x, second_x = send_rows(where_ref[2], 10)
    first_y, second_y = send_rows(where_ref[3], 18)
    at_one = pl.ds(first_x, 2)
    at_two = pl.ds(second_x, 2)
    if outside is not None:
        volume[...] = jnp.full(volume.shape, outside, F32)
    volume[2:10, 2:18, 2:10, :] = centre[which].astype(F32)
    volume[at_one, 2:18, 2:10, :] = x_one[which].astype(F32)
    volume[at_two, 2:18, 2:10, :] = x_two[which].astype(F32)
    sides = ((y_one, pl.ds(first_y, 2)), (y_two, pl.ds(second_y, 2)))
    spans = ((at_one, slice(0, 2)), (slice(2, 10), slice(2, 10)), (at_two, slice(10, 12)))
    for came, at_y in sides:
        values = came[which].astype(F32)
        for at_x, rows in spans:
            volume[at_x, at_y, 2:10, :] = values[rows, :, 0:8]
    for side, at_z in ((0, slice(10, 12)), (1, slice(0, 2))):

        @pl.when(where_ref[0] == side)
        def _():
            volume[2:10, 2:18, at_z, :] = layer[which].astype(F32)
            volume[at_one, 2:18, at_z, :] = layer_one[which].astype(F32)
            volume[at_two, 2:18, at_z, :] = layer_two[which].astype(F32)
            for came, at_y in sides:
                values = came[which].astype(F32)
                for at_x, rows in spans:
                    volume[at_x, at_y, at_z, :] = values[rows, :, 8:10]

    if outside is None:
        return

    @pl.when(where_ref[2] == 0)
    def _():
        volume[0:2] = jnp.full((2, 20, 16, 128), outside, F32)

    @pl.when(where_ref[2] == 7)
    def _():
        volume[10:12] = jnp.full((2, 20, 16, 128), outside, F32)

    @pl.when(where_ref[3] == 0)
    def _():
        volume[:, 0:2] = jnp.full((12, 2, 16, 128), outside, F32)

    @pl.when(where_ref[3] == 7)
    def _():
        volume[:, 18:20] = jnp.full((12, 2, 16, 128), outside, F32)


def grads_kernel(
    where_ref,
    gain,
    p0, p1, p2, p3, p4, p5, p6, p7,
    first_hbm,
    second_hbm,
    act_hbm,
    pre_hbm,
    own_hbm,
    send_hbm,
    cells,
    cots,
    normed3,
    masked3,
    act_t,
    normed_t,
    row_cells,
    pair_cells,
    masked_even,
    masked_odd,
    pre_even,
    pre_odd,
    found,
    s0, s1, s2, s3, s4, s5, s6, s7,
    first,
    second_t,
    act_ref,
    pre_ref,
    sems,
):
    core = where_ref[1]
    pieces = (s0, s1, s2, s3, s4, s5, s6, s7)
    copies = [
        pltpu.make_async_copy(source, target, sems.at[n])
        for n, (source, target) in enumerate(
            zip((p0, p1, p2, p3, p4, p5, p6, p7, first_hbm, second_hbm), (*pieces, first, second_t))
        )
    ]
    for copy in copies:
        copy.start()
    for copy in copies[:8]:
        copy.wait()
    fill(cells, 0, pieces, where_ref, OUT)
    fill(cots, 1, pieces, where_ref, None)
    act_t[:, 0:128] = jnp.zeros((128, 128), BF16)
    act_t[:, 1408:1536] = jnp.zeros((128, 128), BF16)

    def turned_columns(target, x, values):
        inner = jnp.where((x >= 2) & (x < 10), values, 0.0).astype(BF16)
        target[:, pl.ds(pl.multiple_of(x * 128, 128), 128)] = inner.T

    def prepare(x, carry):
        values = cells[x].reshape(320, 128)
        live = jnp.abs(values) < LIMIT
        held = jnp.where(live, values, 0.0)
        inverse = lax.rsqrt(jnp.mean(held * held, axis=-1, keepdims=True) + epsilon)
        normed = held * inverse * gain[...]
        normed3[x] = neighbours(normed).reshape(20, 16, 384)
        row_cells[...] = normed.reshape(20, 16, 128)
        turned_columns(normed_t, x, row_cells[2:18, 2:10, :].reshape(128, 128))
        masked = jnp.where(live, cots[x].reshape(320, 128), 0.0)
        masked3[x] = neighbours(masked).reshape(20, 16, 384)
        cots[x] = masked.reshape(20, 16, 128)
        parts = [cots[x, :, 1 + k : 9 + k, :].reshape(160, 128) for k in range(3)]
        masked_even[x] = jnp.concatenate([part.astype(BF16) for part in parts], axis=1)
        masked_odd[x] = jnp.concatenate([part[8:152].astype(BF16) for part in parts], axis=1)
        return carry

    lax.fori_loop(0, 12, prepare, 0)
    for copy in copies[8:]:
        copy.wait()

    def convolve(step, carry):
        x = step * 2
        values = cells[pl.ds(x + 1, 2), 1:19, :, :].reshape(576, 128)
        before = convolve_pair(normed3, x, 18, first)
        before = jnp.where(jnp.abs(values) < LIMIT, before, 0.0)
        sigmoid = jax.nn.sigmoid(before)
        active = before * sigmoid
        act_ref[pl.ds(x, 2)] = active.astype(BF16).reshape(2, 18, 16, 128)
        pair_cells[...] = active.reshape(2, 18, 16, 128)
        for n in range(2):
            inner = pair_cells[n, 1:17, 2:10, :].reshape(128, 128)
            turned_columns(act_t, x + 1 + n, inner)
        active_grad = convolve_pair(masked3, x, 18, second_t)
        pre = active_grad * sigmoid * (1.0 + before * (1.0 - sigmoid))
        pre = jnp.where(values > -LIMIT, pre, 0.0)
        pre_ref[pl.ds(x, 2)] = pre.astype(BF16).reshape(2, 18, 16, 128)
        pair_cells[...] = pre.reshape(2, 18, 16, 128)
        for n in range(2):
            parts = [pair_cells[n, :, 1 + k : 9 + k, :].reshape(144, 128) for k in range(3)]
            pre_even[x + n] = jnp.concatenate([part.astype(BF16) for part in parts], axis=1)
            pre_odd[x + n] = jnp.concatenate([part[8:136].astype(BF16) for part in parts], axis=1)
        return carry

    lax.fori_loop(0, 5, convolve, 0)
    results = [
        pltpu.make_async_copy(source, target, sems.at[n])
        for n, (source, target) in enumerate(((act_ref, act_hbm), (pre_ref, pre_hbm)))
    ]
    for copy in results:
        copy.start()

    for which, left, sides in (
        (1, act_t, ((masked_odd, 16), (masked_even, 16), (masked_odd, 0))),
        (0, normed_t, ((pre_even, 16), (pre_odd, 0), (pre_even, 0))),
    ):
        own = jnp.concatenate([left[:, 128 * i : 128 * (i + 10)] for i in range(3)], axis=0)
        for j, (cots_at, row) in enumerate(sides):
            start = which
            cot = cots_at[start : start + 10, row : row + 128, :].reshape(1280, 384)
            total = jnp.dot(own, cot, preferred_element_type=F32).astype(BF16)
            for i in range(3):
                for k in range(3):
                    found[which, i * 9 + j * 3 + k] = total[
                        i * 128 : (i + 1) * 128, (2 - k) * 128 : (3 - k) * 128
                    ]

    results += [
        pltpu.make_async_copy(found.at[core], own_hbm, sems.at[2]),
        pltpu.make_async_copy(found.at[1 - core], send_hbm, sems.at[3]),
    ]
    for copy in results[2:]:
        copy.start()
    for copy in results:
        copy.wait()


def grads_call(where, gain, pieces, first, second_t):
    return pl.pallas_call(
        grads_kernel,
        out_shape=(
            jax.ShapeDtypeStruct((10, 18, 16, 128), BF16),
            jax.ShapeDtypeStruct((10, 18, 16, 128), BF16),
            jax.ShapeDtypeStruct((27, 128, 128), BF16),
            jax.ShapeDtypeStruct((27, 128, 128), BF16),
        ),
        in_specs=[SM, VM] + [AN] * 8 + [HB] * 2,
        out_specs=(HB, HB, HB, HB),
        scratch_shapes=[
            pltpu.VMEM((12, 20, 16, 128), F32),
            pltpu.VMEM((12, 20, 16, 128), F32),
            pltpu.VMEM((12, 20, 16, 384), BF16),
            pltpu.VMEM((12, 20, 16, 384), BF16),
            pltpu.VMEM((128, 1536), BF16),
            pltpu.VMEM((128, 1536), BF16),
            pltpu.VMEM((20, 16, 128), F32),
            pltpu.VMEM((2, 18, 16, 128), F32),
            pltpu.VMEM((12, 160, 384), BF16),
            pltpu.VMEM((12, 144, 384), BF16),
            pltpu.VMEM((10, 144, 384), BF16),
            pltpu.VMEM((10, 128, 384), BF16),
            pltpu.VMEM((2, 27, 128, 128), BF16),
            *[pltpu.VMEM(shape, BF16) for shape in PIECES],
            pltpu.VMEM((4608, 256), BF16),
            pltpu.VMEM((4608, 256), BF16),
            pltpu.VMEM((10, 18, 16, 128), BF16),
            pltpu.VMEM((10, 18, 16, 128), BF16),
            pltpu.SemaphoreType.DMA((10,)),
        ],
        compiler_params=pltpu.CompilerParams(vmem_limit_bytes=60 << 20),
        cost_estimate=pl.CostEstimate(flops=10 << 30, bytes_accessed=8 << 20, transcendentals=1 << 20),
    )(where, gain, *pieces, first, second_t)


def outputs_kernel(
    gain,
    both_hbm,
    act_hbm,
    pre_hbm,
    second_hbm,
    first_hbm,
    block_ref,
    grad_ref,
    gain_ref,
    both,
    act,
    pre,
    second,
    first_t,
    act3,
    pre3,
    spread,
    sems,
):
    copies = [
        pltpu.make_async_copy(source, target, sems.at[n])
        for n, (source, target) in enumerate(
            (
                (act_hbm, act),
                (pre_hbm, pre),
                (both_hbm, both),
                (second_hbm, second),
                (first_hbm, first_t),
            )
        )
    ]
    for copy in copies:
        copy.start()
    for copy, source, target in ((copies[0], act, act3), (copies[1], pre, pre3)):
        copy.wait()

        def prepare(x, carry):
            values = source[x].reshape(288, 128).astype(F32)
            target[x] = neighbours(values).reshape(18, 16, 384)
            return carry

        lax.fori_loop(0, 10, prepare, 0)

    for copy in copies[2:]:
        copy.wait()
    gains = gain[...]

    def convolve(step, total):
        x = step * 2
        branch = convolve_pair(act3, x, 16, second)
        spread[...] = branch.reshape(2, 16, 16, 128)
        branch = spread[:, :, 2:10, :].reshape(256, 128)
        values = both[0, pl.ds(x, 2)].astype(F32).reshape(256, 128)
        live = values < LIMIT
        held = jnp.where(live, values, 0.0)
        block = jnp.where(live, branch, 0.0) + held
        block_ref[pl.ds(x, 2)] = block.astype(BF16).reshape(2, 16, 8, 128)
        normed_grad = convolve_pair(pre3, x, 16, first_t)
        spread[...] = normed_grad.reshape(2, 16, 16, 128)
        normed_grad = jnp.where(live, spread[:, :, 2:10, :].reshape(256, 128), 0.0)
        inverse = lax.rsqrt(jnp.mean(held * held, axis=-1, keepdims=True) + epsilon)
        total = total + jnp.sum((normed_grad * held * inverse).reshape(32, 8, 128), axis=0)
        upstream = normed_grad * gains
        centred = jnp.mean(held * upstream, axis=-1, keepdims=True)
        extra = inverse * upstream - held * (inverse * inverse * inverse * centred)
        cot = both[1, pl.ds(x, 2)].astype(F32).reshape(256, 128)
        grad = cot + jnp.where(live, extra, 0.0)
        grad_ref[pl.ds(x, 2)] = grad.astype(BF16).reshape(2, 16, 8, 128)
        return total

    total = lax.fori_loop(0, 4, convolve, jnp.zeros((8, 128), F32))
    gain_ref[...] = total


def outputs_call(gain, both, act, pre, second, first_t):
    return pl.pallas_call(
        outputs_kernel,
        out_shape=(
            jax.ShapeDtypeStruct((8, 16, 8, 128), BF16),
            jax.ShapeDtypeStruct((8, 16, 8, 128), BF16),
            jax.ShapeDtypeStruct((8, 128), F32),
        ),
        in_specs=[VM, AN, HB, HB, HB, HB],
        out_specs=(VM,) * 3,
        scratch_shapes=[
            pltpu.VMEM((2, 8, 16, 8, 128), BF16),
            pltpu.VMEM((10, 18, 16, 128), BF16),
            pltpu.VMEM((10, 18, 16, 128), BF16),
            pltpu.VMEM((4608, 256), BF16),
            pltpu.VMEM((4608, 256), BF16),
            pltpu.VMEM((10, 18, 16, 384), BF16),
            pltpu.VMEM((10, 18, 16, 384), BF16),
            pltpu.VMEM((2, 16, 16, 128), F32),
            pltpu.SemaphoreType.DMA((5,)),
        ],
        compiler_params=pltpu.CompilerParams(vmem_limit_bytes=60 << 20),
        cost_estimate=pl.CostEstimate(flops=8 << 30, bytes_accessed=6 << 20, transcendentals=4096),
    )(gain, both, act, pre, second, first_t)


def add_kernel(own_ref, other_ref, out_ref):
    out_ref[...] = (own_ref[...].astype(F32) + other_ref[...].astype(F32)).astype(BF16)


def add_pair(own, other):
    return pl.pallas_call(
        add_kernel,
        out_shape=jax.ShapeDtypeStruct((27, 128, 128), BF16),
        in_specs=[VM, VM],
        out_specs=VM,
        compiler_params=pltpu.CompilerParams(vmem_limit_bytes=6 << 20),
        cost_estimate=pl.CostEstimate(flops=1 << 19, bytes_accessed=3 << 20, transcendentals=0),
    )(own, other)


FIRST = [(i, i ^ 1) for i in range(8)]
SECOND = [(i, i - 1 if i % 2 == 0 else i + 1) for i in range(1, 7)]


def across(pairs):
    return [(a * 2 + s, b * 2 + 1 - s) for a, b in pairs for s in range(2)]


def edges(both, send_one, send_two, layer, layer_one, layer_two):
    x_one = lax.ppermute(send_one, GX, FIRST)
    x_two = lax.ppermute(send_two, GX, SECOND)
    came = lax.ppermute(layer, SA, [(0, 1), (1, 0)])
    came_one = lax.ppermute(layer_one, PLANE, across(FIRST))
    came_two = lax.ppermute(layer_two, PLANE, across(SECOND))

    def wide(start):
        def rows(part):
            return lax.dynamic_slice_in_dim(part, start, 2, axis=2)

        inner = jnp.concatenate([rows(part) for part in (x_one, both, x_two)], axis=1)
        outer = jnp.concatenate([rows(part) for part in (came_one, came, came_two)], axis=1)
        return jnp.concatenate([inner, outer], axis=3)

    first_y, second_y = send_rows(lax.axis_index(GY), 14)
    y_one = lax.ppermute(wide(first_y), GY, FIRST)
    y_two = lax.ppermute(wide(second_y), GY, SECOND)
    return both, x_one, x_two, came, came_one, came_two, y_one, y_two


def exchange(values, axes):
    return lax.all_to_all(values, axes, split_axis=0, concat_axis=0, tiled=True)


def local(sweep_bricks, target_rank, target_slot, conv_first, conv_second, norm_gain, out_grad):
    gain = norm_gain.reshape(1, 128)
    core = lax.axis_index("c")
    where = jnp.stack([lax.axis_index(SA), core, lax.axis_index(GX), lax.axis_index(GY)])
    where = where.astype(jnp.int32)
    both, ((first, first_t), (second, second_t)), where = regroup(
        sweep_bricks.reshape(128, 64, 128),
        target_rank.reshape(1, 128),
        target_slot.reshape(1, 128),
        out_grad,
        where,
        (pair_weights(conv_first), pair_weights(conv_second)),
    )
    pieces = edges(*both)
    act, pre, own, send = grads_call(where, gain, pieces, first, second_t)
    other = lax.ppermute(send, "c", [(0, 1), (1, 0)])
    shares = exchange(add_pair(own, other).reshape(16, 216, 128), PLANE)
    block_out, grid_grad, gain_part = outputs_call(gain, pieces[0], act, pre, second, first_t)

    def halves(row):
        high = row.astype(BF16)
        low = (row - high.astype(F32)).astype(BF16)
        return [high, low, jnp.zeros((6, 128), BF16)]

    def joined(total, row):
        return jnp.concatenate([total.astype(BF16)] + halves(row), axis=0)

    total = jnp.sum(shares.astype(F32), axis=0)
    sent = joined(total, jnp.sum(gain_part, axis=0, keepdims=True))
    parts = [sent] + [along("z", sent, shift) for shift in (1, 2, 3)]
    parts = [part.astype(F32) for part in parts]
    layers = (parts[0] + parts[2]) + (parts[1] + parts[3])
    sent = joined(layers[:216], layers[216:217] + layers[217:218])
    gathered = exchange(jnp.broadcast_to(sent[None], (16, 224, 128)), PLANE)
    swapped = lax.ppermute(gathered, "c", [(0, 1), (1, 0)])
    factor = 1.0 / math.sqrt(131072.0)

    def weights(low, high):
        picked = jnp.where(core == 0, low[:, :216], high[:, :216])
        return (picked.astype(F32) * factor).reshape(27, 128, 128)

    gains = jnp.sum(gathered[:, 216:218].astype(F32), axis=(0, 1))
    gains = gains + jnp.sum(swapped[:, 216:218].astype(F32), axis=(0, 1))
    return (
        block_out,
        grid_grad,
        weights(gathered, swapped),
        weights(swapped, gathered),
        gains * factor,
    )


def solution(mesh):
    inner = Mesh(mesh.devices.reshape(4, 2, 4, 2, 2), ("y", "xl", "z", "c", "xh"))
    in_specs = (
        P(GX, GY, SA, None, None),
        P(GX, GY, SA, None),
        P(GX, GY, SA),
        P(),
        P(),
        P(),
        P(GX, GY, SA, None),
    )
    out_specs = (P(GX, GY, SA, None), P(GX, GY, SA, None), P(), P(), P())
    return jax.shard_map(local, mesh=inner, in_specs=in_specs, out_specs=out_specs, check_vma=False)
```
